128 devices in a mesh: tm: 16 (over y, z), table: 8 (over x, core).
Axes of the slice: x: 4, y: 4, z: 4, core: 2. Of those that a mesh axis runs over, the one named last changes fastest.
Arguments:
- item_owner: int32 [16, 12288, 1], P('table', 'tm'), may hold values from 0 to 127; in each aligned block of 768 rows (0 to 767, 768 to 1535, ..., all dimensions but the last counted through in order) at most 12 rows name the same one
- item_row: int32 [16, 12288], P('table', 'tm'), may hold values from 0 to 4095
- history_len: int32 [16], P('table'), may hold values from 3072 to 12288, as said below
- event_gap: float32 [16, 12288], P('table', 'tm'), may hold values from 0 to 36864, as said below
- item_table: bfloat16 [524288, 512], P(('tm', 'table')), may hold values from -6 to 6
- norm_gain: float32 [512], replicated, may hold values from 0.1 to 1.9
- in_weight: bfloat16 [512, 2192], replicated, may hold values from -0.25 to 0.25
- conv_weight: float32 [4, 1152], replicated, may hold values from -3 to 3
- conv_bias: float32 [1152], replicated, may hold values from -3 to 3
- dt_bias: float32 [16], replicated, may hold values from -1 to 1
- decay_rate: float32 [16], replicated, may hold values from 0 to 16, as said below
- out_gain: float32 [1024], replicated, may hold values from 0.1 to 1.9
- emitted_projection: bfloat16 [1024, 512], replicated, may hold values from -0.1875 to 0.1875
Outputs:
- layer_out: bfloat16 [16, 12288, 512], P('table', 'tm')
The draws below stay inside these ranges and needn't reach their ends.
Inputs may be any that keep to these rules, and one draw needn't show every extreme that they name: `item_owner`: in every user's 768 events held by one device no owner is named more than 12 times, a bound that some block reaches. `history_len`: some user has all 12288 events and some user 12288 // 4. `event_gap`: Positive. `decay_rate`: Positive.
All inputs are finite; a program needn't handle non-finite values.
Results may differ from the reference program's by a relative error of at most 0.01.
Values may be sent and summed in bfloat16 or wider, within the bound.
No kernel may reach another device: no remote copies, remote signals or barrier semaphores. Data moves between devices by JAX's collectives and lax.ppermute only.
A program may use at most 192 MiB of HBM per device.

```python
import math
import jax
import jax.numpy as jnp
import numpy as np
from jax import lax

D = 512
HEADS = 16
HEAD_DIM = 64
STATE = 64
BLOCK = 256
ITEMS_DEV = 4096
EV = 768
DI = 1024
CONVW = 1152
PROJ = 2192
CUSTOMER_COUNT = 16
PAST_ACTIONS = 12288
CAP = 12
ITEMS = 524288
DEVICES = 128


def draw_history_len(key, part):
    first_key, auxiliary_seed, third_key = jax.random.split(key, 3)
    lengths = jax.random.randint(first_key, (CUSTOMER_COUNT,), PAST_ACTIONS // 4, PAST_ACTIONS + 1)
    longest = jax.random.randint(auxiliary_seed, (), 0, CUSTOMER_COUNT)
    shortest = (longest + jax.random.randint(third_key, (), 1, CUSTOMER_COUNT)) % CUSTOMER_COUNT
    user_index = jnp.arange(CUSTOMER_COUNT)
    lengths = jnp.where(user_index == longest, PAST_ACTIONS, lengths)
    lengths = jnp.where(user_index == shortest, PAST_ACTIONS // 4, lengths)
    return lengths.astype(jnp.int32)


def draw_event_gap(key, part):
    first_key, auxiliary_seed, third_key = jax.random.split(key, 3)
    typical_scenario = jnp.exp(jax.random.uniform(first_key, (CUSTOMER_COUNT, PAST_ACTIONS), jnp.float32, math.log(0.5), math.log(2.0)))
    action_cluster = jax.random.randint(auxiliary_seed, (CUSTOMER_COUNT, PAST_ACTIONS), 0, PAST_ACTIONS) < 4
    extended_record = PAST_ACTIONS * jax.random.uniform(third_key, (CUSTOMER_COUNT, PAST_ACTIONS), jnp.float32, 1.5, 3.0)
    return jnp.where(action_cluster, extended_record, typical_scenario).astype(jnp.float32)


def draw_decay_rate(key, part):
    first_key, auxiliary_seed, third_key = jax.random.split(key, 3)
    slow_share = 5
    slow_heads = jax.random.randint(first_key, (HEADS,), 0, 10) < slow_share
    slow_rate = jnp.exp(jax.random.uniform(auxiliary_seed, (HEADS,), jnp.float32, math.log(1.0 / (8 * PAST_ACTIONS)), math.log(1.0 / (2 * PAST_ACTIONS))))
    fast_rate = jnp.exp(jax.random.uniform(third_key, (HEADS,), jnp.float32, math.log(4.0 / BLOCK), math.log(16.0 / BLOCK)))
    return jnp.where(slow_heads, slow_rate, fast_rate).astype(jnp.float32)


def plant(entries, own_key, smallest, largest):
    longest = entries.shape.index(max(entries.shape))
    spots = []
    for shift in (0, 1):
        where = [jax.random.randint(jax.random.fold_in(own_key, axis), (), 0, length) for axis, length in enumerate(entries.shape)]
        where[longest] = (where[longest] + shift) % entries.shape[longest]
        spots.append(tuple(where))
    return entries.at[spots[0]].set(smallest).at[spots[1]].set(largest)


def levels(stream_key, shape, pieces, smallest, high):
    level = 1.0
    for position, parts in pieces:
        steps = jax.random.uniform(jax.random.fold_in(jax.random.fold_in(stream_key, 6), position), (parts,), jnp.float32, smallest / len(pieces), high / len(pieces))
        level = level * jnp.repeat(jnp.exp(steps), shape[position] // parts).reshape((-1,) + (1,) * (len(shape) - 1 - position))
    return level


def deal_out(key, own, number, rows, number_of, top, limit, skew):
    order = jax.random.permutation(key, number_of)
    crowded, usual = portions_of(number_of, rows * top, limit, skew, True), portions_of(number_of, rows * top, limit, skew, False)
    places = jnp.arange(number_of)

    def named(sizes, rotation):
        used = int((sizes > 0).sum())
        fixed = max(1, used // 4)
        passed = fixed + (places - fixed + rotation * (used - fixed)) % max(1, number_of - fixed)
        return jnp.zeros((number_of,), jnp.int32).at[order[jnp.where(places < fixed, places, passed)]].set(jnp.asarray(sizes, jnp.int32))

    sizes = jnp.where(number % 4 == 0, named(crowded, number // 4), named(usual, number - number // 4 - 1))
    mixed = jax.random.permutation(jax.random.fold_in(own, 3), number_of)
    giver, sink = mixed[0:number_of // 2 * 2:2], mixed[1:number_of // 2 * 2:2]
    room = jnp.minimum(sizes[giver] - 1, limit - sizes[sink]) // 2
    room = jnp.where((giver == order[0]) | (sink == order[0]) | (sizes[sink] == 0), 0, jnp.maximum(room, 0))
    passed = jax.random.randint(jax.random.fold_in(own, 4), (number_of // 2,), 0, 1 << 20) % (room + 1)
    sizes = sizes.at[giver].add(-passed).at[sink].add(passed)
    members = jnp.searchsorted(jnp.cumsum(sizes), jnp.arange(rows * top), side="right").astype(jnp.int32)
    listing = members.reshape(top, rows).T
    listing = listing[jax.random.permutation(jax.random.fold_in(own, 1), rows)]
    rotation = jax.random.randint(jax.random.fold_in(own, 2), (rows, 1), 0, top)
    return jnp.take_along_axis(listing, (jnp.arange(top)[None, :] + rotation) % top, axis=1)


def portions_of(amount, total, most, slope, full):
    weights = [(1 << 20) // math.isqrt(grade ** slope) + 1 for grade in range(1, amount + 1)]
    largest = most if full else min(most, max(-(-total // amount), total * weights[0] // sum(weights)))
    least = 1 if total - largest >= amount - 1 else 0
    holding, surplus = [largest] + [least] * (amount - 1), total - largest - least * (amount - 1)
    while surplus > 0:
        movable = [i for i in range(1, amount) if holding[i] < largest] or [i for i in range(1, amount) if holding[i] < most]
        pool, budget = sum([weights[i] for i in movable]), surplus
        for i in movable:
            addition = min(most - holding[i], max(1, budget * weights[i] // pool), surplus)
            holding[i] = holding[i] + addition
            surplus = surplus - addition
    return np.array(holding)


def scatter_about(own_key, extent, width, reach, pieces=(), held_as=jnp.bfloat16):
    level = levels(own_key, extent, pieces, -0.22, 0.18) if pieces else 1.0
    result = jax.random.normal(own_key, extent, jnp.float32) * width * level
    return jnp.minimum(jnp.maximum(result, -reach), reach).astype(held_as)


def setup_inputs(seed: int = 0) -> dict:
    splits = jax.random.split(jax.random.key(seed), 14)
    item_owner_keys = jax.random.split(jax.random.fold_in(splits[0], 1), CUSTOMER_COUNT * PAST_ACTIONS // EV)
    item_owner_turns = jax.random.permutation(jax.random.fold_in(splits[0], 3), CUSTOMER_COUNT * PAST_ACTIONS // EV)
    item_owner = jax.vmap(lambda own, number: deal_out(jax.random.fold_in(splits[0], 2), own, number, EV, DEVICES, 1, CAP, 1))(item_owner_keys, item_owner_turns).reshape((CUSTOMER_COUNT, PAST_ACTIONS, 1))
    item_row = plant(jax.random.randint(splits[1], (CUSTOMER_COUNT, PAST_ACTIONS), 0, ITEMS_DEV), jax.random.fold_in(splits[1], 1), 0, ITEMS_DEV - 1).astype(jnp.int32)
    history_len = draw_history_len(jax.random.fold_in(splits[13], 71), 0)
    event_gap = draw_event_gap(jax.random.fold_in(splits[13], 71), 0)
    item_table = scatter_about(splits[4], (ITEMS, D), 1.0, 6.0, ((0, 128),))
    norm_gain = jnp.clip(1.0 + 0.18 * jax.random.normal(splits[5], (D,), jnp.float32), 0.1, 1.9)
    in_weight = scatter_about(splits[6], (D, PROJ), D ** -0.5, 0.25)
    conv_weight = scatter_about(splits[7], (4, CONVW), 4 ** -0.5, 3.0, (), jnp.float32)
    conv_bias = scatter_about(splits[8], (CONVW,), 0.5, 3.0, (), jnp.float32)
    dt_bias = jnp.clip(jax.random.uniform(splits[9], (HEADS,), jnp.float32, -1.0, 1.0), -1.0, 1.0)
    decay_rate = draw_decay_rate(jax.random.fold_in(splits[13], 71), 0)
    out_gain = jnp.clip(1.0 + 0.18 * jax.random.normal(splits[11], (DI,), jnp.float32), 0.1, 1.9)
    emitted_projection = scatter_about(splits[12], (DI, D), DI ** -0.5, 0.1875)
    return {"item_owner": item_owner, "item_row": item_row, "history_len": history_len, "event_gap": event_gap, "item_table": item_table, "norm_gain": norm_gain, "in_weight": in_weight, "conv_weight": conv_weight, "conv_bias": conv_bias, "dt_bias": dt_bias, "decay_rate": decay_rate, "out_gain": out_gain, "emitted_projection": emitted_projection}


def rounded(value):
    return lax.optimization_barrier(value.astype(jnp.bfloat16))

def reference(item_owner, item_row, history_len, event_gap, item_table, norm_gain, in_weight, conv_weight, conv_bias, dt_bias, decay_rate, out_gain, emitted_projection):
    inner_dim = HEADS * HEAD_DIM
    conv_dim = inner_dim + 2 * STATE
    block_count = PAST_ACTIONS // BLOCK
    forward_only = jnp.arange(BLOCK)[:, None] >= jnp.arange(BLOCK)[None, :]

    def one_block(carried, packed):
        streams, in_coef, out_coef, steps, log_decay = packed
        cum_decay = jnp.cumsum(log_decay, axis=0)
        scores = jnp.dot(out_coef, in_coef.T, preferred_element_type=jnp.float32)
        cum_heads = cum_decay.T
        spread = cum_heads[:, :, None] - cum_heads[:, None, :]
        fading = jnp.exp(jnp.where(forward_only, spread, 0.0))
        mixing = rounded(jnp.where(forward_only, scores[None] * fading * steps.T[:, None, :], 0.0))
        local_y = jnp.einsum('hqs,shp->qhp', mixing.astype(jnp.float32), streams.astype(jnp.float32))
        held = rounded(carried).astype(jnp.float32)
        carried_y = jnp.exp(cum_decay)[:, :, None] * jnp.einsum('qn,hpn->qhp', out_coef.astype(jnp.float32), held)
        to_end = jnp.exp(cum_decay[-1:] - cum_decay) * steps
        scaled = rounded(to_end[:, :, None] * streams.astype(jnp.float32)).astype(jnp.float32)
        block_state = jnp.einsum('qhp,qn->hpn', scaled, in_coef.astype(jnp.float32))
        carried = jnp.exp(cum_decay[-1])[:, None, None] * carried + block_state
        return (carried, local_y + carried_y)

    def one_user(packed):
        owners, row_ids, length, gap_values = packed
        item_vec = item_table[owners[:, 0] * ITEMS_DEV + row_ids]
        item_wide = item_vec.astype(jnp.float32)
        normed = rounded(item_wide * lax.rsqrt(lax.optimization_barrier(jnp.mean(item_wide * item_wide, axis=-1, keepdims=True)) + 1e-05) * norm_gain)
        projected = rounded(jnp.dot(normed, in_weight, preferred_element_type=jnp.float32))
        gate_raw = projected[:, :inner_dim].astype(jnp.float32)
        conv_in = projected[:, inner_dim:inner_dim + conv_dim]
        raw_step_size = projected[:, inner_dim + conv_dim:].astype(jnp.float32)
        padded = jnp.pad(conv_in, ((3, 0), (0, 0))).astype(jnp.float32)
        conv_sum = conv_bias + conv_weight[0] * padded[0:PAST_ACTIONS]
        for tap_index in range(1, 4):
            conv_sum = conv_sum + conv_weight[tap_index] * padded[tap_index:tap_index + PAST_ACTIONS]
        conv_out = rounded(jax.nn.silu(conv_sum))
        streams = conv_out[:, :inner_dim].reshape(block_count, BLOCK, HEADS, HEAD_DIM)
        in_coef = conv_out[:, inner_dim:inner_dim + STATE].reshape(block_count, BLOCK, STATE)
        out_coef = conv_out[:, inner_dim + STATE:].reshape(block_count, BLOCK, STATE)
        alive = (jnp.arange(PAST_ACTIONS, dtype=jnp.int32) < length).astype(jnp.float32)
        steps = alive[:, None] * jax.nn.softplus(raw_step_size + dt_bias)
        log_decay = -decay_rate * gap_values[:, None] * steps
        start = jnp.zeros((HEADS, HEAD_DIM, STATE), jnp.float32)
        unused, response = lax.scan(one_block, start, (streams, in_coef, out_coef, steps.reshape(block_count, BLOCK, HEADS), log_decay.reshape(block_count, BLOCK, HEADS)))
        response = response.reshape(PAST_ACTIONS, HEADS, HEAD_DIM)
        gated = response * jax.nn.silu(gate_raw.reshape(PAST_ACTIONS, HEADS, HEAD_DIM))
        gated = gated * lax.rsqrt(lax.optimization_barrier(jnp.mean(gated * gated, axis=-1, keepdims=True)) + 1e-05)
        normed_y = rounded(gated.reshape(PAST_ACTIONS, inner_dim) * out_gain)
        layer_out = item_wide + jnp.dot(normed_y, emitted_projection, preferred_element_type=jnp.float32)
        return (alive[:, None] * layer_out).astype(jnp.bfloat16)
    return lax.map(one_user, (item_owner, item_row, history_len, event_gap))
```

```python
import functools

import jax
import jax.numpy as jnp
from jax import lax
from jax.experimental import pallas as pl
from jax.experimental.pallas import tpu as pltpu
from jax.sharding import PartitionSpec as P

F32 = jnp.float32
BF16 = jnp.bfloat16
EPS = 1e-05
LANES = 128
CHUNK = 128
ROWS3 = 256
TABLE_STEP = 512
VMEM_LIMIT = 56 * 1024 * 1024


def params(axes):
    return pltpu.CompilerParams(
        dimension_semantics=("arbitrary",) * axes, vmem_limit_bytes=VMEM_LIMIT
    )


def full(shape):
    return pl.BlockSpec(shape, lambda *_: (0,) * len(shape))


def iota(shape, axis):
    return lax.broadcasted_iota(jnp.int32, shape, axis)


def nt(a, b):
    return lax.dot_general(a, b, (((1,), (1,)), ((), ())), preferred_element_type=F32)


def mm(a, b):
    return jnp.dot(a, b, preferred_element_type=F32)


def silu(v):
    half = 0.5 * v
    return half + half * jnp.tanh(half)


def route_kernel(owner_ref, row_ref, req_ref, place_ref, *, devices, cap, width):
    users, events = owner_ref.shape
    tri = jnp.where(
        (iota((LANES, 2 * LANES), 0) < iota((LANES, 2 * LANES), 1))
        | (iota((LANES, 2 * LANES), 1) >= LANES),
        1.0,
        0.0,
    ).astype(BF16)
    slots = users * cap
    req = jnp.zeros((devices, width), F32)
    for u in range(users):
        running = jnp.zeros((devices, LANES), F32)
        for c in range(events // LANES):
            own = owner_ref[u : u + 1, c * LANES : (c + 1) * LANES]
            row = row_ref[u : u + 1, c * LANES : (c + 1) * LANES]
            hot = iota((devices, LANES), 0) == own
            hot_b = jnp.where(hot, 1.0, 0.0).astype(BF16)
            counts = mm(hot_b, tri)
            rank = counts[:, :LANES] + running
            running = running + counts[:, LANES:]
            slot = jnp.sum(jnp.where(hot, rank, 0.0), axis=0, keepdims=True).astype(jnp.int32)
            slot = slot + u * cap
            match = iota((width, LANES), 0) == slot
            high = jnp.where(match, (row >> 6).astype(F32), 0.0).astype(BF16)
            low = jnp.where(match, (row & 63).astype(F32), 0.0).astype(BF16)
            req = req + 64.0 * nt(hot_b, high) + nt(hot_b, low)
            place = (own * (slots * 2 // 3) + slot - u * (slots // 3)).astype(F32)
            place_ref[u, c * LANES : (c + 1) * LANES, :] = jnp.broadcast_to(
                place, (LANES, LANES)
            ).T.astype(jnp.int32)
    req_ref[:, 0, :] = req.astype(jnp.int32)


def route(owners, rows, devices, cap, width):
    users, events = owners.shape
    return pl.pallas_call(
        functools.partial(route_kernel, devices=devices, cap=cap, width=width),
        out_shape=(
            jax.ShapeDtypeStruct((devices, 1, width), jnp.int32),
            jax.ShapeDtypeStruct((users, events, LANES), jnp.int32),
        ),
        compiler_params=params(0),
        name="route",
    )(owners, rows)


def fetch_kernel(idx_ref, tab_ref, out_ref, tab4, rows4, *, slots):
    i = pl.program_id(0)
    step, dim = tab_ref.shape
    tiles = dim // LANES
    for cb in range(tiles):
        tab4[pl.ds(i * step * tiles + cb, step, stride=tiles), :] = tab_ref[
            :, cb * LANES : (cb + 1) * LANES
        ].astype(F32)

    @pl.when(i == pl.num_programs(0) - 1)
    def _():
        owners = idx_ref.shape[0]

        def body(o, carry):
            base = pl.multiple_of(o * slots * tiles, 8)
            for s in range(slots):
                r = idx_ref[o, 0, s]
                rows4[pl.ds(base + tiles * s, tiles), :] = tab4[
                    pl.ds(pl.multiple_of(r * tiles, tiles), tiles), :
                ]
            return carry

        lax.fori_loop(0, owners, body, 0)

        def pack(g, carry):
            for half in range(2):
                for cb in range(tiles):
                    start = (g * 2 + half) * 16 * tiles + cb
                    out_ref[
                        pl.ds(pl.multiple_of((g * 2 + half) * 16, 16), 16),
                        cb * LANES : (cb + 1) * LANES,
                    ] = rows4[pl.ds(start, 16, stride=tiles), :].astype(BF16)
            return carry

        lax.fori_loop(0, owners * slots // 32, pack, 0)


def fetch(idx, table, slots):
    owners = idx.shape[0]
    items, dim = table.shape
    tiles = dim // LANES
    return pl.pallas_call(
        functools.partial(fetch_kernel, slots=slots),
        out_shape=jax.ShapeDtypeStruct((owners * slots, dim), BF16),
        grid=(items // TABLE_STEP,),
        in_specs=[
            pl.BlockSpec(memory_space=pltpu.SMEM),
            pl.BlockSpec((TABLE_STEP, dim), lambda i: (i, 0)),
        ],
        out_specs=full((owners * slots, dim)),
        scratch_shapes=[
            pltpu.VMEM((items * tiles, LANES), F32),
            pltpu.VMEM((owners * slots * tiles, LANES), F32),
        ],
        compiler_params=params(1),
        name="fetch",
    )(idx, table)


def project_kernel(
    got_ref, place_ref, gain_ref, w_ref, x_ref, gate_ref, conv_ref, step_ref, tail_ref, *, inner
):
    u = pl.program_id(0)
    owners, slots, dim = got_ref.shape
    window = slots * 2 // 3
    rows = place_ref.shape[1]
    shift = pl.multiple_of(u * (slots // 3), 8)
    got = got_ref[:, pl.ds(shift, window), :].reshape(owners * window, dim)
    place = place_ref[0]
    pieces = [
        jnp.where(place == iota((rows, LANES), 1) + k * LANES, 1.0, 0.0).astype(BF16)
        for k in range(owners * window // LANES)
    ]
    x = mm(jnp.concatenate(pieces, axis=1), got)
    x_ref[0] = x.astype(BF16)
    normed = x * lax.rsqrt(jnp.mean(x * x, axis=-1, keepdims=True) + EPS) * gain_ref[...]
    normed = normed.astype(BF16)
    conv_dim = conv_ref.shape[2]
    heads = step_ref.shape[1]
    conv = mm(normed, w_ref[:, inner : inner + conv_dim]).astype(BF16)
    conv_ref[0] = conv
    raw = mm(normed, w_ref[:, inner + conv_dim : inner + conv_dim + heads])
    step_ref[0] = raw.astype(BF16).astype(F32).T
    gate_ref[0] = mm(normed, w_ref[:, :inner]).astype(BF16)
    tail_ref[0] = conv[rows - 8 :, :]


def project(got, place, gain, weight, inner, conv_dim, heads):
    users, events, _ = place.shape
    dim = got.shape[2]
    rows = ROWS3
    block = lambda width: pl.BlockSpec((1, rows, width), lambda u, i: (u, i, 0))
    return pl.pallas_call(
        functools.partial(project_kernel, inner=inner),
        out_shape=(
            jax.ShapeDtypeStruct((users, events, dim), BF16),
            jax.ShapeDtypeStruct((users, events, inner), BF16),
            jax.ShapeDtypeStruct((users, events, conv_dim), BF16),
            jax.ShapeDtypeStruct((users, heads, events), F32),
            jax.ShapeDtypeStruct((users, 8, conv_dim), BF16),
        ),
        grid=(users, events // rows),
        in_specs=[full(got.shape), block(LANES), full(gain.shape), full(weight.shape)],
        out_specs=(
            block(dim),
            block(inner),
            block(conv_dim),
            pl.BlockSpec((1, heads, rows), lambda u, i: (u, 0, i)),
            pl.BlockSpec((1, 8, conv_dim), lambda u, i: (u, 0, 0)),
        ),
        compiler_params=params(2),
        name="project",
    )(got, place, gain, weight)


def lane_halves(rows_a, rows_b):
    return jnp.where(iota(rows_a.shape, rows_a.ndim - 1) < LANES // 2, rows_a, rows_b)


def running_sum(values, reverse):
    lane = iota(values.shape, 1)
    size = values.shape[1]
    k = 1
    while k < size:
        if reverse:
            values = values + jnp.where(lane < size - k, pltpu.roll(values, size - k, 1), 0.0)
        else:
            values = values + jnp.where(lane >= k, pltpu.roll(values, k, 1), 0.0)
        k *= 2
    return values


def pair_rhs(pair):
    low = iota(pair.shape, 1) < LANES // 2
    zero = jnp.zeros_like(pair)
    return jnp.concatenate([jnp.where(low, pair, zero), jnp.where(low, zero, pair)], axis=0)


def states_kernel(
    len_ref,
    pos_ref,
    conv_ref,
    edge_ref,
    step_ref,
    gap_ref,
    cw_ref,
    cb_ref,
    dt_ref,
    rate_ref,
    xbc_ref,
    cum_ref,
    steps_ref,
    hold_ref,
    decay_ref,
    end_ref,
    window,
    state,
    pref,
):
    u = pl.program_id(0)
    c = pl.program_id(1)
    heads = step_ref.shape[1]
    pairs = heads // 2
    inner = pairs * LANES
    n_state = state.shape[0]

    @pl.when(c == 0)
    def _():
        window[0:8, :] = edge_ref[0].astype(F32)
        state[...] = jnp.zeros_like(state)
        pref[...] = jnp.zeros_like(pref)

    @pl.when(c > 0)
    def _():
        window[0:8, :] = window[CHUNK : CHUNK + 8, :]

    window[8 : CHUNK + 8, :] = conv_ref[0].astype(F32)
    total = cb_ref[...]
    for k in range(4):
        total = total + cw_ref[k : k + 1, :] * window[5 + k : 5 + k + CHUNK, :]
    xbc = silu(total).astype(BF16)
    xbc_ref[0] = xbc

    position = pos_ref[0] + c * CHUNK + iota((heads, CHUNK), 1)
    alive = jnp.where(position < len_ref[u], 1.0, 0.0)
    raw = step_ref[0] + dt_ref[...]
    steps = alive * (jnp.maximum(raw, 0.0) + jnp.log1p(jnp.exp(-jnp.abs(raw))))
    log_decay = -rate_ref[...] * gap_ref[0] * steps
    cum = running_sum(log_decay, False)
    back = running_sum(log_decay, True)
    after = jnp.where(
        iota(back.shape, 1) < CHUNK - 1, pltpu.roll(back, CHUNK - 1, 1), 0.0
    )
    cum_ref[0] = cum
    steps_ref[0] = steps
    weight = jnp.exp(after) * steps
    tot = jnp.broadcast_to(back[:, 0:1], (heads, LANES))

    decay_ref[0, 0] = jnp.exp(pref[...])
    hold_ref[0, 0] = state[...].astype(BF16)
    coef_t = xbc[:, inner : inner + LANES].astype(F32).T[:n_state, :]
    for j in range(pairs):
        lanes = slice(j * LANES, (j + 1) * LANES)
        left = jnp.concatenate(
            [coef_t * weight[2 * j : 2 * j + 1, :], coef_t * weight[2 * j + 1 : 2 * j + 2, :]],
            axis=1,
        ).astype(BF16)
        add = mm(left, pair_rhs(xbc[:, lanes]))
        tot_pair = lane_halves(tot[2 * j : 2 * j + 1, :], tot[2 * j + 1 : 2 * j + 2, :])
        state[:, lanes] = jnp.exp(tot_pair) * state[:, lanes] + add
        pref[:, lanes] = pref[:, lanes] + tot_pair

    @pl.when(c == pl.num_programs(1) - 1)
    def _():
        half = LANES // 2

        def put(user):
            for h in range(heads):
                lanes = slice((h // 2) * LANES, (h // 2 + 1) * LANES)
                value = state[:, lanes]
                low = jnp.broadcast_to(pref[:, lanes], (8, LANES))
                if h % 2 != user:
                    value = pltpu.roll(value, half, 1)
                    low = pltpu.roll(low, half, 1)
                high = low.astype(BF16).astype(F32)
                row = iota((8, LANES), 0)
                extra = jnp.where(row == 0, high, jnp.where(row == 1, low - high, 0.0))
                packed = jnp.concatenate([value, extra], axis=0)
                if user:
                    packed = lane_halves(end_ref[h].astype(F32), packed)
                end_ref[h] = packed.astype(BF16)

        for user in range(2):
            pl.when(u == user)(functools.partial(put, user))


def chunk_states(lens, pos, conv, edge, step, gap, cw, cb, dt, rate, n_state):
    users, events, conv_dim = conv.shape
    heads = step.shape[1]
    inner = conv_dim - 2 * n_state
    chunks = events // CHUNK
    smem = pl.BlockSpec(memory_space=pltpu.SMEM)
    head_block = pl.BlockSpec((1, heads, CHUNK), lambda u, c: (u, 0, c))
    return pl.pallas_call(
        states_kernel,
        out_shape=(
            jax.ShapeDtypeStruct((users, events, conv_dim), BF16),
            jax.ShapeDtypeStruct((users, heads, events), F32),
            jax.ShapeDtypeStruct((users, heads, events), F32),
            jax.ShapeDtypeStruct((users, chunks, n_state, inner), BF16),
            jax.ShapeDtypeStruct((users, chunks, 1, inner), F32),
            jax.ShapeDtypeStruct((heads, n_state + 8, LANES), BF16),
        ),
        grid=(users, chunks),
        in_specs=[
            smem,
            smem,
            pl.BlockSpec((1, CHUNK, conv_dim), lambda u, c: (u, c, 0)),
            pl.BlockSpec((1, 8, conv_dim), lambda u, c: (u, 0, 0)),
            head_block,
            pl.BlockSpec((1, 1, CHUNK), lambda u, c: (u, 0, c)),
            full(cw.shape),
            full(cb.shape),
            full(dt.shape),
            full(rate.shape),
        ],
        out_specs=(
            pl.BlockSpec((1, CHUNK, conv_dim), lambda u, c: (u, c, 0)),
            head_block,
            head_block,
            pl.BlockSpec((1, 1, n_state, inner), lambda u, c: (u, c, 0, 0)),
            pl.BlockSpec((1, 1, 1, inner), lambda u, c: (u, c, 0, 0)),
            full((heads, n_state + 8, LANES)),
        ),
        scratch_shapes=[
            pltpu.VMEM((CHUNK + 8, conv_dim), F32),
            pltpu.VMEM((n_state, inner), F32),
            pltpu.VMEM((1, inner), F32),
        ],
        compiler_params=params(2),
        name="chunk_states",
    )(lens, pos, conv, edge, step, gap, cw, cb, dt, rate)


def scan_kernel(in_ref, out_ref):
    spans, rows, lanes = in_ref.shape
    n_state = rows - 8
    running = jnp.zeros((n_state, lanes), F32)
    for k in range(spans):
        out_ref[k] = running.astype(BF16)
        block = in_ref[k].astype(F32)
        log_decay = block[n_state : n_state + 1, :] + block[n_state + 1 : n_state + 2, :]
        running = jnp.exp(log_decay) * running + block[:n_state, :]


def scan_spans(ends):
    spans, rows, lanes = ends.shape
    return pl.pallas_call(
        scan_kernel,
        out_shape=jax.ShapeDtypeStruct((spans, rows - 8, lanes), BF16),
        compiler_params=params(0),
        name="scan_spans",
    )(ends)


def local_kernel(xbc_ref, cum_ref, steps_ref, y_ref):
    heads = cum_ref.shape[1]
    pairs = heads // 2
    inner = pairs * LANES
    half = LANES // 2
    xbc = xbc_ref[0]
    in_coef = xbc[:, inner : inner + half]
    out_coef = xbc[:, inner + half : inner + LANES]
    scores = nt(out_coef, in_coef)
    causal = iota((CHUNK, CHUNK), 0) >= iota((CHUNK, CHUNK), 1)
    scores = jnp.where(causal, scores, 0.0)
    cum = cum_ref[0]
    steps = steps_ref[0]
    cum_t = jnp.concatenate([cum, jnp.zeros((LANES - heads, CHUNK), F32)], axis=0).T

    def mixing(h):
        spread = jnp.broadcast_to(cum_t[:, h : h + 1], (CHUNK, CHUNK)) - cum[h : h + 1, :]
        fading = jnp.exp(jnp.minimum(spread, 0.0))
        return (scores * fading * steps[h : h + 1, :]).astype(BF16)

    for j in range(pairs):
        lanes = slice(j * LANES, (j + 1) * LANES)
        left = jnp.concatenate([mixing(2 * j), mixing(2 * j + 1)], axis=1)
        y_ref[0, :, lanes] = mm(left, pair_rhs(xbc[:, lanes])).astype(BF16)


def local_response(xbc, cum, steps, inner):
    users, events, conv_dim = xbc.shape
    heads = cum.shape[1]
    head_block = pl.BlockSpec((1, heads, CHUNK), lambda u, c: (u, 0, c))
    return pl.pallas_call(
        local_kernel,
        out_shape=jax.ShapeDtypeStruct((users, events, inner), BF16),
        grid=(users, events // CHUNK),
        in_specs=[
            pl.BlockSpec((1, CHUNK, conv_dim), lambda u, c: (u, c, 0)),
            head_block,
            head_block,
        ],
        out_specs=pl.BlockSpec((1, CHUNK, inner), lambda u, c: (u, c, 0)),
        compiler_params=params(2),
        name="local_response",
    )(xbc, cum, steps)


def finish_kernel(
    len_ref,
    pos_ref,
    y_ref,
    coef_ref,
    gate_ref,
    x_ref,
    cum_ref,
    hold_ref,
    decay_ref,
    hin_ref,
    gain_ref,
    w_ref,
    out_ref,
    incoming,
    gated_ref,
    normed_ref,
):
    u = pl.program_id(0)
    c = pl.program_id(1)
    heads = cum_ref.shape[1]
    pairs = heads // 2
    half = LANES // 2

    def take(user):
        for j in range(pairs):
            a = hin_ref[2 * j].astype(F32)
            b = hin_ref[2 * j + 1].astype(F32)
            if user:
                a = pltpu.roll(a, half, 1)
            else:
                b = pltpu.roll(b, half, 1)
            incoming[:, j * LANES : (j + 1) * LANES] = lane_halves(a, b)

    for user in range(2):
        pl.when((c == 0) & (u == user))(functools.partial(take, user))

    held = (hold_ref[0, 0].astype(F32) + decay_ref[0, 0] * incoming[...]).astype(BF16)
    carried = mm(coef_ref[0][:, half:], held)
    cum = cum_ref[0]
    cum_t = jnp.concatenate([cum, jnp.zeros((LANES - heads, CHUNK), F32)], axis=0).T
    size = 2 * LANES
    same = jnp.where(
        iota((size, size), 0) // half == iota((size, size), 1) // half, 1.0 / half, 0.0
    ).astype(BF16)
    for j in range(pairs):
        lanes = slice(j * LANES, (j + 1) * LANES)
        fade = jnp.exp(
            lane_halves(
                jnp.broadcast_to(cum_t[:, 2 * j : 2 * j + 1], (CHUNK, LANES)),
                jnp.broadcast_to(cum_t[:, 2 * j + 1 : 2 * j + 2], (CHUNK, LANES)),
            )
        )
        response = y_ref[0, :, lanes].astype(F32) + fade * carried[:, lanes]
        gated_ref[:, lanes] = response * silu(gate_ref[0, :, lanes].astype(F32))
    for j in range(pairs // 2):
        lanes = slice(j * size, (j + 1) * size)
        gated = gated_ref[:, lanes]
        mean = mm((gated * gated).astype(BF16), same)
        normed_ref[:, lanes] = (gated * lax.rsqrt(mean + EPS) * gain_ref[:, lanes]).astype(BF16)
    mixed = mm(normed_ref[...], w_ref[...])
    position = pos_ref[0] + c * CHUNK + iota((CHUNK, 1), 0)
    alive = jnp.where(position < len_ref[u], 1.0, 0.0)
    out_ref[0] = (alive * (x_ref[0].astype(F32) + mixed)).astype(BF16)


def finish(lens, pos, y, xbc, gate, x, cum, hold, decay, hin, gain, weight):
    users, events, inner = y.shape
    heads = cum.shape[1]
    n_state = hold.shape[2]
    dim = x.shape[2]
    smem = pl.BlockSpec(memory_space=pltpu.SMEM)
    block = lambda width: pl.BlockSpec((1, CHUNK, width), lambda u, c: (u, c, 0))
    return pl.pallas_call(
        finish_kernel,
        out_shape=jax.ShapeDtypeStruct((users, events, dim), BF16),
        grid=(users, events // CHUNK),
        in_specs=[
            smem,
            smem,
            block(inner),
            pl.BlockSpec((1, CHUNK, LANES), lambda u, c: (u, c, inner // LANES)),
            block(inner),
            block(dim),
            pl.BlockSpec((1, heads, CHUNK), lambda u, c: (u, 0, c)),
            pl.BlockSpec((1, 1, n_state, inner), lambda u, c: (u, c, 0, 0)),
            pl.BlockSpec((1, 1, 1, inner), lambda u, c: (u, c, 0, 0)),
            full(hin.shape),
            full(gain.shape),
            full(weight.shape),
        ],
        out_specs=block(dim),
        scratch_shapes=[
            pltpu.VMEM((n_state, inner), F32),
            pltpu.VMEM((CHUNK, inner), F32),
            pltpu.VMEM((CHUNK, inner), BF16),
        ],
        compiler_params=params(2),
        name="finish",
    )(lens, pos, y, xbc, gate, x, cum, hold, decay, hin, gain, weight)


def exchange(values, axes):
    return lax.all_to_all(values, axes, split_axis=0, concat_axis=0, tiled=True)


def per_device(
    item_owner,
    item_row,
    history_len,
    event_gap,
    item_table,
    norm_gain,
    in_weight,
    conv_weight,
    conv_bias,
    dt_bias,
    decay_rate,
    out_gain,
    emitted_projection,
):
    users, events = item_row.shape
    dim = item_table.shape[1]
    heads = dt_bias.shape[0]
    inner = emitted_projection.shape[0]
    conv_dim = conv_weight.shape[1]
    n_state = (conv_dim - inner) // 2
    times = lax.axis_size("tm")
    devices = times * lax.axis_size("table")
    cap = 2 * events // devices
    slots = users * cap
    everyone = ("tm", "table")
    pos = (lax.axis_index("tm") * events).reshape(1).astype(jnp.int32)

    requests, place = route(item_owner[..., 0], item_row, devices, cap, 32)
    asked = exchange(requests, everyone)
    rows = fetch(asked, item_table, slots)
    got = exchange(rows.reshape(devices, slots, dim), everyone)
    x, gate, conv, step, tail = project(
        got, place, norm_gain[None, :], in_weight, inner, conv_dim, heads
    )
    edge = lax.ppermute(tail, "tm", [(i, i + 1) for i in range(times - 1)])
    xbc, cum, steps, hold, decay, ends = chunk_states(
        history_len,
        pos,
        conv,
        edge,
        step,
        event_gap[:, None, :],
        conv_weight,
        conv_bias[None, :],
        dt_bias[:, None],
        decay_rate[:, None],
        n_state,
    )
    by_head = exchange(ends, "tm")
    y = local_response(xbc, cum, steps, inner)
    hin = exchange(scan_spans(by_head), "tm")
    return finish(
        history_len,
        pos,
        y,
        xbc,
        gate,
        x,
        cum,
        hold,
        decay,
        hin,
        out_gain[None, :],
        emitted_projection,
    )


def solution(mesh):
    in_specs = (
        P("table", "tm", None),
        P("table", "tm"),
        P("table"),
        P("table", "tm"),
        P(("tm", "table"), None),
        P(),
        P(),
        P(),
        P(),
        P(),
        P(),
        P(),
        P(),
    )
    out_specs = P("table", "tm", None)
    return jax.shard_map(
        per_device, mesh=mesh, in_specs=in_specs, out_specs=out_specs, check_vma=False
    )
```

```python
import functools

import jax
import jax.numpy as jnp
from jax import lax
from jax.experimental import pallas as pl
from jax.experimental.pallas import tpu as pltpu
from jax.sharding import PartitionSpec as P

F32 = jnp.float32
BF16 = jnp.bfloat16
EPS = 1e-05
LANES = 128
CHUNK = 128
TABLE_STEP = 512
FINISH_ROWS = 256
VMEM_LIMIT = 16 * 1024 * 1024


def params(axes):
    return pltpu.CompilerParams(
        dimension_semantics=("arbitrary",) * axes, vmem_limit_bytes=VMEM_LIMIT
    )


ON_CHIP = pl.BlockSpec(memory_space=pltpu.VMEM)
SCALARS = pl.BlockSpec(memory_space=pltpu.SMEM)


def near(array):
    return pltpu.with_memory_space_constraint(array, pltpu.VMEM)


def iota(shape, axis):
    return lax.broadcasted_iota(jnp.int32, shape, axis)


def nt(a, b):
    return lax.dot_general(a, b, (((1,), (1,)), ((), ())), preferred_element_type=F32)


def mm(a, b):
    return jnp.dot(a, b, preferred_element_type=F32)


def silu(v):
    half = 0.5 * v
    return half + half * jnp.tanh(half)


def route_kernel(owner_ref, row_ref, req_ref, place_ref, *, devices, cap, width):
    users, events = row_ref.shape
    tri = jnp.where(
        (iota((LANES, 2 * LANES), 0) < iota((LANES, 2 * LANES), 1))
        | (iota((LANES, 2 * LANES), 1) >= LANES),
        1.0,
        0.0,
    ).astype(BF16)
    slots = users * cap
    req = jnp.zeros((devices, width), F32)
    for u in range(users):
        running = jnp.zeros((devices, LANES), F32)
        for c in range(events // LANES):
            own = owner_ref[u, :, c * LANES : (c + 1) * LANES]
            row = row_ref[u : u + 1, c * LANES : (c + 1) * LANES]
            hot = iota((devices, LANES), 0) == own
            hot_b = jnp.where(hot, 1.0, 0.0).astype(BF16)
            counts = mm(hot_b, tri)
            rank = counts[:, :LANES] + running
            running = running + counts[:, LANES:]
            slot = jnp.sum(jnp.where(hot, rank, 0.0), axis=0, keepdims=True).astype(jnp.int32)
            slot = slot + u * cap
            match = iota((width, LANES), 0) == slot
            high = jnp.where(match, (row >> 6).astype(F32), 0.0).astype(BF16)
            low = jnp.where(match, (row & 63).astype(F32), 0.0).astype(BF16)
            req = req + 64.0 * nt(hot_b, high) + nt(hot_b, low)
            place = (own * (slots * 2 // 3) + slot - u * (slots // 3)).astype(F32)
            place_ref[u, c * LANES : (c + 1) * LANES, :] = jnp.broadcast_to(
                place, (LANES, LANES)
            ).T.astype(jnp.int32)
    req_ref[:, 0, :] = req.astype(jnp.int32)


def route(owners, rows, devices, cap, width):
    users, events = rows.shape
    return pl.pallas_call(
        functools.partial(route_kernel, devices=devices, cap=cap, width=width),
        out_shape=(
            jax.ShapeDtypeStruct((devices, 1, width), jnp.int32),
            pltpu.VMEM((users, events, LANES), jnp.int32),
        ),
        out_specs=(ON_CHIP, ON_CHIP),
        compiler_params=params(0),
        name="route",
    )(owners, rows)


def spread_kernel(tab_ref, out_ref):
    i = pl.program_id(0)
    step, dim = tab_ref.shape
    tiles = dim // LANES
    for cb in range(tiles):
        out_ref[pl.ds(i * step * tiles + cb, step, stride=tiles), :] = tab_ref[
            :, cb * LANES : (cb + 1) * LANES
        ].astype(F32)


def spread(table):
    items, dim = table.shape
    return pl.pallas_call(
        spread_kernel,
        out_shape=pltpu.VMEM((items * (dim // LANES), LANES), F32),
        grid=(items // TABLE_STEP,),
        in_specs=[pl.BlockSpec((TABLE_STEP, dim), lambda i: (i, 0))],
        out_specs=ON_CHIP,
        compiler_params=params(1),
        name="spread",
    )(table)


def fetch_kernel(idx_ref, tab_ref, out_ref, rows_ref, *, slots):
    owners = idx_ref.shape[0]
    tiles = out_ref.shape[1] // LANES

    def body(o, carry):
        base = pl.multiple_of(o * slots * tiles, 8)
        for s in range(slots):
            r = idx_ref[o, 0, s]
            rows_ref[pl.ds(base + tiles * s, tiles), :] = tab_ref[
                pl.ds(pl.multiple_of(r * tiles, tiles), tiles), :
            ]
        return carry

    lax.fori_loop(0, owners, body, 0)

    def pack(g, carry):
        for part in range(4):
            for cb in range(tiles):
                start = (g * 4 + part) * 16 * tiles + cb
                out_ref[
                    pl.ds(pl.multiple_of((g * 4 + part) * 16, 16), 16),
                    cb * LANES : (cb + 1) * LANES,
                ] = rows_ref[pl.ds(start, 16, stride=tiles), :].astype(BF16)
        return carry

    lax.fori_loop(0, owners * slots // 64, pack, 0)


def fetch(idx, table, slots, dim):
    owners = idx.shape[0]
    return pl.pallas_call(
        functools.partial(fetch_kernel, slots=slots),
        out_shape=jax.ShapeDtypeStruct((owners * slots, dim), BF16),
        in_specs=[SCALARS, ON_CHIP],
        scratch_shapes=[pltpu.VMEM((owners * slots * (dim // LANES), LANES), F32)],
        compiler_params=params(0),
        name="fetch",
    )(idx, near(table))


def choose_kernel(place_ref, out_ref):
    users, events, _ = place_ref.shape
    width = out_ref.shape[1]
    rows = LANES

    def body(i, carry):
        at = pl.ds(pl.multiple_of(i * rows, rows), rows)
        for u in range(users):
            place = place_ref[u, at, :]
            to = pl.ds(pl.multiple_of(u * events + i * rows, rows), rows)
            for k in range(width // LANES):
                out_ref[to, k * LANES : (k + 1) * LANES] = jnp.where(
                    place == iota((rows, LANES), 1) + k * LANES, 1.0, 0.0
                ).astype(BF16)
        return carry

    lax.fori_loop(0, events // rows, body, 0)


def choose(place, width):
    users, events, _ = place.shape
    return pl.pallas_call(
        choose_kernel,
        out_shape=pltpu.VMEM((users * events, width), BF16),
        in_specs=[ON_CHIP],
        out_specs=ON_CHIP,
        compiler_params=params(0),
        name="choose",
    )(near(place))


def project_kernel(
    got_ref, hot_ref, gain_ref, w_ref, x_ref, normed_ref, conv_ref, step_ref, tail_ref, *, inner
):
    owners, slots, dim = got_ref.shape
    users, events, conv_dim = conv_ref.shape
    heads = step_ref.shape[1]
    window = slots * 2 // 3
    for u in range(users):
        shift = u * (slots // 3)
        got = got_ref[:, shift : shift + window, :].reshape(owners * window, dim)
        x = mm(hot_ref[u * events : (u + 1) * events, :], got)
        x_ref[u] = x.astype(BF16)
        normed = x * lax.rsqrt(jnp.mean(x * x, axis=-1, keepdims=True) + EPS) * gain_ref[...]
        normed = normed.astype(BF16)
        normed_ref[u] = normed
        conv = mm(normed, w_ref[:, inner : inner + conv_dim]).astype(BF16)
        conv_ref[u] = conv
        tail_ref[u] = conv[events - 8 :, :]
        raw = mm(normed, w_ref[:, inner + conv_dim : inner + conv_dim + heads])
        step_ref[u] = raw.astype(BF16).astype(F32).T


def project(got, hot, gain, weight, inner, conv_dim, heads, users):
    events = hot.shape[0] // users
    dim = got.shape[2]
    return pl.pallas_call(
        functools.partial(project_kernel, inner=inner),
        out_shape=(
            pltpu.VMEM((users, events, dim), BF16),
            pltpu.VMEM((users, events, dim), BF16),
            pltpu.VMEM((users, events, conv_dim), BF16),
            pltpu.VMEM((users, heads, events), F32),
            jax.ShapeDtypeStruct((users, 8, conv_dim), BF16),
        ),
        in_specs=[ON_CHIP] * 4,
        out_specs=(ON_CHIP,) * 5,
        compiler_params=params(0),
        name="project",
    )(near(got), near(hot), gain, near(weight))


def lane_halves(rows_a, rows_b):
    return jnp.where(iota(rows_a.shape, rows_a.ndim - 1) < LANES // 2, rows_a, rows_b)


def running_sums(values):
    lane = iota(values.shape, 1)
    size = values.shape[1]
    ahead, back = values, values
    k = 1
    while k < size:
        ahead = ahead + jnp.where(lane >= k, pltpu.roll(ahead, k, 1), 0.0)
        back = back + jnp.where(lane < size - k, pltpu.roll(back, size - k, 1), 0.0)
        k *= 2
    return ahead, back


def pair_rhs(pair):
    low = iota(pair.shape, 1) < LANES // 2
    zero = jnp.zeros_like(pair)
    return jnp.concatenate([jnp.where(low, pair, zero), jnp.where(low, zero, pair)], axis=0)


def column(row):
    size = row.shape[1]
    return jnp.sum(
        jnp.where(iota((size, size), 0) == iota((size, size), 1), row, 0.0), axis=1, keepdims=True
    )


def states_kernel(
    len_ref,
    pos_ref,
    conv_ref,
    edge_ref,
    step_ref,
    gap_ref,
    cw_ref,
    cb_ref,
    dt_ref,
    rate_ref,
    xbc_ref,
    cum_ref,
    steps_ref,
    hold_ref,
    decay_ref,
    end_ref,
    prev,
    moves,
    weights,
    totals,
    state,
    pref,
):
    users, events, conv_dim = conv_ref.shape
    heads = step_ref.shape[1]
    chunks = events // CHUNK
    pairs = heads // 2
    inner = pairs * LANES
    n_state = state.shape[1]
    half = LANES // 2

    dt = column(dt_ref[...])
    rate = column(rate_ref[...])
    steps_all, decay_all = [], []
    for c in range(chunks):
        lanes = slice(c * CHUNK, (c + 1) * CHUNK)
        for u in range(users):
            position = pos_ref[0] + c * CHUNK + iota((heads, CHUNK), 1)
            alive = jnp.where(position < len_ref[u], 1.0, 0.0)
            raw = step_ref[u, :, lanes] + dt
            steps = alive * (jnp.maximum(raw, 0.0) + jnp.log1p(jnp.exp(-jnp.abs(raw))))
            steps_all.append(steps)
            decay_all.append(-rate * gap_ref[u : u + 1, lanes] * steps)
    steps = jnp.concatenate(steps_all, axis=0)
    ahead, back = running_sums(jnp.concatenate(decay_all, axis=0))
    after = jnp.where(iota(back.shape, 1) < CHUNK - 1, pltpu.roll(back, CHUNK - 1, 1), 0.0)
    cum_ref[...] = ahead
    steps_ref[...] = steps
    weights[...] = jnp.exp(after) * steps
    totals[...] = jnp.broadcast_to(back[:, 0:1], totals.shape)

    state[...] = jnp.zeros_like(state)
    pref[...] = jnp.zeros_like(pref)
    prev[:, 0:8, :] = jnp.zeros((users, 8, conv_dim), BF16)
    prev[:, 8:16, :] = edge_ref[...]
    for k in range(3):
        source = iota((CHUNK, CHUNK + 16), 0) - (3 - k)
        source = jnp.where(source < 0, source + CHUNK + 16, source)
        moves[k] = jnp.where(source == iota((CHUNK, CHUNK + 16), 1), 1.0, 0.0).astype(BF16)

    def chunk(c, carry):
        for u in range(users):
            time = pl.ds(pl.multiple_of(c * CHUNK, CHUNK), CHUNK)
            at = 0
            while at < conv_dim:
                width = min(2 * LANES, conv_dim - at)
                cols = slice(at, at + width)
                here = conv_ref[u, time, cols]
                both = jnp.concatenate([here, prev[u, :, cols]], axis=0)
                prev[u, :, cols] = here[CHUNK - 16 :, :]
                total = cb_ref[:, cols] + cw_ref[3:4, cols] * here.astype(F32)
                for k in range(3):
                    total = total + cw_ref[k : k + 1, cols] * mm(moves[k], both)
                xbc_ref[u, time, cols] = silu(total).astype(BF16)
                at += width
            decay_ref[u, c] = jnp.exp(pref[u])
            hold_ref[u, c] = state[u].astype(BF16)
            coef_t = xbc_ref[u, time, inner : inner + LANES].astype(F32).T[:n_state, :]
            first = pl.multiple_of((c * users + u) * heads, heads)
            weight = weights[pl.ds(first, heads), :]
            total = totals[pl.ds(first, heads), :]
            for j in range(pairs):
                lanes = slice(j * LANES, (j + 1) * LANES)
                a, b = 2 * j, 2 * j + 1
                left = jnp.concatenate(
                    [coef_t * weight[a : a + 1, :], coef_t * weight[b : b + 1, :]], axis=1
                ).astype(BF16)
                add = mm(left, pair_rhs(xbc_ref[u, time, lanes]))
                tot = lane_halves(total[a : a + 1, :], total[b : b + 1, :])
                state[u, :, lanes] = jnp.exp(tot) * state[u, :, lanes] + add
                pref[u, :, lanes] = pref[u, :, lanes] + tot
        return carry

    lax.fori_loop(0, chunks, chunk, 0)

    for h in range(heads):
        lanes = slice((h // 2) * LANES, (h // 2 + 1) * LANES)
        parts = []
        for u in range(users):
            value = state[u, :, lanes]
            low = jnp.broadcast_to(pref[u, :, lanes], (8, LANES))
            if h % 2 != u:
                value = pltpu.roll(value, half, 1)
                low = pltpu.roll(low, half, 1)
            high = low.astype(BF16).astype(F32)
            row = iota((8, LANES), 0)
            extra = jnp.where(row == 0, high, jnp.where(row == 1, low - high, 0.0))
            parts.append(jnp.concatenate([value, extra], axis=0))
        end_ref[h] = lane_halves(*parts).astype(BF16)


def chunk_states(lens, pos, conv, edge, step, gap, cw, cb, dt, rate, n_state):
    users, events, conv_dim = conv.shape
    heads = step.shape[1]
    inner = conv_dim - 2 * n_state
    chunks = events // CHUNK
    lines = chunks * users * heads
    return pl.pallas_call(
        states_kernel,
        out_shape=(
            pltpu.VMEM((users, events, conv_dim), BF16),
            pltpu.VMEM((lines, CHUNK), F32),
            pltpu.VMEM((lines, CHUNK), F32),
            pltpu.VMEM((users, chunks, n_state, inner), BF16),
            pltpu.VMEM((users, chunks, 1, inner), F32),
            jax.ShapeDtypeStruct((heads, n_state + 8, LANES), BF16),
        ),
        in_specs=[SCALARS] * 2 + [ON_CHIP] * 8,
        out_specs=(ON_CHIP,) * 6,
        scratch_shapes=[
            pltpu.VMEM((users, 16, conv_dim), BF16),
            pltpu.VMEM((3, CHUNK, CHUNK + 16), BF16),
            pltpu.VMEM((lines, CHUNK), F32),
            pltpu.VMEM((lines, LANES), F32),
            pltpu.VMEM((users, n_state, inner), F32),
            pltpu.VMEM((users, 1, inner), F32),
        ],
        compiler_params=params(0),
        name="chunk_states",
    )(lens, pos, near(conv), near(edge), near(step), gap, cw, cb, dt, rate)


def scan_kernel(in_ref, out_ref):
    spans, rows, lanes = in_ref.shape
    n_state = rows - 8
    running = jnp.zeros((n_state, lanes), F32)
    for k in range(spans):
        out_ref[k] = running.astype(BF16)
        block = in_ref[k].astype(F32)
        log_decay = block[n_state : n_state + 1, :] + block[n_state + 1 : n_state + 2, :]
        running = jnp.exp(log_decay) * running + block[:n_state, :]


def scan_spans(ends):
    spans, rows, lanes = ends.shape
    return pl.pallas_call(
        scan_kernel,
        out_shape=jax.ShapeDtypeStruct((spans, rows - 8, lanes), BF16),
        in_specs=[ON_CHIP],
        out_specs=ON_CHIP,
        compiler_params=params(0),
        name="scan_spans",
    )(near(ends))


def local_kernel(normed_ref, w_ref, xbc_ref, cum_ref, steps_ref, y_ref, fade_ref, gates, *, user):
    events, inner = y_ref.shape
    users = xbc_ref.shape[0]
    chunks = events // CHUNK
    heads = cum_ref.shape[0] // (users * chunks)
    pairs = heads // 2
    half = LANES // 2

    def chunk(c, carry):
        time = pl.ds(pl.multiple_of(c * CHUNK, CHUNK), CHUNK)
        gates[...] = silu(mm(normed_ref[user, time, :], w_ref[:, :inner]).astype(BF16).astype(F32))
        coef = xbc_ref[user, time, inner : inner + LANES]
        scores = nt(coef[:, half:], coef[:, :half])
        causal = iota((CHUNK, CHUNK), 0) >= iota((CHUNK, CHUNK), 1)
        scores = jnp.where(causal, scores, 0.0)
        first = pl.multiple_of((c * users + user) * heads, heads)
        cum = cum_ref[pl.ds(first, heads), :]
        steps = steps_ref[pl.ds(first, heads), :]
        cum_t = jnp.concatenate([cum, jnp.zeros((LANES - heads, CHUNK), F32)], axis=0).T

        def mixing(h):
            own = jnp.broadcast_to(cum_t[:, h : h + 1], (CHUNK, CHUNK))
            fading = jnp.exp(jnp.minimum(own - cum[h : h + 1, :], 0.0))
            return own, (scores * fading * steps[h : h + 1, :]).astype(BF16)

        for j in range(pairs):
            lanes = slice(j * LANES, (j + 1) * LANES)
            own_a, mix_a = mixing(2 * j)
            own_b, mix_b = mixing(2 * j + 1)
            left = jnp.concatenate([mix_a, mix_b], axis=1)
            gate = gates[:, lanes]
            y_ref[time, lanes] = gate * mm(left, pair_rhs(xbc_ref[user, time, lanes]))
            fade_ref[time, lanes] = gate * jnp.exp(lane_halves(own_a, own_b))
        return carry

    lax.fori_loop(0, chunks, chunk, 0)


def local_response(normed, weight, xbc, cum, steps, inner, user):
    events = xbc.shape[1]
    return pl.pallas_call(
        functools.partial(local_kernel, user=user),
        out_shape=(pltpu.VMEM((events, inner), F32), pltpu.VMEM((events, inner), F32)),
        in_specs=[ON_CHIP] * 5,
        out_specs=(ON_CHIP, ON_CHIP),
        scratch_shapes=[pltpu.VMEM((CHUNK, inner), F32)],
        compiler_params=params(0),
        name="local_response",
    )(near(normed), near(weight), near(xbc), near(cum), near(steps))


def finish_kernel(
    len_ref,
    pos_ref,
    y0_ref,
    y1_ref,
    fade0_ref,
    fade1_ref,
    xbc_ref,
    x_ref,
    hold_ref,
    decay_ref,
    hin_ref,
    gain_ref,
    w_ref,
    out_ref,
    incoming,
    same,
    normed,
):
    u = pl.program_id(0)
    b = pl.program_id(1)
    heads = hin_ref.shape[0]
    pairs = heads // 2
    inner = pairs * LANES
    half = LANES // 2
    size = 2 * LANES
    rows = out_ref.shape[1]

    @pl.when((u == 0) & (b == 0))
    def _():
        same[...] = jnp.where(
            iota((size, size), 0) // half == iota((size, size), 1) // half, 1.0 / half, 0.0
        ).astype(BF16)
        for j in range(pairs):
            a = hin_ref[2 * j].astype(F32)
            b = hin_ref[2 * j + 1].astype(F32)
            lanes = slice(j * LANES, (j + 1) * LANES)
            incoming[0, :, lanes] = lane_halves(a, pltpu.roll(b, half, 1))
            incoming[1, :, lanes] = lane_halves(pltpu.roll(a, half, 1), b)

    def work(y_ref, fade_ref):
        for part in range(rows // CHUNK):
            c = b * (rows // CHUNK) + part
            time = pl.ds(pl.multiple_of(c * CHUNK, CHUNK), CHUNK)
            here = slice(part * CHUNK, (part + 1) * CHUNK)
            held = (hold_ref[u, c].astype(F32) + decay_ref[u, c] * incoming[u]).astype(BF16)
            coef = xbc_ref[u, time, inner : inner + LANES][:, half:]
            for j in range(pairs // 2):
                lanes = slice(j * size, (j + 1) * size)
                carried = mm(coef, held[:, lanes])
                gated = y_ref[time, lanes] + fade_ref[time, lanes] * carried
                mean = mm((gated * gated).astype(BF16), same[...])
                normed[here, lanes] = (
                    gated * lax.rsqrt(mean + EPS) * gain_ref[:, lanes]
                ).astype(BF16)
        mixed = mm(normed[...], w_ref[...])
        position = pos_ref[0] + b * rows + iota((rows, 1), 0)
        alive = jnp.where(position < len_ref[u], 1.0, 0.0)
        span = pl.ds(pl.multiple_of(b * rows, rows), rows)
        out_ref[0] = (alive * (x_ref[u, span, :].astype(F32) + mixed)).astype(BF16)

    pl.when(u == 0)(functools.partial(work, y0_ref, fade0_ref))
    pl.when(u == 1)(functools.partial(work, y1_ref, fade1_ref))


def finish(lens, pos, ys, fades, xbc, x, hold, decay, hin, gain, weight):
    events, inner = ys[0].shape
    n_state = hold.shape[2]
    users, _, dim = x.shape
    size = 2 * LANES
    return pl.pallas_call(
        finish_kernel,
        out_shape=jax.ShapeDtypeStruct((users, events, dim), BF16),
        grid=(users, events // FINISH_ROWS),
        in_specs=[SCALARS] * 2 + [ON_CHIP] * 11,
        out_specs=pl.BlockSpec((1, FINISH_ROWS, dim), lambda u, b: (u, b, 0)),
        scratch_shapes=[
            pltpu.VMEM((users, n_state, inner), F32),
            pltpu.VMEM((size, size), BF16),
            pltpu.VMEM((FINISH_ROWS, inner), BF16),
        ],
        compiler_params=params(2),
        name="finish",
    )(
        lens,
        pos,
        *[near(v) for v in (*ys, *fades, xbc, x, hold, decay, hin, gain, weight)],
    )


def exchange(values, axes):
    return lax.all_to_all(values, axes, split_axis=0, concat_axis=0, tiled=True)


def per_device(
    item_owner,
    item_row,
    history_len,
    event_gap,
    item_table,
    norm_gain,
    in_weight,
    conv_weight,
    conv_bias,
    dt_bias,
    decay_rate,
    out_gain,
    emitted_projection,
):
    users, events = item_row.shape
    dim = item_table.shape[1]
    heads = dt_bias.shape[0]
    inner = emitted_projection.shape[0]
    conv_dim = conv_weight.shape[1]
    n_state = (conv_dim - inner) // 2
    times = lax.axis_size("tm")
    devices = times * lax.axis_size("table")
    cap = 2 * events // devices
    slots = users * cap
    everyone = ("tm", "table")
    pos = (lax.axis_index("tm") * events).reshape(1).astype(jnp.int32)

    requests, place = route(jnp.swapaxes(item_owner, 1, 2), item_row, devices, cap, 32)
    asked = exchange(requests, everyone)
    rows = fetch(asked, spread(item_table), slots, dim)
    got = exchange(rows.reshape(devices, slots, dim), everyone)
    hot = choose(place, devices * (slots * 2 // 3))
    x, normed, conv, step, tail = project(
        got, hot, norm_gain[None, :], in_weight, inner, conv_dim, heads, users
    )
    edge = lax.ppermute(tail, "tm", [(i, i + 1) for i in range(times - 1)])
    xbc, cum, steps, hold, decay, ends = chunk_states(
        history_len,
        pos,
        conv,
        edge,
        step,
        event_gap,
        conv_weight,
        conv_bias[None, :],
        dt_bias[None, :],
        decay_rate[None, :],
        n_state,
    )
    by_head = exchange(ends, "tm")
    ys, fades = zip(
        *[local_response(normed, in_weight, xbc, cum, steps, inner, u) for u in range(users)]
    )
    hin = exchange(scan_spans(by_head), "tm")
    return finish(
        history_len,
        pos,
        ys,
        fades,
        xbc,
        x,
        hold,
        decay,
        hin,
        out_gain[None, :],
        emitted_projection,
    )


def solution(mesh):
    in_specs = (
        P("table", "tm", None),
        P("table", "tm"),
        P("table"),
        P("table", "tm"),
        P(("tm", "table"), None),
        P(),
        P(),
        P(),
        P(),
        P(),
        P(),
        P(),
        P(),
    )
    out_specs = P("table", "tm", None)
    return jax.shard_map(
        per_device, mesh=mesh, in_specs=in_specs, out_specs=out_specs, check_vma=False
    )
```

```python
import functools

import jax
import jax.numpy as jnp
from jax import lax
from jax.experimental import pallas as pl
from jax.experimental.pallas import tpu as pltpu
from jax.sharding import PartitionSpec as P

F32 = jnp.float32
BF16 = jnp.bfloat16
EPS = 1e-05
LANES = 128
CHUNK = 128
TABLE_STEP = 512
FINISH_ROWS = 256
MEBI = 1024 * 1024


def params(axes, mebi=16):
    return pltpu.CompilerParams(
        dimension_semantics=("arbitrary",) * axes, vmem_limit_bytes=mebi * MEBI
    )


def full(shape):
    return pl.BlockSpec(shape, lambda *_: (0,) * len(shape))


def first_position(events):
    return lax.axis_index("tm") * events


ON_CHIP = pl.BlockSpec(memory_space=pltpu.VMEM)
SCALARS = pl.BlockSpec(memory_space=pltpu.SMEM)


def near(array):
    return pltpu.with_memory_space_constraint(array, pltpu.VMEM)


def far(array):
    return pltpu.with_memory_space_constraint(array, pltpu.HBM)


def iota(shape, axis):
    return lax.broadcasted_iota(jnp.int32, shape, axis)


def nt(a, b):
    return lax.dot_general(a, b, (((1,), (1,)), ((), ())), preferred_element_type=F32)


def mm(a, b):
    return jnp.dot(a, b, preferred_element_type=F32)


def silu(v):
    half = 0.5 * v
    return half + half * jnp.tanh(half)


def route_kernel(owner_ref, row_ref, req_ref, place_ref, *, devices, cap, width):
    users, events = row_ref.shape
    tri = jnp.where(
        (iota((LANES, 2 * LANES), 0) < iota((LANES, 2 * LANES), 1))
        | (iota((LANES, 2 * LANES), 1) >= LANES),
        1.0,
        0.0,
    ).astype(BF16)
    slots = users * cap
    req = jnp.zeros((devices, width), F32)
    for u in range(users):
        running = jnp.zeros((devices, LANES), F32)
        for c in range(events // LANES):
            own = owner_ref[u, :, c * LANES : (c + 1) * LANES]
            row = row_ref[u : u + 1, c * LANES : (c + 1) * LANES]
            hot = iota((devices, LANES), 0) == own
            hot_b = jnp.where(hot, 1.0, 0.0).astype(BF16)
            counts = mm(hot_b, tri)
            rank = counts[:, :LANES] + running
            running = running + counts[:, LANES:]
            slot = jnp.sum(jnp.where(hot, rank, 0.0), axis=0, keepdims=True).astype(jnp.int32)
            slot = slot + u * cap
            match = iota((width, LANES), 0) == slot
            high = jnp.where(match, (row >> 6).astype(F32), 0.0).astype(BF16)
            low = jnp.where(match, (row & 63).astype(F32), 0.0).astype(BF16)
            req = req + 64.0 * nt(hot_b, high) + nt(hot_b, low)
            place = (own * (slots * 2 // 3) + slot - u * (slots // 3)).astype(F32)
            place_ref[u, c * LANES : (c + 1) * LANES, :] = jnp.broadcast_to(
                place, (LANES, LANES)
            ).T.astype(jnp.int32)
    req_ref[:, 0, :] = req.astype(jnp.int32)


def route(owners, rows, devices, cap, width):
    users, events = rows.shape
    return pl.pallas_call(
        functools.partial(route_kernel, devices=devices, cap=cap, width=width),
        out_shape=(
            jax.ShapeDtypeStruct((devices, 1, width), jnp.int32),
            pltpu.HBM((users, events, LANES), jnp.int32),
        ),
        out_specs=(ON_CHIP, ON_CHIP),
        compiler_params=params(0),
        name="route",
    )(owners, rows)


def fetch_kernel(idx_ref, tab_ref, out_ref, wide_ref, rows_ref, *, slots):
    i = pl.program_id(0)
    step, dim = tab_ref.shape
    owners = idx_ref.shape[0]
    tiles = dim // LANES
    for cb in range(tiles):
        wide_ref[pl.ds(i * step * tiles + cb, step, stride=tiles), :] = tab_ref[
            :, cb * LANES : (cb + 1) * LANES
        ].astype(F32)

    @pl.when(i == pl.num_programs(0) - 1)
    def _():
        def body(o, carry):
            base = pl.multiple_of(o * slots * tiles, 8)
            for s in range(slots):
                r = idx_ref[o, 0, s]
                rows_ref[pl.ds(base + tiles * s, tiles), :] = wide_ref[
                    pl.ds(pl.multiple_of(r * tiles, tiles), tiles), :
                ]
            return carry

        lax.fori_loop(0, owners, body, 0)

        def pack(g, carry):
            for part in range(4):
                for cb in range(tiles):
                    start = (g * 4 + part) * 16 * tiles + cb
                    out_ref[
                        pl.ds(pl.multiple_of((g * 4 + part) * 16, 16), 16),
                        cb * LANES : (cb + 1) * LANES,
                    ] = rows_ref[pl.ds(start, 16, stride=tiles), :].astype(BF16)
            return carry

        lax.fori_loop(0, owners * slots // 64, pack, 0)


def fetch(idx, table, slots):
    owners = idx.shape[0]
    items, dim = table.shape
    tiles = dim // LANES
    return pl.pallas_call(
        functools.partial(fetch_kernel, slots=slots),
        out_shape=jax.ShapeDtypeStruct((owners * slots, dim), BF16),
        grid=(items // TABLE_STEP,),
        in_specs=[SCALARS, pl.BlockSpec((TABLE_STEP, dim), lambda i: (i, 0))],
        out_specs=full((owners * slots, dim)),
        scratch_shapes=[
            pltpu.VMEM((items * tiles, LANES), F32),
            pltpu.VMEM((owners * slots * tiles, LANES), F32),
        ],
        compiler_params=params(1, 26),
        name="fetch",
    )(idx, far(table))


def project_kernel(
    got_ref, place_ref, gain_ref, w_ref, x_ref, normed_ref, conv_ref, step_ref, tail_ref, hot
):
    u = pl.program_id(0)
    owners, slots, dim = got_ref.shape
    events, width = hot.shape
    conv_dim = conv_ref.shape[2]
    heads = step_ref.shape[1]
    window = slots * 2 // 3
    rows = LANES
    for i in range(events // rows):
        at = slice(i * rows, (i + 1) * rows)
        place = place_ref[0, at, :]
        for k in range(width // LANES):
            hot[at, k * LANES : (k + 1) * LANES] = jnp.where(
                place == iota((rows, LANES), 1) + k * LANES, 1.0, 0.0
            ).astype(BF16)
    shift = pl.multiple_of(u * (slots // 3), 8)
    got = got_ref[:, pl.ds(shift, window), :].reshape(owners * window, dim)
    x = mm(hot[...], got)
    x_ref[0] = x.astype(BF16)
    normed = x * lax.rsqrt(jnp.mean(x * x, axis=-1, keepdims=True) + EPS) * gain_ref[...]
    normed = normed.astype(BF16)
    normed_ref[0] = normed
    conv = mm(normed, w_ref[:, :conv_dim]).astype(BF16)
    conv_ref[u] = conv
    tail_ref[u] = conv[events - 8 :, :]
    raw = mm(normed, w_ref[:, conv_dim : conv_dim + heads])
    step_ref[u] = raw.astype(BF16).astype(F32).T


def project(got, place, gain, weight, conv_dim, heads):
    users, events, _ = place.shape
    owners, slots, dim = got.shape
    block = lambda width: pl.BlockSpec((1, events, width), lambda u: (u, 0, 0))
    return pl.pallas_call(
        project_kernel,
        out_shape=(
            pltpu.HBM((users, events, dim), BF16),
            pltpu.HBM((users, events, dim), BF16),
            pltpu.VMEM((users, events, conv_dim), BF16),
            pltpu.VMEM((users, heads, events), F32),
            jax.ShapeDtypeStruct((users, 8, conv_dim), BF16),
        ),
        grid=(users,),
        in_specs=[ON_CHIP, block(LANES), full(gain.shape), ON_CHIP],
        out_specs=(block(dim), block(dim), ON_CHIP, ON_CHIP, full((users, 8, conv_dim))),
        scratch_shapes=[pltpu.VMEM((events, owners * (slots * 2 // 3)), BF16)],
        compiler_params=params(1, 24),
        name="project",
    )(near(got), far(place), gain, near(weight))


def lane_halves(rows_a, rows_b):
    return jnp.where(iota(rows_a.shape, rows_a.ndim - 1) < LANES // 2, rows_a, rows_b)


def running_sums(values):
    lane = iota(values.shape, 1)
    size = values.shape[1]
    ahead, back = values, values
    k = 1
    while k < size:
        ahead = ahead + jnp.where(lane >= k, pltpu.roll(ahead, k, 1), 0.0)
        back = back + jnp.where(lane < size - k, pltpu.roll(back, size - k, 1), 0.0)
        k *= 2
    return ahead, back


def pair_rhs(pair):
    low = iota(pair.shape, 1) < LANES // 2
    zero = jnp.zeros_like(pair)
    return jnp.concatenate([jnp.where(low, pair, zero), jnp.where(low, zero, pair)], axis=0)


def column(row):
    size = row.shape[1]
    return jnp.sum(
        jnp.where(iota((size, size), 0) == iota((size, size), 1), row, 0.0), axis=1, keepdims=True
    )


def states_kernel(
    len_ref,
    conv_ref,
    edge_ref,
    step_ref,
    gap_ref,
    cw_ref,
    cb_ref,
    dt_ref,
    rate_ref,
    xbc_ref,
    cum_ref,
    steps_ref,
    hold_ref,
    decay_ref,
    end_ref,
    prev,
    moves,
    weights,
    totals,
    state,
    pref,
):
    users, events, conv_dim = conv_ref.shape
    heads = step_ref.shape[1]
    chunks = events // CHUNK
    pairs = heads // 2
    inner = pairs * LANES
    n_state = state.shape[1]
    half = LANES // 2

    c = pl.program_id(0)

    @pl.when(c == 0)
    def _():
        dt = column(dt_ref[...])
        rate = column(rate_ref[...])
        start = first_position(events)
        steps_all, decay_all = [], []
        for k in range(chunks):
            lanes = slice(k * CHUNK, (k + 1) * CHUNK)
            for u in range(users):
                position = start + k * CHUNK + iota((heads, CHUNK), 1)
                alive = jnp.where(position < len_ref[u], 1.0, 0.0)
                raw = step_ref[u, :, lanes] + dt
                steps = alive * (jnp.maximum(raw, 0.0) + jnp.log1p(jnp.exp(-jnp.abs(raw))))
                steps_all.append(steps)
                decay_all.append(-rate * gap_ref[u : u + 1, lanes] * steps)
        steps = jnp.concatenate(steps_all, axis=0)
        ahead, back = running_sums(jnp.concatenate(decay_all, axis=0))
        after = jnp.where(iota(back.shape, 1) < CHUNK - 1, pltpu.roll(back, CHUNK - 1, 1), 0.0)
        cum_ref[...] = ahead
        steps_ref[...] = steps
        weights[...] = jnp.exp(after) * steps
        totals[...] = jnp.broadcast_to(back[:, 0:1], totals.shape)
        state[...] = jnp.zeros_like(state)
        pref[...] = jnp.zeros_like(pref)
        prev[:, 0:8, :] = jnp.zeros((users, 8, conv_dim), BF16)
        prev[:, 8:16, :] = edge_ref[...]
        for k in range(3):
            source = iota((CHUNK, CHUNK + 16), 0) - (3 - k)
            source = jnp.where(source < 0, source + CHUNK + 16, source)
            moves[k] = jnp.where(source == iota((CHUNK, CHUNK + 16), 1), 1.0, 0.0).astype(BF16)

    for u in range(users):
        time = pl.ds(pl.multiple_of(c * CHUNK, CHUNK), CHUNK)
        at = 0
        while at < conv_dim:
            width = min(2 * LANES, conv_dim - at)
            cols = slice(at, at + width)
            here = conv_ref[u, time, cols]
            both = jnp.concatenate([here, prev[u, :, cols]], axis=0)
            prev[u, :, cols] = here[CHUNK - 16 :, :]
            total = cb_ref[cols].reshape(1, width) + cw_ref[3:4, cols] * here.astype(F32)
            for k in range(3):
                total = total + cw_ref[k : k + 1, cols] * mm(moves[k], both)
            xbc_ref[u, :, cols] = silu(total).astype(BF16)
            at += width
        decay_ref[u, 0] = jnp.exp(pref[u])
        hold_ref[u, 0] = state[u].astype(BF16)
        coef_t = xbc_ref[u, :, inner : inner + LANES].astype(F32).T[:n_state, :]
        first = pl.multiple_of((c * users + u) * heads, heads)
        weight = weights[pl.ds(first, heads), :]
        total = totals[pl.ds(first, heads), :]
        for j in range(pairs):
            lanes = slice(j * LANES, (j + 1) * LANES)
            a, b = 2 * j, 2 * j + 1
            left = jnp.concatenate(
                [coef_t * weight[a : a + 1, :], coef_t * weight[b : b + 1, :]], axis=1
            ).astype(BF16)
            add = mm(left, pair_rhs(xbc_ref[u, :, lanes]))
            tot = lane_halves(total[a : a + 1, :], total[b : b + 1, :])
            state[u, :, lanes] = jnp.exp(tot) * state[u, :, lanes] + add
            pref[u, :, lanes] = pref[u, :, lanes] + tot

    @pl.when(c == chunks - 1)
    def _():
        for h in range(heads):
            lanes = slice((h // 2) * LANES, (h // 2 + 1) * LANES)
            parts = []
            for u in range(users):
                value = state[u, :, lanes]
                low = jnp.broadcast_to(pref[u, :, lanes], (8, LANES))
                if h % 2 != u:
                    value = pltpu.roll(value, half, 1)
                    low = pltpu.roll(low, half, 1)
                high = low.astype(BF16).astype(F32)
                row = iota((8, LANES), 0)
                extra = jnp.where(row == 0, high, jnp.where(row == 1, low - high, 0.0))
                parts.append(jnp.concatenate([value, extra], axis=0))
            end_ref[h] = lane_halves(*parts).astype(BF16)


def chunk_states(lens, conv, edge, step, gap, cw, cb, dt, rate, n_state):
    users, events, conv_dim = conv.shape
    heads = step.shape[1]
    inner = conv_dim - 2 * n_state
    chunks = events // CHUNK
    lines = chunks * users * heads
    return pl.pallas_call(
        states_kernel,
        out_shape=(
            pltpu.HBM((users, events, conv_dim), BF16),
            pltpu.HBM((lines, CHUNK), F32),
            pltpu.HBM((lines, CHUNK), F32),
            pltpu.HBM((users, chunks, n_state, inner), BF16),
            pltpu.HBM((users, chunks, 1, inner), F32),
            pltpu.HBM((heads, n_state + 8, LANES), BF16),
        ),
        grid=(chunks,),
        in_specs=[SCALARS, ON_CHIP, full(edge.shape), ON_CHIP]
        + [full(v.shape) for v in (gap, cw, cb, dt, rate)],
        out_specs=(
            pl.BlockSpec((users, CHUNK, conv_dim), lambda c: (0, c, 0)),
            full((lines, CHUNK)),
            full((lines, CHUNK)),
            pl.BlockSpec((users, 1, n_state, inner), lambda c: (0, c, 0, 0)),
            pl.BlockSpec((users, 1, 1, inner), lambda c: (0, c, 0, 0)),
            full((heads, n_state + 8, LANES)),
        ),
        scratch_shapes=[
            pltpu.VMEM((users, 16, conv_dim), BF16),
            pltpu.VMEM((3, CHUNK, CHUNK + 16), BF16),
            pltpu.VMEM((lines, CHUNK), F32),
            pltpu.VMEM((lines, LANES), F32),
            pltpu.VMEM((users, n_state, inner), F32),
            pltpu.VMEM((users, 1, inner), F32),
        ],
        compiler_params=params(1),
        name="chunk_states",
    )(lens, near(conv), edge, near(step), gap, cw, cb, dt, rate)


def scan_kernel(in_ref, out_ref):
    spans, rows, lanes = in_ref.shape
    n_state = rows - 8
    running = jnp.zeros((n_state, lanes), F32)
    for k in range(spans):
        out_ref[k] = running.astype(BF16)
        block = in_ref[k].astype(F32)
        log_decay = block[n_state : n_state + 1, :] + block[n_state + 1 : n_state + 2, :]
        running = jnp.exp(log_decay) * running + block[:n_state, :]


def scan_spans(ends):
    spans, rows, lanes = ends.shape
    return pl.pallas_call(
        scan_kernel,
        out_shape=jax.ShapeDtypeStruct((spans, rows - 8, lanes), BF16),
        in_specs=[ON_CHIP],
        out_specs=ON_CHIP,
        compiler_params=params(0),
        name="scan_spans",
    )(near(ends))


def local_kernel(normed_ref, w_ref, xbc_ref, cum_ref, steps_ref, y_ref, fade_ref, gates):
    _, inner = y_ref.shape
    heads = cum_ref.shape[0]
    pairs = heads // 2
    half = LANES // 2
    gates[...] = silu(mm(normed_ref[0], w_ref[...]).astype(BF16).astype(F32))
    coef = xbc_ref[0, :, inner : inner + LANES]
    scores = nt(coef[:, half:], coef[:, :half])
    causal = iota((CHUNK, CHUNK), 0) >= iota((CHUNK, CHUNK), 1)
    scores = jnp.where(causal, scores, 0.0)
    cum = cum_ref[...]
    steps = steps_ref[...]
    cum_t = jnp.concatenate([cum, jnp.zeros((LANES - heads, CHUNK), F32)], axis=0).T

    def mixing(h):
        own = jnp.broadcast_to(cum_t[:, h : h + 1], (CHUNK, CHUNK))
        fading = jnp.exp(jnp.minimum(own - cum[h : h + 1, :], 0.0))
        return own, (scores * fading * steps[h : h + 1, :]).astype(BF16)

    for j in range(pairs):
        lanes = slice(j * LANES, (j + 1) * LANES)
        own_a, mix_a = mixing(2 * j)
        own_b, mix_b = mixing(2 * j + 1)
        left = jnp.concatenate([mix_a, mix_b], axis=1)
        gate = gates[:, lanes]
        y_ref[:, lanes] = gate * mm(left, pair_rhs(xbc_ref[0, :, lanes]))
        fade_ref[:, lanes] = gate * jnp.exp(lane_halves(own_a, own_b))


def local_response(normed, weight, xbc, cum, steps, user):
    users, events, conv_dim = xbc.shape
    dim, inner = weight.shape
    heads = cum.shape[0] * CHUNK // (users * events)
    block = lambda width: pl.BlockSpec((1, CHUNK, width), lambda c: (user, c, 0))
    lines = pl.BlockSpec((heads, CHUNK), lambda c: (c * users + user, 0))
    result = pl.BlockSpec((CHUNK, inner), lambda c: (c, 0))
    return pl.pallas_call(
        local_kernel,
        out_shape=(pltpu.HBM((events, inner), F32),) * 2,
        grid=(events // CHUNK,),
        in_specs=[block(dim), full(weight.shape), block(conv_dim), lines, lines],
        out_specs=(result, result),
        scratch_shapes=[pltpu.VMEM((CHUNK, inner), F32)],
        compiler_params=params(1),
        name="local_response",
    )(*[far(v) for v in (normed, weight, xbc, cum, steps)])


def finish_kernel(
    len_ref,
    y0_ref,
    y1_ref,
    fade0_ref,
    fade1_ref,
    coef_ref,
    x_ref,
    hold_ref,
    decay_ref,
    hin_ref,
    gain_ref,
    w_ref,
    out_ref,
    incoming,
    same,
    normed,
    *,
    blocks,
):
    u = pl.program_id(0) // blocks
    b = pl.program_id(0) % blocks
    heads = hin_ref.shape[0]
    pairs = heads // 2
    half = LANES // 2
    size = 2 * LANES
    rows = out_ref.shape[1]

    @pl.when(pl.program_id(0) == 0)
    def _():
        same[...] = jnp.where(
            iota((size, size), 0) // half == iota((size, size), 1) // half, 1.0 / half, 0.0
        ).astype(BF16)
        for j in range(pairs):
            a = hin_ref[2 * j].astype(F32)
            b = hin_ref[2 * j + 1].astype(F32)
            lanes = slice(j * LANES, (j + 1) * LANES)
            incoming[0, :, lanes] = lane_halves(a, pltpu.roll(b, half, 1))
            incoming[1, :, lanes] = lane_halves(pltpu.roll(a, half, 1), b)

    def work(y_ref, fade_ref):
        for part in range(rows // CHUNK):
            here = slice(part * CHUNK, (part + 1) * CHUNK)
            held = hold_ref[0, part].astype(F32) + decay_ref[0, part] * incoming[u]
            held = held.astype(BF16)
            coef = coef_ref[0, here, half:]
            for j in range(pairs // 2):
                lanes = slice(j * size, (j + 1) * size)
                carried = mm(coef, held[:, lanes])
                gated = y_ref[here, lanes] + fade_ref[here, lanes] * carried
                mean = mm((gated * gated).astype(BF16), same[...])
                normed[here, lanes] = (
                    gated * lax.rsqrt(mean + EPS) * gain_ref[:, lanes]
                ).astype(BF16)
        mixed = mm(normed[...], w_ref[...])
        position = first_position(blocks * rows) + b * rows + iota((rows, 1), 0)
        alive = jnp.where(position < len_ref[u], 1.0, 0.0)
        out_ref[0] = (alive * (x_ref[0].astype(F32) + mixed)).astype(BF16)

    pl.when(u == 0)(functools.partial(work, y0_ref, fade0_ref))
    pl.when(u == 1)(functools.partial(work, y1_ref, fade1_ref))


def finish(lens, ys, fades, xbc, x, hold, decay, hin, gain, weight):
    events, inner = ys[0].shape
    n_state = hold.shape[2]
    users, _, dim = x.shape
    size = 2 * LANES
    rows = FINISH_ROWS
    blocks = events // rows
    parts = rows // CHUNK
    early = pl.BlockSpec((rows, inner), lambda i: (jnp.minimum(i, blocks - 1), 0))
    late = pl.BlockSpec((rows, inner), lambda i: (jnp.maximum(i - blocks, 0), 0))
    block = pl.BlockSpec((1, rows, dim), lambda i: (i // blocks, i % blocks, 0))
    per_chunk = lambda *shape: pl.BlockSpec(
        (1, parts) + shape, lambda i: (i // blocks, i % blocks, 0, 0)
    )
    return pl.pallas_call(
        functools.partial(finish_kernel, blocks=blocks),
        out_shape=jax.ShapeDtypeStruct((users, events, dim), BF16),
        grid=(users * blocks,),
        in_specs=[
            SCALARS,
            early,
            late,
            early,
            late,
            pl.BlockSpec((1, rows, LANES), lambda i: (i // blocks, i % blocks, inner // LANES)),
            block,
            per_chunk(n_state, inner),
            per_chunk(1, inner),
            full(hin.shape),
            full(gain.shape),
            full(weight.shape),
        ],
        out_specs=block,
        scratch_shapes=[
            pltpu.VMEM((users, n_state, inner), F32),
            pltpu.VMEM((size, size), BF16),
            pltpu.VMEM((rows, inner), BF16),
        ],
        compiler_params=params(1, 24),
        name="finish",
    )(lens, *[far(v) for v in (*ys, *fades, xbc, x, hold, decay)], hin, gain, weight)


def exchange(values, axes):
    return lax.all_to_all(values, axes, split_axis=0, concat_axis=0, tiled=True)


def per_device(
    item_owner,
    item_row,
    history_len,
    event_gap,
    item_table,
    norm_gain,
    in_weight,
    conv_weight,
    conv_bias,
    dt_bias,
    decay_rate,
    out_gain,
    emitted_projection,
):
    users, events = item_row.shape
    dim = item_table.shape[1]
    heads = dt_bias.shape[0]
    inner = emitted_projection.shape[0]
    conv_dim = conv_weight.shape[1]
    n_state = (conv_dim - inner) // 2
    times = lax.axis_size("tm")
    devices = times * lax.axis_size("table")
    cap = 2 * events // devices
    slots = users * cap
    everyone = ("tm", "table")

    requests, place = route(jnp.swapaxes(item_owner, 1, 2), item_row, devices, cap, 32)
    asked = exchange(requests, everyone)
    rows = fetch(asked, item_table, slots)
    got = exchange(rows.reshape(devices, slots, dim), everyone)
    got, gate_weight, conv_in_weight = lax.optimization_barrier(
        (got, in_weight[:, :inner], in_weight[:, inner:])
    )
    x, normed, conv, step, tail = project(
        got, place, norm_gain[None, :], conv_in_weight, conv_dim, heads
    )
    edge = lax.ppermute(tail, "tm", [(i, i + 1) for i in range(times - 1)])
    xbc, cum, steps, hold, decay, ends = chunk_states(
        history_len,
        conv,
        edge,
        step,
        event_gap,
        conv_weight,
        conv_bias,
        dt_bias[None, :],
        decay_rate[None, :],
        n_state,
    )
    by_head = exchange(ends, "tm")
    y0, fade0 = local_response(normed, gate_weight, xbc, cum, steps, 0)
    by_head, y0, fade0 = lax.optimization_barrier((by_head, y0, fade0))
    hin = exchange(scan_spans(by_head), "tm")
    y1, fade1 = local_response(normed, gate_weight, xbc, cum, steps, 1)
    return finish(
        history_len,
        (y0, y1),
        (fade0, fade1),
        xbc,
        x,
        hold,
        decay,
        hin,
        out_gain[None, :],
        emitted_projection,
    )


def solution(mesh):
    in_specs = (
        P("table", "tm", None),
        P("table", "tm"),
        P("table"),
        P("table", "tm"),
        P(("tm", "table"), None),
        P(),
        P(),
        P(),
        P(),
        P(),
        P(),
        P(),
        P(),
    )
    out_specs = P("table", "tm", None)
    return jax.shard_map(
        per_device, mesh=mesh, in_specs=in_specs, out_specs=out_specs, check_vma=False
    )
```

```python
import functools

import jax
import jax.numpy as jnp
from jax import lax
from jax.experimental import pallas as pl
from jax.experimental.pallas import tpu as pltpu
from jax.sharding import PartitionSpec as P

F32 = jnp.float32
BF16 = jnp.bfloat16
EPS = 1e-05
LANES = 128
CHUNK = 128
FINISH_ROWS = 384
LOCAL_CHUNKS = 2
STATE_CHUNKS = 2
PIECES = 4
MEBI = 1024 * 1024
ANYWHERE = pl.BlockSpec(memory_space=pl.ANY)


def params(axes, mebi=16):
    return pltpu.CompilerParams(
        dimension_semantics=("arbitrary",) * axes, vmem_limit_bytes=mebi * MEBI
    )


def full(shape):
    return pl.BlockSpec(shape, lambda *_: (0,) * len(shape))


def first_position(events):
    return lax.axis_index("tm") * events


ON_CHIP = pl.BlockSpec(memory_space=pltpu.VMEM)
SCALARS = pl.BlockSpec(memory_space=pltpu.SMEM)


def near(array):
    return pltpu.with_memory_space_constraint(array, pltpu.VMEM)


def far(array):
    return pltpu.with_memory_space_constraint(array, pltpu.HBM)


def iota(shape, axis):
    return lax.broadcasted_iota(jnp.int32, shape, axis)


def nt(a, b):
    return lax.dot_general(a, b, (((1,), (1,)), ((), ())), preferred_element_type=F32)


def mm(a, b):
    return jnp.dot(a, b, preferred_element_type=F32)


def silu(v):
    half = 0.5 * v
    return half + half * jnp.tanh(half)


def route_kernel(owner_ref, row_ref, req_ref, place_ref, *, devices, cap, width):
    users, events = row_ref.shape
    tri = jnp.where(
        (iota((LANES, 2 * LANES), 0) < iota((LANES, 2 * LANES), 1))
        | (iota((LANES, 2 * LANES), 1) >= LANES),
        1.0,
        0.0,
    ).astype(BF16)
    slots = users * cap
    req = jnp.zeros((devices, width), F32)
    for u in range(users):
        running = jnp.zeros((devices, LANES), F32)
        for c in range(events // LANES):
            own = owner_ref[u, :, c * LANES : (c + 1) * LANES]
            row = row_ref[u : u + 1, c * LANES : (c + 1) * LANES]
            hot = iota((devices, LANES), 0) == own
            hot_b = jnp.where(hot, 1.0, 0.0).astype(BF16)
            counts = mm(hot_b, tri)
            rank = counts[:, :LANES] + running
            running = running + counts[:, LANES:]
            slot = jnp.sum(jnp.where(hot, rank, 0.0), axis=0, keepdims=True).astype(jnp.int32)
            slot = slot + u * cap
            match = iota((width, LANES), 0) == slot
            high = jnp.where(match, (row >> 6).astype(F32), 0.0).astype(BF16)
            low = jnp.where(match, (row & 63).astype(F32), 0.0).astype(BF16)
            req = req + 64.0 * nt(hot_b, high) + nt(hot_b, low)
            place = (own * (slots * 2 // 3) + slot - u * (slots // 3)).astype(F32)
            place_ref[u, c * LANES : (c + 1) * LANES, :] = jnp.broadcast_to(
                place, (LANES, LANES)
            ).T.astype(jnp.int32)
    req_ref[:, 0, :] = req.astype(jnp.int32)


def route(owners, rows, devices, cap, width):
    users, events = rows.shape
    return pl.pallas_call(
        functools.partial(route_kernel, devices=devices, cap=cap, width=width),
        out_shape=(
            jax.ShapeDtypeStruct((devices, 1, width), jnp.int32),
            pltpu.HBM((users, events, LANES), jnp.int32),
        ),
        out_specs=(ON_CHIP, ON_CHIP),
        compiler_params=params(0),
        name="route",
    )(far(owners), far(rows))


def fetch_kernel(
    idx_ref, tab_ref, out_ref, idx, tab, wide, picked, packed, idx_sem, in_sems, out_sems
):
    owners, _, _ = idx.shape
    items, dim = tab.shape
    tiles = dim // LANES
    total = packed.shape[0]
    slots = total // owners
    part = items // PIECES
    piece = total // PIECES
    asked = pltpu.make_async_copy(idx_ref, idx, idx_sem)
    asked.start()
    loads = [
        pltpu.make_async_copy(
            tab_ref.at[pl.ds(k * part, part), :], tab.at[pl.ds(k * part, part), :], in_sems.at[k]
        )
        for k in range(PIECES)
    ]
    for load in loads:
        load.start()
    for k in range(PIECES):
        loads[k].wait()
        for cb in range(tiles):
            wide[pl.ds(k * part * tiles + cb, part, stride=tiles), :] = tab[
                k * part : (k + 1) * part, cb * LANES : (cb + 1) * LANES
            ].astype(F32)
    asked.wait()
    stores = []
    for k in range(PIECES):

        def pick(o, carry):
            base = pl.multiple_of(o * slots * tiles, 8)
            for s in range(slots):
                r = idx[k * (owners // PIECES) + o, 0, s]
                picked[pl.ds(base + tiles * s, tiles), :] = wide[
                    pl.ds(pl.multiple_of(r * tiles, tiles), tiles), :
                ]
            return carry

        lax.fori_loop(0, owners // PIECES, pick, 0)

        def pack(g, carry):
            for part in range(4):
                for cb in range(tiles):
                    start = (g * 4 + part) * 16 * tiles + cb
                    packed[
                        pl.ds(pl.multiple_of(k * piece + (g * 4 + part) * 16, 16), 16),
                        cb * LANES : (cb + 1) * LANES,
                    ] = picked[pl.ds(start, 16, stride=tiles), :].astype(BF16)
            return carry

        lax.fori_loop(0, piece // 64, pack, 0)
        store = pltpu.make_async_copy(
            packed.at[pl.ds(k * piece, piece), :],
            out_ref.at[pl.ds(k * piece, piece), :],
            out_sems.at[k],
        )
        store.start()
        stores.append(store)
    for store in stores:
        store.wait()


def fetch(idx, table, slots):
    owners = idx.shape[0]
    items, dim = table.shape
    tiles = dim // LANES
    total = owners * slots
    return pl.pallas_call(
        fetch_kernel,
        out_shape=pltpu.HBM((total, dim), BF16),
        in_specs=[ANYWHERE, ANYWHERE],
        out_specs=ANYWHERE,
        scratch_shapes=[
            pltpu.SMEM(idx.shape, jnp.int32),
            pltpu.VMEM((items, dim), BF16),
            pltpu.VMEM((items * tiles, LANES), F32),
            pltpu.VMEM((total // PIECES * tiles, LANES), F32),
            pltpu.VMEM((total, dim), BF16),
            pltpu.SemaphoreType.DMA,
            pltpu.SemaphoreType.DMA((PIECES,)),
            pltpu.SemaphoreType.DMA((PIECES,)),
        ],
        compiler_params=params(0, 24),
        name="fetch",
    )(idx, far(table))


def project_kernel(
    got_ref, place_ref, gain_ref, w_ref, x_ref, normed_ref, conv_ref, step_ref, tail_ref, hot
):
    u = pl.program_id(0)
    owners, slots, dim = got_ref.shape
    events, width = hot.shape
    conv_dim = conv_ref.shape[2]
    heads = step_ref.shape[1]
    window = slots * 2 // 3
    rows = LANES
    for i in range(events // rows):
        at = slice(i * rows, (i + 1) * rows)
        place = place_ref[0, at, :]
        for k in range(width // LANES):
            hot[at, k * LANES : (k + 1) * LANES] = jnp.where(
                place == iota((rows, LANES), 1) + k * LANES, 1.0, 0.0
            ).astype(BF16)
    shift = pl.multiple_of(u * (slots // 3), 8)
    got = got_ref[:, pl.ds(shift, window), :].reshape(owners * window, dim)
    x = mm(hot[...], got)
    x_ref[0] = x.astype(BF16)
    normed = x * lax.rsqrt(jnp.mean(x * x, axis=-1, keepdims=True) + EPS) * gain_ref[...]
    normed = normed.astype(BF16)
    normed_ref[0] = normed
    conv = mm(normed, w_ref[:, :conv_dim]).astype(BF16)
    conv_ref[u] = conv
    tail_ref[u] = conv[events - 8 :, :]
    raw = mm(normed, w_ref[:, conv_dim : conv_dim + heads])
    step_ref[u] = raw.astype(BF16).astype(F32).T


def project(got, place, gain, weight, conv_dim, heads):
    users, events, _ = place.shape
    owners, slots, dim = got.shape
    block = lambda width: pl.BlockSpec((1, events, width), lambda u: (u, 0, 0))
    return pl.pallas_call(
        project_kernel,
        out_shape=(
            pltpu.HBM((users, events, dim), BF16),
            pltpu.HBM((users, events, dim), BF16),
            pltpu.VMEM((users, events, conv_dim), BF16),
            pltpu.VMEM((users, heads, events), F32),
            jax.ShapeDtypeStruct((users, 8, conv_dim), BF16),
        ),
        grid=(users,),
        in_specs=[ON_CHIP, block(LANES), full(gain.shape), full(weight.shape)],
        out_specs=(block(dim), block(dim), ON_CHIP, ON_CHIP, full((users, 8, conv_dim))),
        scratch_shapes=[pltpu.VMEM((events, owners * (slots * 2 // 3)), BF16)],
        compiler_params=params(1, 24),
        name="project",
    )(near(got), far(place), gain, far(weight))


def lane_halves(rows_a, rows_b):
    return jnp.where(iota(rows_a.shape, rows_a.ndim - 1) < LANES // 2, rows_a, rows_b)


def running_sums(values):
    lane = iota(values.shape, 1)
    size = values.shape[1]
    ahead, back = values, values
    k = 1
    while k < size:
        ahead = ahead + jnp.where(lane >= k, pltpu.roll(ahead, k, 1), 0.0)
        back = back + jnp.where(lane < size - k, pltpu.roll(back, size - k, 1), 0.0)
        k *= 2
    return ahead, back


def pair_rhs(pair):
    low = iota(pair.shape, 1) < LANES // 2
    zero = jnp.zeros_like(pair)
    return jnp.concatenate([jnp.where(low, pair, zero), jnp.where(low, zero, pair)], axis=0)


def column(row):
    size = row.shape[1]
    return jnp.sum(
        jnp.where(iota((size, size), 0) == iota((size, size), 1), row, 0.0), axis=1, keepdims=True
    )


def states_kernel(
    len_ref,
    conv_ref,
    edge_ref,
    step_ref,
    gap_ref,
    cw_ref,
    cb_ref,
    dt_ref,
    rate_ref,
    xbc_ref,
    cum_ref,
    steps_ref,
    hold_ref,
    decay_ref,
    end_ref,
    prev,
    moves,
    weights,
    totals,
    state,
    pref,
):
    users, events, conv_dim = conv_ref.shape
    heads = step_ref.shape[1]
    chunks = events // CHUNK
    pairs = heads // 2
    inner = pairs * LANES
    n_state = state.shape[1]
    half = LANES // 2

    step_index = pl.program_id(0)

    @pl.when(step_index == 0)
    def _():
        dt = column(dt_ref[...])
        rate = column(rate_ref[...])
        start = first_position(events)
        steps_all, decay_all = [], []
        for u in range(users):
            for k in range(chunks):
                lanes = slice(k * CHUNK, (k + 1) * CHUNK)
                position = start + k * CHUNK + iota((heads, CHUNK), 1)
                alive = jnp.where(position < len_ref[u], 1.0, 0.0)
                raw = step_ref[u, :, lanes] + dt
                steps = alive * (jnp.maximum(raw, 0.0) + jnp.log1p(jnp.exp(-jnp.abs(raw))))
                steps_all.append(steps)
                decay_all.append(-rate * gap_ref[u : u + 1, lanes] * steps)
        steps = jnp.concatenate(steps_all, axis=0)
        ahead, back = running_sums(jnp.concatenate(decay_all, axis=0))
        after = jnp.where(iota(back.shape, 1) < CHUNK - 1, pltpu.roll(back, CHUNK - 1, 1), 0.0)
        cum_ref[...] = ahead
        steps_ref[...] = steps
        weights[...] = jnp.exp(after) * steps
        totals[...] = jnp.broadcast_to(back[:, 0:1], totals.shape)
        state[...] = jnp.zeros_like(state)
        pref[...] = jnp.zeros_like(pref)
        prev[:, 0:8, :] = jnp.zeros((users, 8, conv_dim), BF16)
        prev[:, 8:16, :] = edge_ref[...]
        for k in range(3):
            source = iota((CHUNK, CHUNK + 16), 0) - (3 - k)
            source = jnp.where(source < 0, source + CHUNK + 16, source)
            moves[k * CHUNK : (k + 1) * CHUNK, :] = jnp.where(
                source == iota((CHUNK, CHUNK + 16), 1), 1.0, 0.0
            ).astype(BF16)

    for part, u in [(p, v) for p in range(STATE_CHUNKS) for v in range(users)]:
        c = step_index * STATE_CHUNKS + part
        time = pl.ds(pl.multiple_of(c * CHUNK, CHUNK), CHUNK)
        rows = slice(part * CHUNK, (part + 1) * CHUNK)
        at = 0
        while at < conv_dim:
            width = min(2 * LANES, conv_dim - at)
            cols = slice(at, at + width)
            here = conv_ref[u, time, cols]
            both = jnp.concatenate([here, prev[u, :, cols]], axis=0)
            prev[u, :, cols] = here[CHUNK - 16 :, :]
            total = cb_ref[cols].reshape(1, width) + cw_ref[3:4, cols] * here.astype(F32)
            moved = mm(moves[...], both)
            for k in range(3):
                total = total + cw_ref[k : k + 1, cols] * moved[k * CHUNK : (k + 1) * CHUNK, :]
            xbc_ref[u, rows, cols] = silu(total).astype(BF16)
            at += width
        decay_ref[u, part] = jnp.exp(pref[u])
        hold_ref[u, part] = state[u].astype(BF16)
        coef_t = xbc_ref[u, rows, inner : inner + LANES].astype(F32).T[:n_state, :]
        first = pl.multiple_of((u * chunks + c) * heads, heads)
        weight = weights[pl.ds(first, heads), :]
        total = totals[pl.ds(first, heads), :]
        for j in range(pairs):
            lanes = slice(j * LANES, (j + 1) * LANES)
            a, b = 2 * j, 2 * j + 1
            left = jnp.concatenate(
                [coef_t * weight[a : a + 1, :], coef_t * weight[b : b + 1, :]], axis=0
            ).astype(BF16)
            both = mm(left, xbc_ref[u, rows, lanes])
            add = lane_halves(both[:n_state], both[n_state:])
            tot = lane_halves(total[a : a + 1, :], total[b : b + 1, :])
            state[u, :, lanes] = jnp.exp(tot) * state[u, :, lanes] + add
            pref[u, :, lanes] = pref[u, :, lanes] + tot

    @pl.when(step_index == pl.num_programs(0) - 1)
    def _():
        for h in range(heads):
            lanes = slice((h // 2) * LANES, (h // 2 + 1) * LANES)
            parts = []
            for u in range(users):
                value = state[u, :, lanes]
                low = jnp.broadcast_to(pref[u, :, lanes], (8, LANES))
                if h % 2 != u:
                    value = pltpu.roll(value, half, 1)
                    low = pltpu.roll(low, half, 1)
                high = low.astype(BF16).astype(F32)
                row = iota((8, LANES), 0)
                extra = jnp.where(row == 0, high, jnp.where(row == 1, low - high, 0.0))
                parts.append(jnp.concatenate([value, extra], axis=0))
            end_ref[h] = lane_halves(*parts).astype(BF16)


def chunk_states(lens, conv, edge, step, gap, cw, cb, dt, rate, n_state):
    users, events, conv_dim = conv.shape
    heads = step.shape[1]
    inner = conv_dim - 2 * n_state
    chunks = events // CHUNK
    lines = chunks * users * heads
    return pl.pallas_call(
        states_kernel,
        out_shape=(
            pltpu.HBM((users, events, conv_dim), BF16),
            pltpu.HBM((lines, CHUNK), F32),
            pltpu.HBM((lines, CHUNK), F32),
            pltpu.HBM((users, chunks, n_state, inner), BF16),
            pltpu.HBM((users, chunks, 1, inner), F32),
            pltpu.HBM((heads, n_state + 8, LANES), BF16),
        ),
        grid=(chunks // STATE_CHUNKS,),
        in_specs=[SCALARS, ON_CHIP, full(edge.shape), ON_CHIP]
        + [full(v.shape) for v in (gap, cw, cb, dt, rate)],
        out_specs=(
            pl.BlockSpec((users, STATE_CHUNKS * CHUNK, conv_dim), lambda c: (0, c, 0)),
            full((lines, CHUNK)),
            full((lines, CHUNK)),
            pl.BlockSpec((users, STATE_CHUNKS, n_state, inner), lambda c: (0, c, 0, 0)),
            pl.BlockSpec((users, STATE_CHUNKS, 1, inner), lambda c: (0, c, 0, 0)),
            full((heads, n_state + 8, LANES)),
        ),
        scratch_shapes=[
            pltpu.VMEM((users, 16, conv_dim), BF16),
            pltpu.VMEM((3 * CHUNK, CHUNK + 16), BF16),
            pltpu.VMEM((lines, CHUNK), F32),
            pltpu.VMEM((lines, LANES), F32),
            pltpu.VMEM((users, n_state, inner), F32),
            pltpu.VMEM((users, 1, inner), F32),
        ],
        compiler_params=params(1),
        name="chunk_states",
    )(lens, near(conv), edge, near(step), gap, cw, cb, dt, rate)


def scan_kernel(in_ref, out_ref):
    spans, rows, lanes = in_ref.shape
    n_state = rows - 8
    running = jnp.zeros((n_state, lanes), F32)
    for k in range(spans):
        out_ref[k] = running.astype(BF16)
        block = in_ref[k].astype(F32)
        log_decay = block[n_state : n_state + 1, :] + block[n_state + 1 : n_state + 2, :]
        running = jnp.exp(log_decay) * running + block[:n_state, :]


def scan_spans(ends):
    spans, rows, lanes = ends.shape
    return pl.pallas_call(
        scan_kernel,
        out_shape=jax.ShapeDtypeStruct((spans, rows - 8, lanes), BF16),
        in_specs=[ON_CHIP],
        out_specs=ON_CHIP,
        compiler_params=params(0),
        name="scan_spans",
    )(near(ends))


def local_kernel(normed_ref, w_ref, xbc_ref, cum_ref, steps_ref, y_ref, fade_ref, gates):
    rows, inner = y_ref.shape
    parts = rows // CHUNK
    heads = cum_ref.shape[0] // parts
    pairs = heads // 2
    half = LANES // 2
    gates[...] = silu(mm(normed_ref[0], w_ref[...]).astype(BF16).astype(F32))
    causal = iota((CHUNK, CHUNK), 0) >= iota((CHUNK, CHUNK), 1)
    for part in range(parts):
        here = slice(part * CHUNK, (part + 1) * CHUNK)
        coef = xbc_ref[0, here, inner : inner + LANES]
        scores = jnp.where(causal, nt(coef[:, half:], coef[:, :half]), 0.0)
        cum = cum_ref[part * heads : (part + 1) * heads, :]
        steps = steps_ref[part * heads : (part + 1) * heads, :]
        cum_t = jnp.concatenate([cum, jnp.zeros((LANES - heads, CHUNK), F32)], axis=0).T

        def mixing(h):
            own = jnp.broadcast_to(cum_t[:, h : h + 1], (CHUNK, CHUNK))
            fading = jnp.exp(jnp.minimum(own - cum[h : h + 1, :], 0.0))
            return own, (scores * fading * steps[h : h + 1, :]).astype(BF16)

        for j in range(pairs):
            lanes = slice(j * LANES, (j + 1) * LANES)
            own_a, mix_a = mixing(2 * j)
            own_b, mix_b = mixing(2 * j + 1)
            left = jnp.concatenate([mix_a, mix_b], axis=1)
            gate = gates[here, lanes]
            y_ref[here, lanes] = (gate * mm(left, pair_rhs(xbc_ref[0, here, lanes]))).astype(BF16)
            fade_ref[here, lanes] = (gate * jnp.exp(lane_halves(own_a, own_b))).astype(BF16)


def local_response(normed, weight, xbc, cum, steps, user):
    users, events, conv_dim = xbc.shape
    dim, inner = weight.shape
    heads = cum.shape[0] * CHUNK // (users * events)
    rows = LOCAL_CHUNKS * CHUNK
    blocks = events // rows
    block = lambda width: pl.BlockSpec((1, rows, width), lambda i: (user, i, 0))
    lines = pl.BlockSpec((LOCAL_CHUNKS * heads, CHUNK), lambda i: (user * blocks + i, 0))
    result = pl.BlockSpec((rows, inner), lambda i: (i, 0))
    return pl.pallas_call(
        local_kernel,
        out_shape=(pltpu.HBM((events, inner), BF16),) * 2,
        grid=(blocks,),
        in_specs=[block(dim), full(weight.shape), block(conv_dim), lines, lines],
        out_specs=(result, result),
        scratch_shapes=[pltpu.VMEM((rows, inner), F32)],
        compiler_params=params(1),
        name="local_response",
    )(*[far(v) for v in (normed, weight, xbc, cum, steps)])


def finish_kernel(
    len_ref,
    y0_ref,
    y1_ref,
    fade0_ref,
    fade1_ref,
    coef_ref,
    x_ref,
    hold_ref,
    decay_ref,
    hin_ref,
    gain_ref,
    w_ref,
    out_ref,
    incoming,
    same,
    normed,
    *,
    blocks,
):
    u = pl.program_id(0) // blocks
    b = pl.program_id(0) % blocks
    heads = hin_ref.shape[0]
    pairs = heads // 2
    half = LANES // 2
    size = 2 * LANES
    rows = out_ref.shape[1]

    @pl.when(pl.program_id(0) == 0)
    def _():
        same[...] = jnp.where(
            iota((size, size), 0) // half == iota((size, size), 1) // half, 1.0 / half, 0.0
        ).astype(BF16)
        for j in range(pairs):
            a = hin_ref[2 * j].astype(F32)
            b = hin_ref[2 * j + 1].astype(F32)
            lanes = slice(j * LANES, (j + 1) * LANES)
            incoming[0, :, lanes] = lane_halves(a, pltpu.roll(b, half, 1))
            incoming[1, :, lanes] = lane_halves(pltpu.roll(a, half, 1), b)

    def work(y_ref, fade_ref):
        for part in range(rows // CHUNK):
            here = slice(part * CHUNK, (part + 1) * CHUNK)
            held = hold_ref[0, part].astype(F32) + decay_ref[0, part] * incoming[u]
            held = held.astype(BF16)
            coef = coef_ref[0, here, half:]
            for j in range(pairs // 2):
                lanes = slice(j * size, (j + 1) * size)
                carried = mm(coef, held[:, lanes])
                gated = y_ref[here, lanes].astype(F32) + fade_ref[here, lanes].astype(F32) * carried
                mean = mm((gated * gated).astype(BF16), same[...])
                normed[here, lanes] = (
                    gated * lax.rsqrt(mean + EPS) * gain_ref[:, lanes]
                ).astype(BF16)
        mixed = mm(normed[...], w_ref[...])
        position = first_position(blocks * rows) + b * rows + iota((rows, 1), 0)
        alive = jnp.where(position < len_ref[u], 1.0, 0.0)
        out_ref[0] = (alive * (x_ref[0].astype(F32) + mixed)).astype(BF16)

    pl.when(u == 0)(functools.partial(work, y0_ref, fade0_ref))
    pl.when(u == 1)(functools.partial(work, y1_ref, fade1_ref))


def finish(lens, ys, fades, xbc, x, hold, decay, hin, gain, weight):
    events, inner = ys[0].shape
    n_state = hold.shape[2]
    users, _, dim = x.shape
    size = 2 * LANES
    rows = FINISH_ROWS
    blocks = events // rows
    parts = rows // CHUNK
    early = pl.BlockSpec((rows, inner), lambda i: (jnp.minimum(i, blocks - 1), 0))
    late = pl.BlockSpec((rows, inner), lambda i: (jnp.maximum(i - blocks, 0), 0))
    block = pl.BlockSpec((1, rows, dim), lambda i: (i // blocks, i % blocks, 0))
    per_chunk = lambda *shape: pl.BlockSpec(
        (1, parts) + shape, lambda i: (i // blocks, i % blocks, 0, 0)
    )
    return pl.pallas_call(
        functools.partial(finish_kernel, blocks=blocks),
        out_shape=jax.ShapeDtypeStruct((users, events, dim), BF16),
        grid=(users * blocks,),
        in_specs=[
            SCALARS,
            early,
            late,
            early,
            late,
            pl.BlockSpec((1, rows, LANES), lambda i: (i // blocks, i % blocks, inner // LANES)),
            block,
            per_chunk(n_state, inner),
            per_chunk(1, inner),
            full(hin.shape),
            full(gain.shape),
            full(weight.shape),
        ],
        out_specs=block,
        scratch_shapes=[
            pltpu.VMEM((users, n_state, inner), F32),
            pltpu.VMEM((size, size), BF16),
            pltpu.VMEM((rows, inner), BF16),
        ],
        compiler_params=params(1, 24),
        name="finish",
    )(lens, *[far(v) for v in (*ys, *fades, xbc, x, hold, decay)], hin, gain, weight)


def exchange(values, axes):
    return lax.all_to_all(values, axes, split_axis=0, concat_axis=0, tiled=True)


def per_device(
    item_owner,
    item_row,
    history_len,
    event_gap,
    item_table,
    norm_gain,
    in_weight,
    conv_weight,
    conv_bias,
    dt_bias,
    decay_rate,
    out_gain,
    emitted_projection,
):
    users, events = item_row.shape
    dim = item_table.shape[1]
    heads = dt_bias.shape[0]
    inner = emitted_projection.shape[0]
    conv_dim = conv_weight.shape[1]
    n_state = (conv_dim - inner) // 2
    times = lax.axis_size("tm")
    devices = times * lax.axis_size("table")
    cap = 2 * events // devices
    slots = users * cap
    everyone = ("tm", "table")

    requests, place = route(jnp.swapaxes(item_owner, 1, 2), item_row, devices, cap, 32)
    asked = exchange(requests, everyone)
    rows = fetch(asked, item_table, slots)
    got = exchange(rows.reshape(devices, slots, dim), everyone)
    got, gate_weight, conv_in_weight = lax.optimization_barrier(
        (got, in_weight[:, :inner], in_weight[:, inner:])
    )
    x, normed, conv, step, tail = project(
        got, place, norm_gain[None, :], conv_in_weight, conv_dim, heads
    )
    edge = lax.ppermute(tail, "tm", [(i, i + 1) for i in range(times - 1)])
    xbc, cum, steps, hold, decay, ends = chunk_states(
        history_len,
        conv,
        edge,
        step,
        event_gap,
        conv_weight,
        conv_bias,
        dt_bias[None, :],
        decay_rate[None, :],
        n_state,
    )
    by_head = exchange(ends, "tm")
    y0, fade0 = local_response(normed, gate_weight, xbc, cum, steps, 0)
    by_head, y0, fade0 = lax.optimization_barrier((by_head, y0, fade0))
    hin = exchange(scan_spans(by_head), "tm")
    y1, fade1 = local_response(normed, gate_weight, xbc, cum, steps, 1)
    return finish(
        history_len,
        (y0, y1),
        (fade0, fade1),
        xbc,
        x,
        hold,
        decay,
        hin,
        out_gain[None, :],
        emitted_projection,
    )


def solution(mesh):
    in_specs = (
        P("table", "tm", None),
        P("table", "tm"),
        P("table"),
        P("table", "tm"),
        P(("tm", "table"), None),
        P(),
        P(),
        P(),
        P(),
        P(),
        P(),
        P(),
        P(),
    )
    out_specs = P("table", "tm", None)
    return jax.shard_map(
        per_device, mesh=mesh, in_specs=in_specs, out_specs=out_specs, check_vma=False
    )
```

```python
import functools

import jax
import jax.numpy as jnp
from jax import lax
from jax.experimental import pallas as pl
from jax.experimental.pallas import tpu as pltpu
from jax.sharding import PartitionSpec as P

F32 = jnp.float32
BF16 = jnp.bfloat16
EPS = 1e-05
LANES = 128
CHUNK = 128
FINISH_ROWS = 384
LOCAL_CHUNKS = 2
STATE_CHUNKS = 2
PIECES = 4
MEBI = 1024 * 1024
ANYWHERE = pl.BlockSpec(memory_space=pl.ANY)


def params(axes, mebi=16):
    return pltpu.CompilerParams(
        dimension_semantics=("arbitrary",) * axes, vmem_limit_bytes=mebi * MEBI
    )


def full(shape):
    return pl.BlockSpec(shape, lambda *_: (0,) * len(shape))


def first_position(events):
    return lax.axis_index("tm") * events


ON_CHIP = pl.BlockSpec(memory_space=pltpu.VMEM)
SCALARS = pl.BlockSpec(memory_space=pltpu.SMEM)


def near(array):
    return pltpu.with_memory_space_constraint(array, pltpu.VMEM)


def far(array):
    return pltpu.with_memory_space_constraint(array, pltpu.HBM)


def iota(shape, axis):
    return lax.broadcasted_iota(jnp.int32, shape, axis)


def nt(a, b):
    return lax.dot_general(a, b, (((1,), (1,)), ((), ())), preferred_element_type=F32)


def mm(a, b):
    return jnp.dot(a, b, preferred_element_type=F32)


def silu(v):
    half = 0.5 * v
    return half + half * jnp.tanh(half)


def route_kernel(owner_ref, row_ref, req_ref, place_ref, *, devices, cap, width):
    users, events = row_ref.shape
    tri = jnp.where(
        (iota((LANES, 2 * LANES), 0) < iota((LANES, 2 * LANES), 1))
        | (iota((LANES, 2 * LANES), 1) >= LANES),
        1.0,
        0.0,
    ).astype(BF16)
    slots = users * cap
    req = jnp.zeros((devices, width), F32)
    for u in range(users):
        running = jnp.zeros((devices, LANES), F32)
        for c in range(events // LANES):
            own = owner_ref[u, :, c * LANES : (c + 1) * LANES]
            row = row_ref[u : u + 1, c * LANES : (c + 1) * LANES]
            hot = iota((devices, LANES), 0) == own
            hot_b = jnp.where(hot, 1.0, 0.0).astype(BF16)
            counts = mm(hot_b, tri)
            rank = counts[:, :LANES] + running
            running = running + counts[:, LANES:]
            slot = jnp.sum(jnp.where(hot, rank, 0.0), axis=0, keepdims=True).astype(jnp.int32)
            slot = slot + u * cap
            match = iota((width, LANES), 0) == slot
            high = jnp.where(match, (row >> 6).astype(F32), 0.0).astype(BF16)
            low = jnp.where(match, (row & 63).astype(F32), 0.0).astype(BF16)
            req = req + 64.0 * nt(hot_b, high) + nt(hot_b, low)
            place = (own * (slots * 2 // 3) + slot - u * (slots // 3)).astype(F32)
            place_ref[u, c * LANES : (c + 1) * LANES, :] = jnp.broadcast_to(
                place, (LANES, LANES)
            ).T.astype(jnp.int32)
    req_ref[:, 0, :] = req.astype(jnp.int32)


def route(owners, rows, devices, cap, width):
    users, events = rows.shape
    return pl.pallas_call(
        functools.partial(route_kernel, devices=devices, cap=cap, width=width),
        out_shape=(
            jax.ShapeDtypeStruct((devices, 1, width), jnp.int32),
            pltpu.HBM((users, events, LANES), jnp.int32),
        ),
        out_specs=(ON_CHIP, ON_CHIP),
        compiler_params=params(0),
        name="route",
    )(far(owners), far(rows))


def fetch_kernel(
    idx_ref, tab_ref, out_ref, idx, tab, wide, picked, packed, idx_sem, in_sems, out_sems
):
    owners, _, _ = idx.shape
    items, dim = tab.shape
    tiles = dim // LANES
    total = packed.shape[0]
    slots = total // owners
    part = items // PIECES
    piece = total // PIECES
    asked = pltpu.make_async_copy(idx_ref, idx, idx_sem)
    asked.start()
    loads = [
        pltpu.make_async_copy(
            tab_ref.at[pl.ds(k * part, part), :], tab.at[pl.ds(k * part, part), :], in_sems.at[k]
        )
        for k in range(PIECES)
    ]
    for load in loads:
        load.start()
    for k in range(PIECES):
        loads[k].wait()
        for cb in range(tiles):
            wide[pl.ds(k * part * tiles + cb, part, stride=tiles), :] = tab[
                k * part : (k + 1) * part, cb * LANES : (cb + 1) * LANES
            ].astype(F32)
    asked.wait()
    stores = []
    for k in range(PIECES):

        def pick(o, carry):
            base = pl.multiple_of(o * slots * tiles, 8)
            for s in range(slots):
                r = idx[k * (owners // PIECES) + o, 0, s]
                picked[pl.ds(base + tiles * s, tiles), :] = wide[
                    pl.ds(pl.multiple_of(r * tiles, tiles), tiles), :
                ]
            return carry

        lax.fori_loop(0, owners // PIECES, pick, 0)

        def pack(g, carry):
            for part in range(4):
                for cb in range(tiles):
                    start = (g * 4 + part) * 16 * tiles + cb
                    packed[
                        pl.ds(pl.multiple_of(k * piece + (g * 4 + part) * 16, 16), 16),
                        cb * LANES : (cb + 1) * LANES,
                    ] = picked[pl.ds(start, 16, stride=tiles), :].astype(BF16)
            return carry

        lax.fori_loop(0, piece // 64, pack, 0)
        store = pltpu.make_async_copy(
            packed.at[pl.ds(k * piece, piece), :],
            out_ref.at[pl.ds(k * piece, piece), :],
            out_sems.at[k],
        )
        store.start()
        stores.append(store)
    for store in stores:
        store.wait()


def fetch(idx, table, slots):
    owners = idx.shape[0]
    items, dim = table.shape
    tiles = dim // LANES
    total = owners * slots
    return pl.pallas_call(
        fetch_kernel,
        out_shape=pltpu.HBM((total, dim), BF16),
        in_specs=[ANYWHERE, ANYWHERE],
        out_specs=ANYWHERE,
        scratch_shapes=[
            pltpu.SMEM(idx.shape, jnp.int32),
            pltpu.VMEM((items, dim), BF16),
            pltpu.VMEM((items * tiles, LANES), F32),
            pltpu.VMEM((total // PIECES * tiles, LANES), F32),
            pltpu.VMEM((total, dim), BF16),
            pltpu.SemaphoreType.DMA,
            pltpu.SemaphoreType.DMA((PIECES,)),
            pltpu.SemaphoreType.DMA((PIECES,)),
        ],
        compiler_params=params(0, 24),
        name="fetch",
    )(idx, far(table))


def project_kernel(
    got_ref, place_ref, gain_ref, w_ref, x_ref, normed_ref, conv_ref, step_ref, tail_ref, hot
):
    u = pl.program_id(0)
    owners, slots, dim = got_ref.shape
    events, width = hot.shape
    conv_dim = conv_ref.shape[2]
    heads = step_ref.shape[1]
    window = slots * 2 // 3
    rows = LANES
    for i in range(events // rows):
        at = slice(i * rows, (i + 1) * rows)
        place = place_ref[0, at, :]
        for k in range(width // LANES):
            hot[at, k * LANES : (k + 1) * LANES] = jnp.where(
                place == iota((rows, LANES), 1) + k * LANES, 1.0, 0.0
            ).astype(BF16)
    shift = pl.multiple_of(u * (slots // 3), 8)
    got = got_ref[:, pl.ds(shift, window), :].reshape(owners * window, dim)
    x = mm(hot[...], got)
    x_ref[0] = x.astype(BF16)
    normed = x * lax.rsqrt(jnp.mean(x * x, axis=-1, keepdims=True) + EPS) * gain_ref[...]
    normed = normed.astype(BF16)
    normed_ref[0] = normed
    conv = mm(normed, w_ref[:, :conv_dim]).astype(BF16)
    conv_ref[u] = conv
    tail_ref[u] = conv[events - 8 :, :]
    raw = mm(normed, w_ref[:, conv_dim : conv_dim + heads])
    step_ref[u] = raw.astype(BF16).astype(F32).T


def project(got, place, gain, weight, conv_dim, heads):
    users, events, _ = place.shape
    owners, slots, dim = got.shape
    block = lambda width: pl.BlockSpec((1, events, width), lambda u: (u, 0, 0))
    return pl.pallas_call(
        project_kernel,
        out_shape=(
            pltpu.HBM((users, events, dim), BF16),
            pltpu.HBM((users, events, dim), BF16),
            pltpu.VMEM((users, events, conv_dim), BF16),
            pltpu.VMEM((users, heads, events), F32),
            jax.ShapeDtypeStruct((users, 8, conv_dim), BF16),
        ),
        grid=(users,),
        in_specs=[ON_CHIP, block(LANES), full(gain.shape), full(weight.shape)],
        out_specs=(block(dim), block(dim), ON_CHIP, ON_CHIP, full((users, 8, conv_dim))),
        scratch_shapes=[pltpu.VMEM((events, owners * (slots * 2 // 3)), BF16)],
        compiler_params=params(1, 24),
        name="project",
    )(near(got), far(place), gain, far(weight))


def lane_halves(rows_a, rows_b):
    return jnp.where(iota(rows_a.shape, rows_a.ndim - 1) < LANES // 2, rows_a, rows_b)


def running_sums(values):
    lane = iota(values.shape, 1)
    size = values.shape[1]
    ahead, back = values, values
    k = 1
    while k < size:
        ahead = ahead + jnp.where(lane >= k, pltpu.roll(ahead, k, 1), 0.0)
        back = back + jnp.where(lane < size - k, pltpu.roll(back, size - k, 1), 0.0)
        k *= 2
    return ahead, back


def pair_rhs(pair):
    low = iota(pair.shape, 1) < LANES // 2
    zero = jnp.zeros_like(pair)
    return jnp.concatenate([jnp.where(low, pair, zero), jnp.where(low, zero, pair)], axis=0)


def column(row):
    size = row.shape[1]
    return jnp.sum(
        jnp.where(iota((size, size), 0) == iota((size, size), 1), row, 0.0), axis=1, keepdims=True
    )


def states_kernel(
    len_ref,
    conv_ref,
    edge_ref,
    step_ref,
    gap_ref,
    cw_ref,
    cb_ref,
    dt_ref,
    rate_ref,
    xbc_ref,
    cum_ref,
    steps_ref,
    hold_ref,
    decay_ref,
    end_ref,
    prev,
    moves,
    weights,
    totals,
    state,
    pref,
):
    users, events, conv_dim = conv_ref.shape
    heads = step_ref.shape[1]
    chunks = events // CHUNK
    pairs = heads // 2
    inner = pairs * LANES
    n_state = state.shape[1]
    half = LANES // 2

    step_index = pl.program_id(0)

    @pl.when(step_index == 0)
    def _():
        dt = column(dt_ref[...])
        rate = column(rate_ref[...])
        start = first_position(events)
        steps_all, decay_all = [], []
        for u in range(users):
            for k in range(chunks):
                lanes = slice(k * CHUNK, (k + 1) * CHUNK)
                position = start + k * CHUNK + iota((heads, CHUNK), 1)
                alive = jnp.where(position < len_ref[u], 1.0, 0.0)
                raw = step_ref[u, :, lanes] + dt
                steps = alive * (jnp.maximum(raw, 0.0) + jnp.log1p(jnp.exp(-jnp.abs(raw))))
                steps_all.append(steps)
                decay_all.append(-rate * gap_ref[u : u + 1, lanes] * steps)
        steps = jnp.concatenate(steps_all, axis=0)
        ahead, back = running_sums(jnp.concatenate(decay_all, axis=0))
        after = jnp.where(iota(back.shape, 1) < CHUNK - 1, pltpu.roll(back, CHUNK - 1, 1), 0.0)
        cum_ref[...] = ahead
        steps_ref[...] = steps
        weights[...] = jnp.exp(after) * steps
        totals[...] = jnp.broadcast_to(back[:, 0:1], totals.shape)
        state[...] = jnp.zeros_like(state)
        pref[...] = jnp.zeros_like(pref)
        prev[:, 0:8, :] = jnp.zeros((users, 8, conv_dim), BF16)
        prev[:, 8:16, :] = edge_ref[...]
        for k in range(3):
            source = iota((CHUNK, CHUNK + 16), 0) - (3 - k)
            source = jnp.where(source < 0, source + CHUNK + 16, source)
            moves[k * CHUNK : (k + 1) * CHUNK, :] = jnp.where(
                source == iota((CHUNK, CHUNK + 16), 1), 1.0, 0.0
            ).astype(BF16)

    for part, u in [(p, v) for p in range(STATE_CHUNKS) for v in range(users)]:
        c = step_index * STATE_CHUNKS + part
        time = pl.ds(pl.multiple_of(c * CHUNK, CHUNK), CHUNK)
        rows = slice(part * CHUNK, (part + 1) * CHUNK)
        at = 0
        while at < conv_dim:
            width = min(2 * LANES, conv_dim - at)
            cols = slice(at, at + width)
            here = conv_ref[u, time, cols]
            both = jnp.concatenate([here, prev[u, :, cols]], axis=0)
            prev[u, :, cols] = here[CHUNK - 16 :, :]
            total = cb_ref[cols].reshape(1, width) + cw_ref[3:4, cols] * here.astype(F32)
            moved = mm(moves[...], both)
            for k in range(3):
                total = total + cw_ref[k : k + 1, cols] * moved[k * CHUNK : (k + 1) * CHUNK, :]
            xbc_ref[u, rows, cols] = silu(total).astype(BF16)
            at += width
        decay_ref[u, part] = jnp.exp(pref[u])
        hold_ref[u, part] = state[u].astype(BF16)
        coef_t = xbc_ref[u, rows, inner : inner + LANES].astype(F32).T[:n_state, :]
        first = pl.multiple_of((u * chunks + c) * heads, heads)
        weight = weights[pl.ds(first, heads), :]
        total = totals[pl.ds(first, heads), :]
        for j in range(pairs):
            lanes = slice(j * LANES, (j + 1) * LANES)
            a, b = 2 * j, 2 * j + 1
            left = jnp.concatenate(
                [coef_t * weight[a : a + 1, :], coef_t * weight[b : b + 1, :]], axis=0
            ).astype(BF16)
            both = mm(left, xbc_ref[u, rows, lanes])
            add = lane_halves(both[:n_state], both[n_state:])
            tot = lane_halves(total[a : a + 1, :], total[b : b + 1, :])
            state[u, :, lanes] = jnp.exp(tot) * state[u, :, lanes] + add
            pref[u, :, lanes] = pref[u, :, lanes] + tot

    @pl.when(step_index == pl.num_programs(0) - 1)
    def _():
        for h in range(heads):
            lanes = slice((h // 2) * LANES, (h // 2 + 1) * LANES)
            parts = []
            for u in range(users):
                value = state[u, :, lanes]
                low = jnp.broadcast_to(pref[u, :, lanes], (8, LANES))
                if h % 2 != u:
                    value = pltpu.roll(value, half, 1)
                    low = pltpu.roll(low, half, 1)
                high = low.astype(BF16).astype(F32)
                row = iota((8, LANES), 0)
                extra = jnp.where(row == 0, high, jnp.where(row == 1, low - high, 0.0))
                parts.append(jnp.concatenate([value, extra], axis=0))
            end_ref[h] = lane_halves(*parts).astype(BF16)


def chunk_states(lens, conv, edge, step, gap, cw, cb, dt, rate, n_state):
    users, events, conv_dim = conv.shape
    heads = step.shape[1]
    inner = conv_dim - 2 * n_state
    chunks = events // CHUNK
    lines = chunks * users * heads
    return pl.pallas_call(
        states_kernel,
        out_shape=(
            pltpu.HBM((users, events, conv_dim), BF16),
            pltpu.HBM((lines, CHUNK), F32),
            pltpu.HBM((lines, CHUNK), F32),
            pltpu.HBM((users, chunks, n_state, inner), BF16),
            pltpu.HBM((users, chunks, 1, inner), F32),
            pltpu.HBM((heads, n_state + 8, LANES), BF16),
        ),
        grid=(chunks // STATE_CHUNKS,),
        in_specs=[SCALARS, ON_CHIP, full(edge.shape), ON_CHIP]
        + [full(v.shape) for v in (gap, cw, cb, dt, rate)],
        out_specs=(
            pl.BlockSpec((users, STATE_CHUNKS * CHUNK, conv_dim), lambda c: (0, c, 0)),
            full((lines, CHUNK)),
            full((lines, CHUNK)),
            pl.BlockSpec((users, STATE_CHUNKS, n_state, inner), lambda c: (0, c, 0, 0)),
            pl.BlockSpec((users, STATE_CHUNKS, 1, inner), lambda c: (0, c, 0, 0)),
            full((heads, n_state + 8, LANES)),
        ),
        scratch_shapes=[
            pltpu.VMEM((users, 16, conv_dim), BF16),
            pltpu.VMEM((3 * CHUNK, CHUNK + 16), BF16),
            pltpu.VMEM((lines, CHUNK), F32),
            pltpu.VMEM((lines, LANES), F32),
            pltpu.VMEM((users, n_state, inner), F32),
            pltpu.VMEM((users, 1, inner), F32),
        ],
        compiler_params=params(1),
        name="chunk_states",
    )(lens, near(conv), edge, near(step), gap, cw, cb, dt, rate)


def scan_kernel(in_ref, out_ref):
    spans, rows, lanes = in_ref.shape
    n_state = rows - 8
    running = jnp.zeros((n_state, lanes), F32)
    for k in range(spans):
        out_ref[k] = running.astype(BF16)
        block = in_ref[k].astype(F32)
        log_decay = block[n_state : n_state + 1, :] + block[n_state + 1 : n_state + 2, :]
        running = jnp.exp(log_decay) * running + block[:n_state, :]


def scan_spans(ends):
    spans, rows, lanes = ends.shape
    return pl.pallas_call(
        scan_kernel,
        out_shape=jax.ShapeDtypeStruct((spans, rows - 8, lanes), BF16),
        in_specs=[ON_CHIP],
        out_specs=ON_CHIP,
        compiler_params=params(0),
        name="scan_spans",
    )(near(ends))


def local_kernel(normed_ref, w_ref, xbc_ref, cum_ref, steps_ref, y_ref, fade_ref, gates):
    rows, inner = y_ref.shape
    parts = rows // CHUNK
    heads = cum_ref.shape[0] // parts
    pairs = heads // 2
    half = LANES // 2
    gates[...] = silu(mm(normed_ref[0], w_ref[...]).astype(BF16).astype(F32))
    causal = iota((CHUNK, CHUNK), 0) >= iota((CHUNK, CHUNK), 1)
    for part in range(parts):
        here = slice(part * CHUNK, (part + 1) * CHUNK)
        coef = xbc_ref[0, here, inner : inner + LANES]
        scores = jnp.where(causal, nt(coef[:, half:], coef[:, :half]), 0.0)
        cum = cum_ref[part * heads : (part + 1) * heads, :]
        steps = steps_ref[part * heads : (part + 1) * heads, :]
        cum_t = jnp.concatenate([cum, jnp.zeros((LANES - heads, CHUNK), F32)], axis=0).T

        def mixing(h):
            own = jnp.broadcast_to(cum_t[:, h : h + 1], (CHUNK, CHUNK))
            fading = jnp.exp(jnp.minimum(own - cum[h : h + 1, :], 0.0))
            return own, (scores * fading * steps[h : h + 1, :]).astype(BF16)

        for j in range(pairs):
            lanes = slice(j * LANES, (j + 1) * LANES)
            own_a, mix_a = mixing(2 * j)
            own_b, mix_b = mixing(2 * j + 1)
            left = jnp.concatenate([mix_a, mix_b], axis=1)
            gate = gates[here, lanes]
            y_ref[here, lanes] = (gate * mm(left, pair_rhs(xbc_ref[0, here, lanes]))).astype(BF16)
            fade_ref[here, lanes] = (gate * jnp.exp(lane_halves(own_a, own_b))).astype(BF16)


def local_response(normed, weight, xbc, cum, steps, user):
    users, events, conv_dim = xbc.shape
    dim, inner = weight.shape
    heads = cum.shape[0] * CHUNK // (users * events)
    rows = LOCAL_CHUNKS * CHUNK
    blocks = events // rows
    block = lambda width: pl.BlockSpec((1, rows, width), lambda i: (user, i, 0))
    lines = pl.BlockSpec((LOCAL_CHUNKS * heads, CHUNK), lambda i: (user * blocks + i, 0))
    result = pl.BlockSpec((rows, inner), lambda i: (i, 0))
    return pl.pallas_call(
        local_kernel,
        out_shape=(pltpu.HBM((events, inner), BF16),) * 2,
        grid=(blocks,),
        in_specs=[block(dim), ON_CHIP, block(conv_dim), lines, lines],
        out_specs=(result, result),
        scratch_shapes=[pltpu.VMEM((rows, inner), F32)],
        compiler_params=params(1),
        name="local_response",
    )(far(normed), near(weight), far(xbc), far(cum), far(steps))


def finish_kernel(
    len_ref,
    y0_ref,
    y1_ref,
    fade0_ref,
    fade1_ref,
    coef_ref,
    x_ref,
    hold_ref,
    decay_ref,
    hin_ref,
    gain_ref,
    w_ref,
    out_ref,
    incoming,
    same,
    normed,
    *,
    blocks,
):
    u = pl.program_id(0) // blocks
    b = pl.program_id(0) % blocks
    heads = hin_ref.shape[0]
    pairs = heads // 2
    half = LANES // 2
    size = 2 * LANES
    rows = out_ref.shape[1]

    @pl.when(pl.program_id(0) == 0)
    def _():
        same[...] = jnp.where(
            iota((size, size), 0) // half == iota((size, size), 1) // half, 1.0 / half, 0.0
        ).astype(BF16)
        for j in range(pairs):
            a = hin_ref[2 * j].astype(F32)
            b = hin_ref[2 * j + 1].astype(F32)
            lanes = slice(j * LANES, (j + 1) * LANES)
            incoming[0, :, lanes] = lane_halves(a, pltpu.roll(b, half, 1))
            incoming[1, :, lanes] = lane_halves(pltpu.roll(a, half, 1), b)

    def work(y_ref, fade_ref):
        for part in range(rows // CHUNK):
            here = slice(part * CHUNK, (part + 1) * CHUNK)
            held = hold_ref[0, part].astype(F32) + decay_ref[0, part] * incoming[u]
            held = held.astype(BF16)
            coef = coef_ref[0, here, half:]
            for j in range(pairs // 2):
                lanes = slice(j * size, (j + 1) * size)
                carried = mm(coef, held[:, lanes])
                gated = y_ref[here, lanes].astype(F32) + fade_ref[here, lanes].astype(F32) * carried
                mean = mm((gated * gated).astype(BF16), same[...])
                normed[here, lanes] = (
                    gated * lax.rsqrt(mean + EPS) * gain_ref[:, lanes]
                ).astype(BF16)
        mixed = mm(normed[...], w_ref[...])
        position = first_position(blocks * rows) + b * rows + iota((rows, 1), 0)
        alive = jnp.where(position < len_ref[u], 1.0, 0.0)
        out_ref[0] = (alive * (x_ref[0].astype(F32) + mixed)).astype(BF16)

    pl.when(u == 0)(functools.partial(work, y0_ref, fade0_ref))
    pl.when(u == 1)(functools.partial(work, y1_ref, fade1_ref))


def finish(lens, ys, fades, xbc, x, hold, decay, hin, gain, weight):
    events, inner = ys[0].shape
    n_state = hold.shape[2]
    users, _, dim = x.shape
    size = 2 * LANES
    rows = FINISH_ROWS
    blocks = events // rows
    parts = rows // CHUNK
    early = pl.BlockSpec((rows, inner), lambda i: (jnp.minimum(i, blocks - 1), 0))
    late = pl.BlockSpec((rows, inner), lambda i: (jnp.maximum(i - blocks, 0), 0))
    block = pl.BlockSpec((1, rows, dim), lambda i: (i // blocks, i % blocks, 0))
    per_chunk = lambda *shape: pl.BlockSpec(
        (1, parts) + shape, lambda i: (i // blocks, i % blocks, 0, 0)
    )
    return pl.pallas_call(
        functools.partial(finish_kernel, blocks=blocks),
        out_shape=jax.ShapeDtypeStruct((users, events, dim), BF16),
        grid=(users * blocks,),
        in_specs=[
            SCALARS,
            early,
            late,
            early,
            late,
            pl.BlockSpec((1, rows, LANES), lambda i: (i // blocks, i % blocks, inner // LANES)),
            block,
            per_chunk(n_state, inner),
            per_chunk(1, inner),
            full(hin.shape),
            full(gain.shape),
            full(weight.shape),
        ],
        out_specs=block,
        scratch_shapes=[
            pltpu.VMEM((users, n_state, inner), F32),
            pltpu.VMEM((size, size), BF16),
            pltpu.VMEM((rows, inner), BF16),
        ],
        compiler_params=params(1, 24),
        name="finish",
    )(lens, *[far(v) for v in (*ys, *fades, xbc, x, hold, decay)], hin, gain, weight)


def exchange(values, axes):
    return lax.all_to_all(values, axes, split_axis=0, concat_axis=0, tiled=True)


def per_device(
    item_owner,
    item_row,
    history_len,
    event_gap,
    item_table,
    norm_gain,
    in_weight,
    conv_weight,
    conv_bias,
    dt_bias,
    decay_rate,
    out_gain,
    emitted_projection,
):
    users, events = item_row.shape
    dim = item_table.shape[1]
    heads = dt_bias.shape[0]
    inner = emitted_projection.shape[0]
    conv_dim = conv_weight.shape[1]
    n_state = (conv_dim - inner) // 2
    times = lax.axis_size("tm")
    devices = times * lax.axis_size("table")
    cap = 2 * events // devices
    slots = users * cap
    everyone = ("tm", "table")

    requests, place = route(jnp.swapaxes(item_owner, 1, 2), item_row, devices, cap, 32)
    asked = exchange(requests, everyone)
    rows = fetch(asked, item_table, slots)
    got = exchange(rows.reshape(devices, slots, dim), everyone)
    got, gate_weight, conv_in_weight = lax.optimization_barrier(
        (got, in_weight[:, :inner], in_weight[:, inner:])
    )
    x, normed, conv, step, tail = project(
        got, place, norm_gain[None, :], conv_in_weight, conv_dim, heads
    )
    edge = lax.ppermute(tail, "tm", [(i, i + 1) for i in range(times - 1)])
    xbc, cum, steps, hold, decay, ends = chunk_states(
        history_len,
        conv,
        edge,
        step,
        event_gap,
        conv_weight,
        conv_bias,
        dt_bias[None, :],
        decay_rate[None, :],
        n_state,
    )
    by_head = exchange(ends, "tm")
    y0, fade0 = local_response(normed, gate_weight, xbc, cum, steps, 0)
    by_head, y0, fade0 = lax.optimization_barrier((by_head, y0, fade0))
    hin = exchange(scan_spans(by_head), "tm")
    y1, fade1 = local_response(normed, gate_weight, xbc, cum, steps, 1)
    return finish(
        history_len,
        (y0, y1),
        (fade0, fade1),
        xbc,
        x,
        hold,
        decay,
        hin,
        out_gain[None, :],
        emitted_projection,
    )


def solution(mesh):
    in_specs = (
        P("table", "tm", None),
        P("table", "tm"),
        P("table"),
        P("table", "tm"),
        P(("tm", "table"), None),
        P(),
        P(),
        P(),
        P(),
        P(),
        P(),
        P(),
        P(),
    )
    out_specs = P("table", "tm", None)
    return jax.shard_map(
        per_device, mesh=mesh, in_specs=in_specs, out_specs=out_specs, check_vma=False
    )
```

```python
import functools

import jax
import jax.numpy as jnp
from jax import lax
from jax.experimental import pallas as pl
from jax.experimental.pallas import tpu as pltpu
from jax.sharding import PartitionSpec as P

F32 = jnp.float32
BF16 = jnp.bfloat16
EPS = 1e-05
LANES = 128
CHUNK = 128
FINISH_ROWS = 384
LOCAL_CHUNKS = 2
STATE_CHUNKS = 2
PIECES = 4
MEBI = 1024 * 1024
ANYWHERE = pl.BlockSpec(memory_space=pl.ANY)


def params(axes, mebi=16):
    return pltpu.CompilerParams(
        dimension_semantics=("arbitrary",) * axes, vmem_limit_bytes=mebi * MEBI
    )


def full(shape):
    return pl.BlockSpec(shape, lambda *_: (0,) * len(shape))


def first_position(events):
    return lax.axis_index("tm") * events


ON_CHIP = pl.BlockSpec(memory_space=pltpu.VMEM)
SCALARS = pl.BlockSpec(memory_space=pltpu.SMEM)


def near(array):
    return pltpu.with_memory_space_constraint(array, pltpu.VMEM)


def far(array):
    return pltpu.with_memory_space_constraint(array, pltpu.HBM)


def iota(shape, axis):
    return lax.broadcasted_iota(jnp.int32, shape, axis)


def nt(a, b):
    return lax.dot_general(a, b, (((1,), (1,)), ((), ())), preferred_element_type=F32)


def mm(a, b):
    return jnp.dot(a, b, preferred_element_type=F32)


def silu(v):
    half = 0.5 * v
    return half + half * jnp.tanh(half)


def route_kernel(owner_ref, row_ref, req_ref, place_ref, *, devices, cap, width):
    users, events = row_ref.shape
    tri = jnp.where(
        (iota((LANES, 2 * LANES), 0) < iota((LANES, 2 * LANES), 1))
        | (iota((LANES, 2 * LANES), 1) >= LANES),
        1.0,
        0.0,
    ).astype(BF16)
    slots = users * cap
    hots = [[] for _ in range(users)]
    digits = [[] for _ in range(users)]
    running = jnp.zeros((users * devices, LANES), F32)
    for c in range(events // LANES):
        lanes = slice(c * LANES, (c + 1) * LANES)
        owns = [owner_ref[u, :, lanes] for u in range(users)]
        marks = [iota((devices, LANES), 0) == own for own in owns]
        hot = jnp.concatenate([jnp.where(m, 1.0, 0.0) for m in marks], axis=0).astype(BF16)
        counts = mm(hot, tri)
        rank = counts[:, :LANES] + running
        running = running + counts[:, LANES:]
        for u in range(users):
            ours = slice(u * devices, (u + 1) * devices)
            row = row_ref[u : u + 1, lanes]
            slot = jnp.sum(jnp.where(marks[u], rank[ours], 0.0), axis=0, keepdims=True)
            slot = slot.astype(jnp.int32) + u * cap
            match = iota((width, LANES), 0) == slot
            high = jnp.where(match, (row >> 6).astype(F32), 0.0)
            low = jnp.where(match, (row & 63).astype(F32), 0.0)
            hots[u].append(hot[ours])
            digits[u].append(jnp.concatenate([high, low], axis=0).astype(BF16))
            place = (owns[u] * (slots * 2 // 3) + slot - u * (slots // 3)).astype(F32)
            place_ref[u, lanes, :] = jnp.broadcast_to(place, (LANES, LANES)).T.astype(jnp.int32)
    both = jnp.zeros((devices, 2 * width), F32)
    for u in range(users):
        both = both + nt(jnp.concatenate(hots[u], axis=1), jnp.concatenate(digits[u], axis=1))
    req = 64.0 * both[:, :width] + both[:, width:]
    req_ref[:, 0, :] = req.astype(jnp.int32)


def route(owners, rows, devices, cap, width):
    users, events = rows.shape
    return pl.pallas_call(
        functools.partial(route_kernel, devices=devices, cap=cap, width=width),
        out_shape=(
            jax.ShapeDtypeStruct((devices, 1, width), jnp.int32),
            pltpu.HBM((users, events, LANES), jnp.int32),
        ),
        out_specs=(ON_CHIP, ON_CHIP),
        compiler_params=params(0),
        name="route",
    )(far(owners), far(rows))


def fetch_kernel(
    idx_ref, tab_ref, out_ref, idx, tab, wide, picked, packed, idx_sem, in_sems, out_sems
):
    owners, _, _ = idx.shape
    items, dim = tab.shape
    tiles = dim // LANES
    total = packed.shape[0]
    slots = total // owners
    part = items // PIECES
    piece = total // PIECES
    asked = pltpu.make_async_copy(idx_ref, idx, idx_sem)
    asked.start()
    loads = [
        pltpu.make_async_copy(
            tab_ref.at[pl.ds(k * part, part), :], tab.at[pl.ds(k * part, part), :], in_sems.at[k]
        )
        for k in range(PIECES)
    ]
    for load in loads:
        load.start()
    for k in range(PIECES):
        loads[k].wait()
        for cb in range(tiles):
            wide[pl.ds(k * part * tiles + cb, part, stride=tiles), :] = tab[
                k * part : (k + 1) * part, cb * LANES : (cb + 1) * LANES
            ].astype(F32)
    asked.wait()
    stores = []
    for k in range(PIECES):

        def pick(o, carry):
            base = pl.multiple_of(o * slots * tiles, 8)
            for s in range(slots):
                r = idx[k * (owners // PIECES) + o, 0, s]
                picked[pl.ds(base + tiles * s, tiles), :] = wide[
                    pl.ds(pl.multiple_of(r * tiles, tiles), tiles), :
                ]
            return carry

        lax.fori_loop(0, owners // PIECES, pick, 0)

        def pack(g, carry):
            for part in range(4):
                for cb in range(tiles):
                    start = (g * 4 + part) * 16 * tiles + cb
                    packed[
                        pl.ds(pl.multiple_of(k * piece + (g * 4 + part) * 16, 16), 16),
                        cb * LANES : (cb + 1) * LANES,
                    ] = picked[pl.ds(start, 16, stride=tiles), :].astype(BF16)
            return carry

        lax.fori_loop(0, piece // 64, pack, 0)
        store = pltpu.make_async_copy(
            packed.at[pl.ds(k * piece, piece), :],
            out_ref.at[pl.ds(k * piece, piece), :],
            out_sems.at[k],
        )
        store.start()
        stores.append(store)
    for store in stores:
        store.wait()


def fetch(idx, table, slots):
    owners = idx.shape[0]
    items, dim = table.shape
    tiles = dim // LANES
    total = owners * slots
    return pl.pallas_call(
        fetch_kernel,
        out_shape=pltpu.HBM((total, dim), BF16),
        in_specs=[ANYWHERE, ANYWHERE],
        out_specs=ANYWHERE,
        scratch_shapes=[
            pltpu.SMEM(idx.shape, jnp.int32),
            pltpu.VMEM((items, dim), BF16),
            pltpu.VMEM((items * tiles, LANES), F32),
            pltpu.VMEM((total // PIECES * tiles, LANES), F32),
            pltpu.VMEM((total, dim), BF16),
            pltpu.SemaphoreType.DMA,
            pltpu.SemaphoreType.DMA((PIECES,)),
            pltpu.SemaphoreType.DMA((PIECES,)),
        ],
        compiler_params=params(0, 24),
        name="fetch",
    )(idx, far(table))


def project_kernel(
    got_ref, place_ref, gain_ref, w_ref, x_ref, normed_ref, conv_ref, step_ref, tail_ref, hot
):
    u = pl.program_id(0)
    owners, slots, dim = got_ref.shape
    events, width = hot.shape
    conv_dim = conv_ref.shape[2]
    heads = step_ref.shape[1]
    window = slots * 2 // 3
    rows = LANES
    for i in range(events // rows):
        at = slice(i * rows, (i + 1) * rows)
        place = place_ref[0, at, :]
        for k in range(width // LANES):
            hot[at, k * LANES : (k + 1) * LANES] = jnp.where(
                place == iota((rows, LANES), 1) + k * LANES, 1.0, 0.0
            ).astype(BF16)
    shift = pl.multiple_of(u * (slots // 3), 8)
    got = got_ref[:, pl.ds(shift, window), :].reshape(owners * window, dim)
    x = mm(hot[...], got)
    x_ref[0] = x.astype(BF16)
    normed = x * lax.rsqrt(jnp.mean(x * x, axis=-1, keepdims=True) + EPS) * gain_ref[...]
    normed = normed.astype(BF16)
    normed_ref[0] = normed
    conv = mm(normed, w_ref[:, :conv_dim]).astype(BF16)
    conv_ref[u] = conv
    tail_ref[u] = conv[events - 8 :, :]
    raw = mm(normed, w_ref[:, conv_dim : conv_dim + heads])
    step_ref[u] = raw.astype(BF16).astype(F32).T


def project(got, place, gain, weight, conv_dim, heads):
    users, events, _ = place.shape
    owners, slots, dim = got.shape
    block = lambda width: pl.BlockSpec((1, events, width), lambda u: (u, 0, 0))
    return pl.pallas_call(
        project_kernel,
        out_shape=(
            pltpu.HBM((users, events, dim), BF16),
            pltpu.HBM((users, events, dim), BF16),
            pltpu.VMEM((users, events, conv_dim), BF16),
            pltpu.VMEM((users, heads, events), F32),
            jax.ShapeDtypeStruct((users, 8, conv_dim), BF16),
        ),
        grid=(users,),
        in_specs=[ON_CHIP, block(LANES), full(gain.shape), full(weight.shape)],
        out_specs=(block(dim), block(dim), ON_CHIP, ON_CHIP, full((users, 8, conv_dim))),
        scratch_shapes=[pltpu.VMEM((events, owners * (slots * 2 // 3)), BF16)],
        compiler_params=params(1, 24),
        name="project",
    )(near(got), far(place), gain, far(weight))


def lane_halves(rows_a, rows_b):
    return jnp.where(iota(rows_a.shape, rows_a.ndim - 1) < LANES // 2, rows_a, rows_b)


def running_sums(values):
    lane = iota(values.shape, 1)
    size = values.shape[1]
    ahead, back = values, values
    k = 1
    while k < size:
        ahead = ahead + jnp.where(lane >= k, pltpu.roll(ahead, k, 1), 0.0)
        back = back + jnp.where(lane < size - k, pltpu.roll(back, size - k, 1), 0.0)
        k *= 2
    return ahead, back


def pair_rhs(pair):
    low = iota(pair.shape, 1) < LANES // 2
    zero = jnp.zeros_like(pair)
    return jnp.concatenate([jnp.where(low, pair, zero), jnp.where(low, zero, pair)], axis=0)


def column(row):
    size = row.shape[1]
    return jnp.sum(
        jnp.where(iota((size, size), 0) == iota((size, size), 1), row, 0.0), axis=1, keepdims=True
    )


def states_kernel(
    len_ref,
    conv_ref,
    edge_ref,
    step_ref,
    gap_ref,
    cw_ref,
    cb_ref,
    dt_ref,
    rate_ref,
    xbc_ref,
    cum_ref,
    steps_ref,
    hold_ref,
    decay_ref,
    end_ref,
    prev,
    moves,
    weights,
    totals,
    state,
    pref,
):
    users, events, conv_dim = conv_ref.shape
    heads = step_ref.shape[1]
    chunks = events // CHUNK
    pairs = heads // 2
    inner = pairs * LANES
    n_state = state.shape[1]
    half = LANES // 2

    step_index = pl.program_id(0)

    @pl.when(step_index == 0)
    def _():
        dt = column(dt_ref[...])
        rate = column(rate_ref[...])
        start = first_position(events)
        steps_all, decay_all = [], []
        for u in range(users):
            for k in range(chunks):
                lanes = slice(k * CHUNK, (k + 1) * CHUNK)
                position = start + k * CHUNK + iota((heads, CHUNK), 1)
                alive = jnp.where(position < len_ref[u], 1.0, 0.0)
                raw = step_ref[u, :, lanes] + dt
                steps = alive * (jnp.maximum(raw, 0.0) + jnp.log1p(jnp.exp(-jnp.abs(raw))))
                steps_all.append(steps)
                decay_all.append(-rate * gap_ref[u : u + 1, lanes] * steps)
        steps = jnp.concatenate(steps_all, axis=0)
        ahead, back = running_sums(jnp.concatenate(decay_all, axis=0))
        after = jnp.where(iota(back.shape, 1) < CHUNK - 1, pltpu.roll(back, CHUNK - 1, 1), 0.0)
        cum_ref[...] = ahead
        steps_ref[...] = steps
        weights[...] = jnp.exp(after) * steps
        totals[...] = jnp.broadcast_to(back[:, 0:1], totals.shape)
        state[...] = jnp.zeros_like(state)
        pref[...] = jnp.zeros_like(pref)
        prev[:, 0:8, :] = jnp.zeros((users, 8, conv_dim), BF16)
        prev[:, 8:16, :] = edge_ref[...]
        for k in range(3):
            source = iota((CHUNK, CHUNK + 16), 0) - (3 - k)
            source = jnp.where(source < 0, source + CHUNK + 16, source)
            moves[k * CHUNK : (k + 1) * CHUNK, :] = jnp.where(
                source == iota((CHUNK, CHUNK + 16), 1), 1.0, 0.0
            ).astype(BF16)

    for part, u in [(p, v) for p in range(STATE_CHUNKS) for v in range(users)]:
        c = step_index * STATE_CHUNKS + part
        time = pl.ds(pl.multiple_of(c * CHUNK, CHUNK), CHUNK)
        rows = slice(part * CHUNK, (part + 1) * CHUNK)
        at = 0
        while at < conv_dim:
            width = min(2 * LANES, conv_dim - at)
            cols = slice(at, at + width)
            here = conv_ref[u, time, cols]
            both = jnp.concatenate([here, prev[u, :, cols]], axis=0)
            prev[u, :, cols] = here[CHUNK - 16 :, :]
            total = cb_ref[cols].reshape(1, width) + cw_ref[3:4, cols] * here.astype(F32)
            moved = mm(moves[...], both)
            for k in range(3):
                total = total + cw_ref[k : k + 1, cols] * moved[k * CHUNK : (k + 1) * CHUNK, :]
            xbc_ref[u, rows, cols] = silu(total).astype(BF16)
            at += width
        decay_ref[u, part] = jnp.exp(pref[u])
        hold_ref[u, part] = state[u].astype(BF16)
        coef_t = xbc_ref[u, rows, inner : inner + LANES].astype(F32).T[:n_state, :]
        first = pl.multiple_of((u * chunks + c) * heads, heads)
        weight = weights[pl.ds(first, heads), :]
        total = totals[pl.ds(first, heads), :]
        for j in range(pairs):
            lanes = slice(j * LANES, (j + 1) * LANES)
            a, b = 2 * j, 2 * j + 1
            left = jnp.concatenate(
                [coef_t * weight[a : a + 1, :], coef_t * weight[b : b + 1, :]], axis=0
            ).astype(BF16)
            both = mm(left, xbc_ref[u, rows, lanes])
            add = lane_halves(both[:n_state], both[n_state:])
            tot = lane_halves(total[a : a + 1, :], total[b : b + 1, :])
            state[u, :, lanes] = jnp.exp(tot) * state[u, :, lanes] + add
            pref[u, :, lanes] = pref[u, :, lanes] + tot

    @pl.when(step_index == pl.num_programs(0) - 1)
    def _():
        for h in range(heads):
            lanes = slice((h // 2) * LANES, (h // 2 + 1) * LANES)
            parts = []
            for u in range(users):
                value = state[u, :, lanes]
                low = jnp.broadcast_to(pref[u, :, lanes], (8, LANES))
                if h % 2 != u:
                    value = pltpu.roll(value, half, 1)
                    low = pltpu.roll(low, half, 1)
                high = low.astype(BF16).astype(F32)
                row = iota((8, LANES), 0)
                extra = jnp.where(row == 0, high, jnp.where(row == 1, low - high, 0.0))
                parts.append(jnp.concatenate([value, extra], axis=0))
            end_ref[h] = lane_halves(*parts).astype(BF16)


def chunk_states(lens, conv, edge, step, gap, cw, cb, dt, rate, n_state):
    users, events, conv_dim = conv.shape
    heads = step.shape[1]
    inner = conv_dim - 2 * n_state
    chunks = events // CHUNK
    lines = chunks * users * heads
    return pl.pallas_call(
        states_kernel,
        out_shape=(
            pltpu.HBM((users, events, conv_dim), BF16),
            pltpu.HBM((lines, CHUNK), F32),
            pltpu.HBM((lines, CHUNK), F32),
            pltpu.HBM((users, chunks, n_state, inner), BF16),
            pltpu.HBM((users, chunks, 1, inner), F32),
            pltpu.HBM((heads, n_state + 8, LANES), BF16),
        ),
        grid=(chunks // STATE_CHUNKS,),
        in_specs=[SCALARS, ON_CHIP, full(edge.shape), ON_CHIP]
        + [full(v.shape) for v in (gap, cw, cb, dt, rate)],
        out_specs=(
            pl.BlockSpec((users, STATE_CHUNKS * CHUNK, conv_dim), lambda c: (0, c, 0)),
            full((lines, CHUNK)),
            full((lines, CHUNK)),
            pl.BlockSpec((users, STATE_CHUNKS, n_state, inner), lambda c: (0, c, 0, 0)),
            pl.BlockSpec((users, STATE_CHUNKS, 1, inner), lambda c: (0, c, 0, 0)),
            full((heads, n_state + 8, LANES)),
        ),
        scratch_shapes=[
            pltpu.VMEM((users, 16, conv_dim), BF16),
            pltpu.VMEM((3 * CHUNK, CHUNK + 16), BF16),
            pltpu.VMEM((lines, CHUNK), F32),
            pltpu.VMEM((lines, LANES), F32),
            pltpu.VMEM((users, n_state, inner), F32),
            pltpu.VMEM((users, 1, inner), F32),
        ],
        compiler_params=params(1),
        name="chunk_states",
    )(lens, near(conv), edge, near(step), gap, cw, cb, dt, rate)


def scan_kernel(in_ref, out_ref):
    spans, rows, lanes = in_ref.shape
    n_state = rows - 8
    running = jnp.zeros((n_state, lanes), F32)
    for k in range(spans):
        out_ref[k] = running.astype(BF16)
        block = in_ref[k].astype(F32)
        log_decay = block[n_state : n_state + 1, :] + block[n_state + 1 : n_state + 2, :]
        running = jnp.exp(log_decay) * running + block[:n_state, :]


def scan_spans(ends):
    spans, rows, lanes = ends.shape
    return pl.pallas_call(
        scan_kernel,
        out_shape=jax.ShapeDtypeStruct((spans, rows - 8, lanes), BF16),
        in_specs=[ON_CHIP],
        out_specs=ON_CHIP,
        compiler_params=params(0),
        name="scan_spans",
    )(near(ends))


def local_kernel(normed_ref, w_ref, xbc_ref, cum_ref, steps_ref, y_ref, fade_ref, gates):
    rows, inner = y_ref.shape
    parts = rows // CHUNK
    heads = cum_ref.shape[0] // parts
    pairs = heads // 2
    half = LANES // 2
    gates[...] = silu(mm(normed_ref[0], w_ref[...]).astype(BF16).astype(F32))
    causal = iota((CHUNK, CHUNK), 0) >= iota((CHUNK, CHUNK), 1)
    for part in range(parts):
        here = slice(part * CHUNK, (part + 1) * CHUNK)
        coef = xbc_ref[0, here, inner : inner + LANES]
        scores = jnp.where(causal, nt(coef[:, half:], coef[:, :half]), 0.0)
        cum = cum_ref[part * heads : (part + 1) * heads, :]
        steps = steps_ref[part * heads : (part + 1) * heads, :]
        cum_t = jnp.concatenate([cum, jnp.zeros((LANES - heads, CHUNK), F32)], axis=0).T

        def mixing(h):
            own = jnp.broadcast_to(cum_t[:, h : h + 1], (CHUNK, CHUNK))
            fading = jnp.exp(jnp.minimum(own - cum[h : h + 1, :], 0.0))
            return own, (scores * fading * steps[h : h + 1, :]).astype(BF16)

        for j in range(pairs):
            lanes = slice(j * LANES, (j + 1) * LANES)
            own_a, mix_a = mixing(2 * j)
            own_b, mix_b = mixing(2 * j + 1)
            left = jnp.concatenate([mix_a, mix_b], axis=1)
            gate = gates[here, lanes]
            y_ref[here, lanes] = (gate * mm(left, pair_rhs(xbc_ref[0, here, lanes]))).astype(BF16)
            fade_ref[here, lanes] = (gate * jnp.exp(lane_halves(own_a, own_b))).astype(BF16)


def local_response(normed, weight, xbc, cum, steps, user):
    users, events, conv_dim = xbc.shape
    dim, inner = weight.shape
    heads = cum.shape[0] * CHUNK // (users * events)
    rows = LOCAL_CHUNKS * CHUNK
    blocks = events // rows
    block = lambda width: pl.BlockSpec((1, rows, width), lambda i: (user, i, 0))
    lines = pl.BlockSpec((LOCAL_CHUNKS * heads, CHUNK), lambda i: (user * blocks + i, 0))
    result = pl.BlockSpec((rows, inner), lambda i: (i, 0))
    return pl.pallas_call(
        local_kernel,
        out_shape=(pltpu.HBM((events, inner), BF16),) * 2,
        grid=(blocks,),
        in_specs=[block(dim), ON_CHIP, block(conv_dim), lines, lines],
        out_specs=(result, result),
        scratch_shapes=[pltpu.VMEM((rows, inner), F32)],
        compiler_params=params(1),
        name="local_response",
    )(far(normed), near(weight), far(xbc), far(cum), far(steps))


def finish_kernel(
    len_ref,
    y0_ref,
    y1_ref,
    fade0_ref,
    fade1_ref,
    coef_ref,
    x_ref,
    hold_ref,
    decay_ref,
    hin_ref,
    gain_ref,
    w_ref,
    out_ref,
    incoming,
    same,
    normed,
    *,
    blocks,
):
    u = pl.program_id(0) // blocks
    b = pl.program_id(0) % blocks
    heads = hin_ref.shape[0]
    pairs = heads // 2
    half = LANES // 2
    size = 2 * LANES
    rows = out_ref.shape[1]

    @pl.when(pl.program_id(0) == 0)
    def _():
        same[...] = jnp.where(
            iota((size, size), 0) // half == iota((size, size), 1) // half, 1.0 / half, 0.0
        ).astype(BF16)
        for j in range(pairs):
            a = hin_ref[2 * j].astype(F32)
            b = hin_ref[2 * j + 1].astype(F32)
            lanes = slice(j * LANES, (j + 1) * LANES)
            incoming[0, :, lanes] = lane_halves(a, pltpu.roll(b, half, 1))
            incoming[1, :, lanes] = lane_halves(pltpu.roll(a, half, 1), b)

    def work(y_ref, fade_ref):
        for part in range(rows // CHUNK):
            here = slice(part * CHUNK, (part + 1) * CHUNK)
            held = hold_ref[0, part].astype(F32) + decay_ref[0, part] * incoming[u]
            held = held.astype(BF16)
            coef = coef_ref[0, here, half:]
            for j in range(pairs // 2):
                lanes = slice(j * size, (j + 1) * size)
                carried = mm(coef, held[:, lanes])
                gated = y_ref[here, lanes].astype(F32) + fade_ref[here, lanes].astype(F32) * carried
                mean = mm((gated * gated).astype(BF16), same[...])
                normed[here, lanes] = (
                    gated * lax.rsqrt(mean + EPS) * gain_ref[:, lanes]
                ).astype(BF16)
        mixed = mm(normed[...], w_ref[...])
        position = first_position(blocks * rows) + b * rows + iota((rows, 1), 0)
        alive = jnp.where(position < len_ref[u], 1.0, 0.0)
        out_ref[0] = (alive * (x_ref[0].astype(F32) + mixed)).astype(BF16)

    pl.when(u == 0)(functools.partial(work, y0_ref, fade0_ref))
    pl.when(u == 1)(functools.partial(work, y1_ref, fade1_ref))


def finish(lens, ys, fades, xbc, x, hold, decay, hin, gain, weight):
    events, inner = ys[0].shape
    n_state = hold.shape[2]
    users, _, dim = x.shape
    size = 2 * LANES
    rows = FINISH_ROWS
    blocks = events // rows
    parts = rows // CHUNK
    early = pl.BlockSpec((rows, inner), lambda i: (jnp.minimum(i, blocks - 1), 0))
    late = pl.BlockSpec((rows, inner), lambda i: (jnp.maximum(i - blocks, 0), 0))
    block = pl.BlockSpec((1, rows, dim), lambda i: (i // blocks, i % blocks, 0))
    per_chunk = lambda *shape: pl.BlockSpec(
        (1, parts) + shape, lambda i: (i // blocks, i % blocks, 0, 0)
    )
    return pl.pallas_call(
        functools.partial(finish_kernel, blocks=blocks),
        out_shape=jax.ShapeDtypeStruct((users, events, dim), BF16),
        grid=(users * blocks,),
        in_specs=[
            SCALARS,
            early,
            late,
            early,
            late,
            pl.BlockSpec((1, rows, LANES), lambda i: (i // blocks, i % blocks, inner // LANES)),
            block,
            per_chunk(n_state, inner),
            per_chunk(1, inner),
            full(hin.shape),
            full(gain.shape),
            full(weight.shape),
        ],
        out_specs=block,
        scratch_shapes=[
            pltpu.VMEM((users, n_state, inner), F32),
            pltpu.VMEM((size, size), BF16),
            pltpu.VMEM((rows, inner), BF16),
        ],
        compiler_params=params(1, 24),
        name="finish",
    )(lens, *[far(v) for v in (*ys, *fades, xbc, x, hold, decay)], hin, gain, weight)


def exchange(values, axes):
    return lax.all_to_all(values, axes, split_axis=0, concat_axis=0, tiled=True)


def per_device(
    item_owner,
    item_row,
    history_len,
    event_gap,
    item_table,
    norm_gain,
    in_weight,
    conv_weight,
    conv_bias,
    dt_bias,
    decay_rate,
    out_gain,
    emitted_projection,
):
    users, events = item_row.shape
    dim = item_table.shape[1]
    heads = dt_bias.shape[0]
    inner = emitted_projection.shape[0]
    conv_dim = conv_weight.shape[1]
    n_state = (conv_dim - inner) // 2
    times = lax.axis_size("tm")
    devices = times * lax.axis_size("table")
    cap = 2 * events // devices
    slots = users * cap
    everyone = ("tm", "table")

    requests, place = route(jnp.swapaxes(item_owner, 1, 2), item_row, devices, cap, 32)
    asked = exchange(requests, everyone)
    rows = fetch(asked, item_table, slots)
    got = exchange(rows.reshape(devices, slots, dim), everyone)
    got, gate_weight, conv_in_weight = lax.optimization_barrier(
        (got, in_weight[:, :inner], in_weight[:, inner:])
    )
    x, normed, conv, step, tail = project(
        got, place, norm_gain[None, :], conv_in_weight, conv_dim, heads
    )
    edge = lax.ppermute(tail, "tm", [(i, i + 1) for i in range(times - 1)])
    xbc, cum, steps, hold, decay, ends = chunk_states(
        history_len,
        conv,
        edge,
        step,
        event_gap,
        conv_weight,
        conv_bias,
        dt_bias[None, :],
        decay_rate[None, :],
        n_state,
    )
    by_head = exchange(ends, "tm")
    y0, fade0 = local_response(normed, gate_weight, xbc, cum, steps, 0)
    by_head, y0, fade0 = lax.optimization_barrier((by_head, y0, fade0))
    hin = exchange(scan_spans(by_head), "tm")
    y1, fade1 = local_response(normed, gate_weight, xbc, cum, steps, 1)
    return finish(
        history_len,
        (y0, y1),
        (fade0, fade1),
        xbc,
        x,
        hold,
        decay,
        hin,
        out_gain[None, :],
        emitted_projection,
    )


def solution(mesh):
    in_specs = (
        P("table", "tm", None),
        P("table", "tm"),
        P("table"),
        P("table", "tm"),
        P(("tm", "table"), None),
        P(),
        P(),
        P(),
        P(),
        P(),
        P(),
        P(),
        P(),
    )
    out_specs = P("table", "tm", None)
    return jax.shard_map(
        per_device, mesh=mesh, in_specs=in_specs, out_specs=out_specs, check_vma=False
    )
```

```python
import functools

import jax
import jax.numpy as jnp
from jax import lax
from jax.experimental import pallas as pl
from jax.experimental.pallas import tpu as pltpu
from jax.sharding import PartitionSpec as P

F32 = jnp.float32
BF16 = jnp.bfloat16
EPS = 1e-05
LANES = 128
CHUNK = 128
FINISH_ROWS = 384
LOCAL_CHUNKS = 2
STATE_CHUNKS = 2
PIECES = 4
MEBI = 1024 * 1024
ANYWHERE = pl.BlockSpec(memory_space=pl.ANY)


def params(axes, mebi=16):
    return pltpu.CompilerParams(
        dimension_semantics=("arbitrary",) * axes, vmem_limit_bytes=mebi * MEBI
    )


def full(shape):
    return pl.BlockSpec(shape, lambda *_: (0,) * len(shape))


def first_position(events):
    return lax.axis_index("tm") * events


ON_CHIP = pl.BlockSpec(memory_space=pltpu.VMEM)
SCALARS = pl.BlockSpec(memory_space=pltpu.SMEM)


def near(array):
    return pltpu.with_memory_space_constraint(array, pltpu.VMEM)


def far(array):
    return pltpu.with_memory_space_constraint(array, pltpu.HBM)


def iota(shape, axis):
    return lax.broadcasted_iota(jnp.int32, shape, axis)


def nt(a, b):
    return lax.dot_general(a, b, (((1,), (1,)), ((), ())), preferred_element_type=F32)


def mm(a, b):
    return jnp.dot(a, b, preferred_element_type=F32)


def silu(v):
    half = 0.5 * v
    return half + half * jnp.tanh(half)


def route_kernel(owner_ref, row_ref, req_ref, place_ref, *, devices, cap, width):
    users, events = row_ref.shape
    tri = jnp.where(
        (iota((LANES, 2 * LANES), 0) < iota((LANES, 2 * LANES), 1))
        | (iota((LANES, 2 * LANES), 1) >= LANES),
        1.0,
        0.0,
    ).astype(BF16)
    slots = users * cap
    hots = [[] for _ in range(users)]
    digits = [[] for _ in range(users)]
    running = jnp.zeros((users * devices, LANES), F32)
    for c in range(events // LANES):
        lanes = slice(c * LANES, (c + 1) * LANES)
        owns = [owner_ref[u, :, lanes] for u in range(users)]
        marks = [iota((devices, LANES), 0) == own for own in owns]
        hot = jnp.concatenate([jnp.where(m, 1.0, 0.0) for m in marks], axis=0).astype(BF16)
        counts = mm(hot, tri)
        rank = counts[:, :LANES] + running
        running = running + counts[:, LANES:]
        for u in range(users):
            ours = slice(u * devices, (u + 1) * devices)
            row = row_ref[u : u + 1, lanes]
            slot = jnp.sum(jnp.where(marks[u], rank[ours], 0.0), axis=0, keepdims=True)
            slot = slot.astype(jnp.int32) + u * cap
            match = iota((width, LANES), 0) == slot
            high = jnp.where(match, (row >> 6).astype(F32), 0.0)
            low = jnp.where(match, (row & 63).astype(F32), 0.0)
            hots[u].append(hot[ours])
            digits[u].append(jnp.concatenate([high, low], axis=0).astype(BF16))
            place = (owns[u] * (slots * 2 // 3) + slot - u * (slots // 3)).astype(F32)
            place_ref[u, lanes, :] = jnp.broadcast_to(place, (LANES, LANES)).T.astype(jnp.int32)
    both = jnp.zeros((devices, 2 * width), F32)
    for u in range(users):
        both = both + nt(jnp.concatenate(hots[u], axis=1), jnp.concatenate(digits[u], axis=1))
    req = 64.0 * both[:, :width] + both[:, width:]
    req_ref[:, 0, :] = req.astype(jnp.int32)


def route(owners, rows, devices, cap, width):
    users, events = rows.shape
    return pl.pallas_call(
        functools.partial(route_kernel, devices=devices, cap=cap, width=width),
        out_shape=(
            jax.ShapeDtypeStruct((devices, 1, width), jnp.int32),
            pltpu.HBM((users, events, LANES), jnp.int32),
        ),
        out_specs=(ON_CHIP, ON_CHIP),
        compiler_params=params(0),
        name="route",
    )(far(owners), far(rows))


def fetch_kernel(
    idx_ref, tab_ref, out_ref, idx, tab, wide, picked, packed, idx_sem, in_sems, out_sems
):
    owners, _, _ = idx.shape
    items, dim = tab.shape
    tiles = dim // LANES
    total = packed.shape[0]
    slots = total // owners
    part = items // PIECES
    piece = total // PIECES
    asked = pltpu.make_async_copy(idx_ref, idx, idx_sem)
    asked.start()
    loads = [
        pltpu.make_async_copy(
            tab_ref.at[pl.ds(k * part, part), :], tab.at[pl.ds(k * part, part), :], in_sems.at[k]
        )
        for k in range(PIECES)
    ]
    for load in loads:
        load.start()
    for k in range(PIECES):
        loads[k].wait()
        for cb in range(tiles):
            wide[pl.ds(k * part * tiles + cb, part, stride=tiles), :] = tab[
                k * part : (k + 1) * part, cb * LANES : (cb + 1) * LANES
            ].astype(F32)
    asked.wait()
    stores = []
    for k in range(PIECES):

        def pick(o, carry):
            base = pl.multiple_of(o * slots * tiles, 8)
            for s in range(slots):
                r = idx[k * (owners // PIECES) + o, 0, s]
                picked[pl.ds(base + tiles * s, tiles), :] = wide[
                    pl.ds(pl.multiple_of(r * tiles, tiles), tiles), :
                ]
            return carry

        lax.fori_loop(0, owners // PIECES, pick, 0)

        def pack(g, carry):
            for part in range(4):
                for cb in range(tiles):
                    start = (g * 4 + part) * 16 * tiles + cb
                    packed[
                        pl.ds(pl.multiple_of(k * piece + (g * 4 + part) * 16, 16), 16),
                        cb * LANES : (cb + 1) * LANES,
                    ] = picked[pl.ds(start, 16, stride=tiles), :].astype(BF16)
            return carry

        lax.fori_loop(0, piece // 64, pack, 0)
        store = pltpu.make_async_copy(
            packed.at[pl.ds(k * piece, piece), :],
            out_ref.at[pl.ds(k * piece, piece), :],
            out_sems.at[k],
        )
        store.start()
        stores.append(store)
    for store in stores:
        store.wait()


def fetch(idx, table, slots):
    owners = idx.shape[0]
    items, dim = table.shape
    tiles = dim // LANES
    total = owners * slots
    return pl.pallas_call(
        fetch_kernel,
        out_shape=pltpu.HBM((total, dim), BF16),
        in_specs=[ANYWHERE, ANYWHERE],
        out_specs=ANYWHERE,
        scratch_shapes=[
            pltpu.SMEM(idx.shape, jnp.int32),
            pltpu.VMEM((items, dim), BF16),
            pltpu.VMEM((items * tiles, LANES), F32),
            pltpu.VMEM((total // PIECES * tiles, LANES), F32),
            pltpu.VMEM((total, dim), BF16),
            pltpu.SemaphoreType.DMA,
            pltpu.SemaphoreType.DMA((PIECES,)),
            pltpu.SemaphoreType.DMA((PIECES,)),
        ],
        compiler_params=params(0, 24),
        name="fetch",
    )(idx, far(table))


def project_kernel(
    got_ref, place_ref, gain_ref, w_ref, x_ref, normed_ref, conv_ref, step_ref, tail_ref, hot
):
    u = pl.program_id(0)
    owners, slots, dim = got_ref.shape
    events, width = hot.shape
    conv_dim = conv_ref.shape[2]
    heads = step_ref.shape[1]
    window = slots * 2 // 3
    rows = LANES
    for i in range(events // rows):
        at = slice(i * rows, (i + 1) * rows)
        place = place_ref[0, at, :]
        for k in range(width // LANES):
            hot[at, k * LANES : (k + 1) * LANES] = jnp.where(
                place == iota((rows, LANES), 1) + k * LANES, 1.0, 0.0
            ).astype(BF16)
    shift = pl.multiple_of(u * (slots // 3), 8)
    got = got_ref[:, pl.ds(shift, window), :].reshape(owners * window, dim)
    x = mm(hot[...], got)
    x_ref[0] = x.astype(BF16)
    normed = x * lax.rsqrt(jnp.mean(x * x, axis=-1, keepdims=True) + EPS) * gain_ref[...]
    normed = normed.astype(BF16)
    normed_ref[0] = normed
    conv = mm(normed, w_ref[:, :conv_dim]).astype(BF16)
    conv_ref[u] = conv
    tail_ref[u] = conv[events - 8 :, :]
    raw = mm(normed, w_ref[:, conv_dim : conv_dim + heads])
    step_ref[u] = raw.astype(BF16).astype(F32).T


def project(got, place, gain, weight, conv_dim, heads):
    users, events, _ = place.shape
    owners, slots, dim = got.shape
    block = lambda width: pl.BlockSpec((1, events, width), lambda u: (u, 0, 0))
    return pl.pallas_call(
        project_kernel,
        out_shape=(
            pltpu.HBM((users, events, dim), BF16),
            pltpu.HBM((users, events, dim), BF16),
            pltpu.VMEM((users, events, conv_dim), BF16),
            pltpu.VMEM((users, heads, events), F32),
            jax.ShapeDtypeStruct((users, 8, conv_dim), BF16),
        ),
        grid=(users,),
        in_specs=[ON_CHIP, block(LANES), full(gain.shape), full(weight.shape)],
        out_specs=(block(dim), block(dim), ON_CHIP, ON_CHIP, full((users, 8, conv_dim))),
        scratch_shapes=[pltpu.VMEM((events, owners * (slots * 2 // 3)), BF16)],
        compiler_params=params(1, 24),
        name="project",
    )(near(got), far(place), gain, far(weight))


def lane_halves(rows_a, rows_b):
    return jnp.where(iota(rows_a.shape, rows_a.ndim - 1) < LANES // 2, rows_a, rows_b)


def running_sums(values):
    lane = iota(values.shape, 1)
    size = values.shape[1]
    ahead, back = values, values
    k = 1
    while k < size:
        ahead = ahead + jnp.where(lane >= k, pltpu.roll(ahead, k, 1), 0.0)
        back = back + jnp.where(lane < size - k, pltpu.roll(back, size - k, 1), 0.0)
        k *= 2
    return ahead, back


def pair_rhs(pair):
    low = iota(pair.shape, 1) < LANES // 2
    zero = jnp.zeros_like(pair)
    return jnp.concatenate([jnp.where(low, pair, zero), jnp.where(low, zero, pair)], axis=0)


def column(row):
    size = row.shape[1]
    return jnp.sum(
        jnp.where(iota((size, size), 0) == iota((size, size), 1), row, 0.0), axis=1, keepdims=True
    )


def states_kernel(
    len_ref,
    conv_ref,
    edge_ref,
    step_ref,
    gap_ref,
    cw_ref,
    cb_ref,
    dt_ref,
    rate_ref,
    xbc_ref,
    cum_ref,
    steps_ref,
    hold_ref,
    decay_ref,
    end_ref,
    prev,
    moves,
    weights,
    totals,
    state,
    pref,
):
    users, events, conv_dim = conv_ref.shape
    heads = step_ref.shape[1]
    chunks = events // CHUNK
    pairs = heads // 2
    inner = pairs * LANES
    n_state = state.shape[1]
    half = LANES // 2

    step_index = pl.program_id(0)

    @pl.when(step_index == 0)
    def _():
        dt = column(dt_ref[...])
        rate = column(rate_ref[...])
        start = first_position(events)
        steps_all, decay_all = [], []
        for u in range(users):
            for k in range(chunks):
                lanes = slice(k * CHUNK, (k + 1) * CHUNK)
                position = start + k * CHUNK + iota((heads, CHUNK), 1)
                alive = jnp.where(position < len_ref[u], 1.0, 0.0)
                raw = step_ref[u, :, lanes] + dt
                steps = alive * (jnp.maximum(raw, 0.0) + jnp.log1p(jnp.exp(-jnp.abs(raw))))
                steps_all.append(steps)
                decay_all.append(-rate * gap_ref[u : u + 1, lanes] * steps)
        steps = jnp.concatenate(steps_all, axis=0)
        ahead, back = running_sums(jnp.concatenate(decay_all, axis=0))
        after = jnp.where(iota(back.shape, 1) < CHUNK - 1, pltpu.roll(back, CHUNK - 1, 1), 0.0)
        cum_ref[...] = ahead
        steps_ref[...] = steps
        weights[...] = jnp.exp(after) * steps
        totals[...] = jnp.broadcast_to(back[:, 0:1], totals.shape)
        state[...] = jnp.zeros_like(state)
        pref[...] = jnp.zeros_like(pref)
        prev[:, 0:8, :] = jnp.zeros((users, 8, conv_dim), BF16)
        prev[:, 8:16, :] = edge_ref[...]
        for k in range(3):
            source = iota((CHUNK, CHUNK + 16), 0) - (3 - k)
            source = jnp.where(source < 0, source + CHUNK + 16, source)
            moves[k * CHUNK : (k + 1) * CHUNK, :] = jnp.where(
                source == iota((CHUNK, CHUNK + 16), 1), 1.0, 0.0
            ).astype(BF16)

    for part, u in [(p, v) for p in range(STATE_CHUNKS) for v in range(users)]:
        c = step_index * STATE_CHUNKS + part
        time = pl.ds(pl.multiple_of(c * CHUNK, CHUNK), CHUNK)
        rows = slice(part * CHUNK, (part + 1) * CHUNK)
        at = 0
        while at < conv_dim:
            width = min(2 * LANES, conv_dim - at)
            cols = slice(at, at + width)
            here = conv_ref[u, time, cols]
            both = jnp.concatenate([here, prev[u, :, cols]], axis=0)
            prev[u, :, cols] = here[CHUNK - 16 :, :]
            total = cb_ref[cols].reshape(1, width) + cw_ref[3:4, cols] * here.astype(F32)
            moved = mm(moves[...], both)
            for k in range(3):
                total = total + cw_ref[k : k + 1, cols] * moved[k * CHUNK : (k + 1) * CHUNK, :]
            xbc_ref[u, rows, cols] = silu(total).astype(BF16)
            at += width
        decay_ref[u, part] = jnp.exp(pref[u])
        hold_ref[u, part] = state[u].astype(BF16)
        coef_t = xbc_ref[u, rows, inner : inner + LANES].astype(F32).T[:n_state, :]
        first = pl.multiple_of((u * chunks + c) * heads, heads)
        weight = weights[pl.ds(first, heads), :]
        total = totals[pl.ds(first, heads), :]
        for j in range(pairs):
            lanes = slice(j * LANES, (j + 1) * LANES)
            a, b = 2 * j, 2 * j + 1
            left = jnp.concatenate(
                [coef_t * weight[a : a + 1, :], coef_t * weight[b : b + 1, :]], axis=0
            ).astype(BF16)
            both = mm(left, xbc_ref[u, rows, lanes])
            add = lane_halves(both[:n_state], both[n_state:])
            tot = lane_halves(total[a : a + 1, :], total[b : b + 1, :])
            state[u, :, lanes] = jnp.exp(tot) * state[u, :, lanes] + add
            pref[u, :, lanes] = pref[u, :, lanes] + tot

    @pl.when(step_index == pl.num_programs(0) - 1)
    def _():
        for h in range(heads):
            lanes = slice((h // 2) * LANES, (h // 2 + 1) * LANES)
            parts = []
            for u in range(users):
                value = state[u, :, lanes]
                low = jnp.broadcast_to(pref[u, :, lanes], (8, LANES))
                if h % 2 != u:
                    value = pltpu.roll(value, half, 1)
                    low = pltpu.roll(low, half, 1)
                high = low.astype(BF16).astype(F32)
                row = iota((8, LANES), 0)
                extra = jnp.where(row == 0, high, jnp.where(row == 1, low - high, 0.0))
                parts.append(jnp.concatenate([value, extra], axis=0))
            end_ref[h] = lane_halves(*parts).astype(BF16)


def chunk_states(lens, conv, edge, step, gap, cw, cb, dt, rate, n_state):
    users, events, conv_dim = conv.shape
    heads = step.shape[1]
    inner = conv_dim - 2 * n_state
    chunks = events // CHUNK
    lines = chunks * users * heads
    return pl.pallas_call(
        states_kernel,
        out_shape=(
            pltpu.HBM((users, events, conv_dim), BF16),
            pltpu.HBM((lines, CHUNK), F32),
            pltpu.HBM((lines, CHUNK), F32),
            pltpu.HBM((users, chunks, n_state, inner), BF16),
            pltpu.HBM((users, chunks, 1, inner), F32),
            pltpu.HBM((heads, n_state + 8, LANES), BF16),
        ),
        grid=(chunks // STATE_CHUNKS,),
        in_specs=[SCALARS, ON_CHIP, full(edge.shape), ON_CHIP]
        + [full(v.shape) for v in (gap, cw, cb, dt, rate)],
        out_specs=(
            pl.BlockSpec((users, STATE_CHUNKS * CHUNK, conv_dim), lambda c: (0, c, 0)),
            full((lines, CHUNK)),
            full((lines, CHUNK)),
            pl.BlockSpec((users, STATE_CHUNKS, n_state, inner), lambda c: (0, c, 0, 0)),
            pl.BlockSpec((users, STATE_CHUNKS, 1, inner), lambda c: (0, c, 0, 0)),
            full((heads, n_state + 8, LANES)),
        ),
        scratch_shapes=[
            pltpu.VMEM((users, 16, conv_dim), BF16),
            pltpu.VMEM((3 * CHUNK, CHUNK + 16), BF16),
            pltpu.VMEM((lines, CHUNK), F32),
            pltpu.VMEM((lines, LANES), F32),
            pltpu.VMEM((users, n_state, inner), F32),
            pltpu.VMEM((users, 1, inner), F32),
        ],
        compiler_params=params(1),
        name="chunk_states",
    )(lens, near(conv), edge, near(step), gap, cw, cb, dt, rate)


def scan_kernel(in_ref, out_ref):
    spans, rows, lanes = in_ref.shape
    n_state = rows - 8
    running = jnp.zeros((n_state, lanes), F32)
    for k in range(spans):
        out_ref[k] = running.astype(BF16)
        block = in_ref[k].astype(F32)
        log_decay = block[n_state : n_state + 1, :] + block[n_state + 1 : n_state + 2, :]
        running = jnp.exp(log_decay) * running + block[:n_state, :]


def scan_spans(ends):
    spans, rows, lanes = ends.shape
    return pl.pallas_call(
        scan_kernel,
        out_shape=jax.ShapeDtypeStruct((spans, rows - 8, lanes), BF16),
        in_specs=[ON_CHIP],
        out_specs=ON_CHIP,
        compiler_params=params(0),
        name="scan_spans",
    )(near(ends))


def local_kernel(normed_ref, w_ref, xbc_ref, cum_ref, steps_ref, *rest):
    y_ref, fade_ref, gates = rest[-3:]
    _, rows, inner = y_ref.shape
    parts = rows // CHUNK
    heads = cum_ref.shape[0] // parts
    pairs = heads // 2
    half = LANES // 2
    gates[...] = silu(mm(normed_ref[0], w_ref[...]).astype(BF16).astype(F32))
    causal = iota((CHUNK, CHUNK), 0) >= iota((CHUNK, CHUNK), 1)
    for part in range(parts):
        here = slice(part * CHUNK, (part + 1) * CHUNK)
        coef = xbc_ref[0, here, inner : inner + LANES]
        scores = jnp.where(causal, nt(coef[:, half:], coef[:, :half]), 0.0)
        cum = cum_ref[part * heads : (part + 1) * heads, :]
        steps = steps_ref[part * heads : (part + 1) * heads, :]
        cum_t = jnp.concatenate([cum, jnp.zeros((LANES - heads, CHUNK), F32)], axis=0).T

        def mixing(h):
            own = jnp.broadcast_to(cum_t[:, h : h + 1], (CHUNK, CHUNK))
            fading = jnp.exp(jnp.minimum(own - cum[h : h + 1, :], 0.0))
            return own, (scores * fading * steps[h : h + 1, :]).astype(BF16)

        for j in range(pairs):
            lanes = slice(j * LANES, (j + 1) * LANES)
            own_a, mix_a = mixing(2 * j)
            own_b, mix_b = mixing(2 * j + 1)
            left = jnp.concatenate([mix_a, mix_b], axis=1)
            gate = gates[here, lanes]
            y_ref[0, here, lanes] = (gate * mm(left, pair_rhs(xbc_ref[0, here, lanes]))).astype(BF16)
            fade_ref[0, here, lanes] = (gate * jnp.exp(lane_halves(own_a, own_b))).astype(BF16)


def local_response(normed, weight, xbc, cum, steps, user, before=()):
    users, events, conv_dim = xbc.shape
    dim, inner = weight.shape
    heads = cum.shape[0] * CHUNK // (users * events)
    rows = LOCAL_CHUNKS * CHUNK
    blocks = events // rows
    block = lambda width: pl.BlockSpec((1, rows, width), lambda i: (user, i, 0))
    lines = pl.BlockSpec((LOCAL_CHUNKS * heads, CHUNK), lambda i: (user * blocks + i, 0))
    result = block(inner)
    return pl.pallas_call(
        local_kernel,
        out_shape=(pltpu.HBM((users, events, inner), BF16),) * 2,
        grid=(blocks,),
        in_specs=[block(dim), ON_CHIP, block(conv_dim), lines, lines] + [ANYWHERE] * len(before),
        out_specs=(result, result),
        scratch_shapes=[pltpu.VMEM((rows, inner), F32)],
        input_output_aliases={5 + k: k for k in range(len(before))},
        compiler_params=params(1),
        name="local_response",
    )(far(normed), near(weight), far(xbc), far(cum), far(steps), *[far(v) for v in before])


def finish_kernel(
    len_ref,
    y_ref,
    fade_ref,
    coef_ref,
    x_ref,
    hold_ref,
    decay_ref,
    hin_ref,
    gain_ref,
    w_ref,
    out_ref,
    incoming,
    same,
    normed,
    *,
    blocks,
):
    u = pl.program_id(0) // blocks
    b = pl.program_id(0) % blocks
    heads = hin_ref.shape[0]
    pairs = heads // 2
    half = LANES // 2
    size = 2 * LANES
    rows = out_ref.shape[1]

    @pl.when(pl.program_id(0) == 0)
    def _():
        same[...] = jnp.where(
            iota((size, size), 0) // half == iota((size, size), 1) // half, 1.0 / half, 0.0
        ).astype(BF16)
        for j in range(pairs):
            a = hin_ref[2 * j].astype(F32)
            b = hin_ref[2 * j + 1].astype(F32)
            lanes = slice(j * LANES, (j + 1) * LANES)
            incoming[0, :, lanes] = lane_halves(a, pltpu.roll(b, half, 1))
            incoming[1, :, lanes] = lane_halves(pltpu.roll(a, half, 1), b)

    for part in range(rows // CHUNK):
        here = slice(part * CHUNK, (part + 1) * CHUNK)
        held = hold_ref[0, part].astype(F32) + decay_ref[0, part] * incoming[u]
        held = held.astype(BF16)
        coef = coef_ref[0, here, half:]
        for j in range(pairs // 2):
            lanes = slice(j * size, (j + 1) * size)
            carried = mm(coef, held[:, lanes])
            gated = y_ref[0, here, lanes].astype(F32) + fade_ref[0, here, lanes].astype(F32) * carried
            mean = mm((gated * gated).astype(BF16), same[...])
            normed[here, lanes] = (
                gated * lax.rsqrt(mean + EPS) * gain_ref[:, lanes]
            ).astype(BF16)
    mixed = mm(normed[...], w_ref[...])
    position = first_position(blocks * rows) + b * rows + iota((rows, 1), 0)
    alive = jnp.where(position < len_ref[u], 1.0, 0.0)
    out_ref[0] = (alive * (x_ref[0].astype(F32) + mixed)).astype(BF16)


def finish(lens, y, fade, xbc, x, hold, decay, hin, gain, weight):
    _, events, inner = y.shape
    n_state = hold.shape[2]
    users, _, dim = x.shape
    size = 2 * LANES
    rows = FINISH_ROWS
    blocks = events // rows
    parts = rows // CHUNK
    wide = pl.BlockSpec((1, rows, inner), lambda i: (i // blocks, i % blocks, 0))
    block = pl.BlockSpec((1, rows, dim), lambda i: (i // blocks, i % blocks, 0))
    per_chunk = lambda *shape: pl.BlockSpec(
        (1, parts) + shape, lambda i: (i // blocks, i % blocks, 0, 0)
    )
    return pl.pallas_call(
        functools.partial(finish_kernel, blocks=blocks),
        out_shape=jax.ShapeDtypeStruct((users, events, dim), BF16),
        grid=(users * blocks,),
        in_specs=[
            SCALARS,
            wide,
            wide,
            pl.BlockSpec((1, rows, LANES), lambda i: (i // blocks, i % blocks, inner // LANES)),
            block,
            per_chunk(n_state, inner),
            per_chunk(1, inner),
            full(hin.shape),
            full(gain.shape),
            full(weight.shape),
        ],
        out_specs=block,
        scratch_shapes=[
            pltpu.VMEM((users, n_state, inner), F32),
            pltpu.VMEM((size, size), BF16),
            pltpu.VMEM((rows, inner), BF16),
        ],
        compiler_params=params(1, 24),
        name="finish",
    )(lens, *[far(v) for v in (y, fade, xbc, x, hold, decay)], hin, gain, weight)


def exchange(values, axes):
    return lax.all_to_all(values, axes, split_axis=0, concat_axis=0, tiled=True)


def per_device(
    item_owner,
    item_row,
    history_len,
    event_gap,
    item_table,
    norm_gain,
    in_weight,
    conv_weight,
    conv_bias,
    dt_bias,
    decay_rate,
    out_gain,
    emitted_projection,
):
    users, events = item_row.shape
    dim = item_table.shape[1]
    heads = dt_bias.shape[0]
    inner = emitted_projection.shape[0]
    conv_dim = conv_weight.shape[1]
    n_state = (conv_dim - inner) // 2
    times = lax.axis_size("tm")
    devices = times * lax.axis_size("table")
    cap = 2 * events // devices
    slots = users * cap
    everyone = ("tm", "table")

    requests, place = route(jnp.swapaxes(item_owner, 1, 2), item_row, devices, cap, 32)
    asked = exchange(requests, everyone)
    rows = fetch(asked, item_table, slots)
    got = exchange(rows.reshape(devices, slots, dim), everyone)
    got, gate_weight, conv_in_weight = lax.optimization_barrier(
        (got, in_weight[:, :inner], in_weight[:, inner:])
    )
    x, normed, conv, step, tail = project(
        got, place, norm_gain[None, :], conv_in_weight, conv_dim, heads
    )
    edge = lax.ppermute(tail, "tm", [(i, i + 1) for i in range(times - 1)])
    xbc, cum, steps, hold, decay, ends = chunk_states(
        history_len,
        conv,
        edge,
        step,
        event_gap,
        conv_weight,
        conv_bias,
        dt_bias[None, :],
        decay_rate[None, :],
        n_state,
    )
    by_head = exchange(ends, "tm")
    y, fade = local_response(normed, gate_weight, xbc, cum, steps, 0)
    by_head, y, fade = lax.optimization_barrier((by_head, y, fade))
    hin = exchange(scan_spans(by_head), "tm")
    y, fade = local_response(normed, gate_weight, xbc, cum, steps, 1, (y, fade))
    return finish(
        history_len,
        y,
        fade,
        xbc,
        x,
        hold,
        decay,
        hin,
        out_gain[None, :],
        emitted_projection,
    )


def solution(mesh):
    in_specs = (
        P("table", "tm", None),
        P("table", "tm"),
        P("table"),
        P("table", "tm"),
        P(("tm", "table"), None),
        P(),
        P(),
        P(),
        P(),
        P(),
        P(),
        P(),
        P(),
    )
    out_specs = P("table", "tm", None)
    return jax.shard_map(
        per_device, mesh=mesh, in_specs=in_specs, out_specs=out_specs, check_vma=False
    )
```

```python
import functools

import jax
import jax.numpy as jnp
from jax import lax
from jax.experimental import pallas as pl
from jax.experimental.pallas import tpu as pltpu
from jax.sharding import PartitionSpec as P

F32 = jnp.float32
BF16 = jnp.bfloat16
EPS = 1e-05
LANES = 128
CHUNK = 128
FINISH_ROWS = 384
LOCAL_CHUNKS = 2
STATE_CHUNKS = 2
PIECES = 8
MEBI = 1024 * 1024
ANYWHERE = pl.BlockSpec(memory_space=pl.ANY)


def params(axes, mebi=16):
    return pltpu.CompilerParams(
        dimension_semantics=("arbitrary",) * axes, vmem_limit_bytes=mebi * MEBI
    )


def full(shape):
    return pl.BlockSpec(shape, lambda *_: (0,) * len(shape))


def first_position(events):
    return lax.axis_index("tm") * events


ON_CHIP = pl.BlockSpec(memory_space=pltpu.VMEM)
SCALARS = pl.BlockSpec(memory_space=pltpu.SMEM)


def near(array):
    return pltpu.with_memory_space_constraint(array, pltpu.VMEM)


def far(array):
    return pltpu.with_memory_space_constraint(array, pltpu.HBM)


def iota(shape, axis):
    return lax.broadcasted_iota(jnp.int32, shape, axis)


def nt(a, b):
    return lax.dot_general(a, b, (((1,), (1,)), ((), ())), preferred_element_type=F32)


def mm(a, b):
    return jnp.dot(a, b, preferred_element_type=F32)


def silu(v):
    half = 0.5 * v
    return half + half * jnp.tanh(half)


def route_kernel(owner_ref, row_ref, req_ref, place_ref, *, devices, cap, width):
    users, events = row_ref.shape
    tri = jnp.where(
        (iota((LANES, 2 * LANES), 0) < iota((LANES, 2 * LANES), 1))
        | (iota((LANES, 2 * LANES), 1) >= LANES),
        1.0,
        0.0,
    ).astype(BF16)
    slots = users * cap
    hots = [[] for _ in range(users)]
    digits = [[] for _ in range(users)]
    running = jnp.zeros((users * devices, LANES), F32)
    for c in range(events // LANES):
        lanes = slice(c * LANES, (c + 1) * LANES)
        owns = [owner_ref[u, :, lanes] for u in range(users)]
        marks = [iota((devices, LANES), 0) == own for own in owns]
        hot = jnp.concatenate([jnp.where(m, 1.0, 0.0) for m in marks], axis=0).astype(BF16)
        counts = mm(hot, tri)
        rank = counts[:, :LANES] + running
        running = running + counts[:, LANES:]
        for u in range(users):
            ours = slice(u * devices, (u + 1) * devices)
            row = row_ref[u : u + 1, lanes]
            slot = jnp.sum(jnp.where(marks[u], rank[ours], 0.0), axis=0, keepdims=True)
            slot = slot.astype(jnp.int32) + u * cap
            match = iota((width, LANES), 0) == slot
            high = jnp.where(match, (row >> 6).astype(F32), 0.0)
            low = jnp.where(match, (row & 63).astype(F32), 0.0)
            hots[u].append(hot[ours])
            digits[u].append(jnp.concatenate([high, low], axis=0).astype(BF16))
            place = (owns[u] * (slots * 2 // 3) + slot - u * (slots // 3)).astype(F32)
            place_ref[u, lanes, :] = jnp.broadcast_to(place, (LANES, LANES)).T.astype(jnp.int32)
    both = jnp.zeros((devices, 2 * width), F32)
    for u in range(users):
        both = both + nt(jnp.concatenate(hots[u], axis=1), jnp.concatenate(digits[u], axis=1))
    req = 64.0 * both[:, :width] + both[:, width:]
    req_ref[:, 0, :] = req.astype(jnp.int32)


def route(owners, rows, devices, cap, width):
    users, events = rows.shape
    return pl.pallas_call(
        functools.partial(route_kernel, devices=devices, cap=cap, width=width),
        out_shape=(
            jax.ShapeDtypeStruct((devices, 1, width), jnp.int32),
            pltpu.HBM((users, events, LANES), jnp.int32),
        ),
        out_specs=(ON_CHIP, ON_CHIP),
        compiler_params=params(0),
        name="route",
    )(far(owners), far(rows))


def fetch_kernel(
    idx_ref, tab_ref, out_ref, idx, tab, wide, picked, packed, idx_sem, in_sems, out_sems
):
    owners, _, _ = idx.shape
    items, dim = tab.shape
    tiles = dim // LANES
    total = packed.shape[0]
    slots = total // owners
    part = items // PIECES
    piece = total // PIECES
    asked = pltpu.make_async_copy(idx_ref, idx, idx_sem)
    asked.start()
    loads = [
        pltpu.make_async_copy(
            tab_ref.at[pl.ds(k * part, part), :], tab.at[pl.ds(k * part, part), :], in_sems.at[k]
        )
        for k in range(PIECES)
    ]
    for load in loads:
        load.start()
    for k in range(PIECES):
        loads[k].wait()
        for cb in range(tiles):
            wide[pl.ds(k * part * tiles + cb, part, stride=tiles), :] = tab[
                k * part : (k + 1) * part, cb * LANES : (cb + 1) * LANES
            ].astype(F32)
    asked.wait()
    stores = []
    for k in range(PIECES):

        def pick(o, carry):
            base = pl.multiple_of(o * slots * tiles, 8)
            for s in range(slots):
                r = idx[k * (owners // PIECES) + o, 0, s]
                picked[pl.ds(base + tiles * s, tiles), :] = wide[
                    pl.ds(pl.multiple_of(r * tiles, tiles), tiles), :
                ]
            return carry

        lax.fori_loop(0, owners // PIECES, pick, 0)

        def pack(g, carry):
            for part in range(4):
                for cb in range(tiles):
                    start = (g * 4 + part) * 16 * tiles + cb
                    packed[
                        pl.ds(pl.multiple_of(k * piece + (g * 4 + part) * 16, 16), 16),
                        cb * LANES : (cb + 1) * LANES,
                    ] = picked[pl.ds(start, 16, stride=tiles), :].astype(BF16)
            return carry

        lax.fori_loop(0, piece // 64, pack, 0)
        store = pltpu.make_async_copy(
            packed.at[pl.ds(k * piece, piece), :],
            out_ref.at[pl.ds(k * piece, piece), :],
            out_sems.at[k],
        )
        store.start()
        stores.append(store)
    for store in stores:
        store.wait()


def fetch(idx, table, slots):
    owners = idx.shape[0]
    items, dim = table.shape
    tiles = dim // LANES
    total = owners * slots
    return pl.pallas_call(
        fetch_kernel,
        out_shape=pltpu.HBM((total, dim), BF16),
        in_specs=[ANYWHERE, ANYWHERE],
        out_specs=ANYWHERE,
        scratch_shapes=[
            pltpu.SMEM(idx.shape, jnp.int32),
            pltpu.VMEM((items, dim), BF16),
            pltpu.VMEM((items * tiles, LANES), F32),
            pltpu.VMEM((total // PIECES * tiles, LANES), F32),
            pltpu.VMEM((total, dim), BF16),
            pltpu.SemaphoreType.DMA,
            pltpu.SemaphoreType.DMA((PIECES,)),
            pltpu.SemaphoreType.DMA((PIECES,)),
        ],
        compiler_params=params(0, 24),
        name="fetch",
    )(idx, far(table))


def project_kernel(
    got_ref, place_ref, gain_ref, w_ref, x_ref, normed_ref, conv_ref, step_ref, tail_ref, hot
):
    u = pl.program_id(0)
    owners, slots, dim = got_ref.shape
    events, width = hot.shape
    conv_dim = conv_ref.shape[2]
    heads = step_ref.shape[1]
    window = slots * 2 // 3
    rows = LANES
    for i in range(events // rows):
        at = slice(i * rows, (i + 1) * rows)
        place = place_ref[0, at, :]
        for k in range(width // LANES):
            hot[at, k * LANES : (k + 1) * LANES] = jnp.where(
                place == iota((rows, LANES), 1) + k * LANES, 1.0, 0.0
            ).astype(BF16)
    shift = pl.multiple_of(u * (slots // 3), 8)
    got = got_ref[:, pl.ds(shift, window), :].reshape(owners * window, dim)
    x = mm(hot[...], got)
    x_ref[0] = x.astype(BF16)
    normed = x * lax.rsqrt(jnp.mean(x * x, axis=-1, keepdims=True) + EPS) * gain_ref[...]
    normed = normed.astype(BF16)
    normed_ref[0] = normed
    conv = mm(normed, w_ref[:, :conv_dim]).astype(BF16)
    conv_ref[u] = conv
    tail_ref[u] = conv[events - 8 :, :]
    raw = mm(normed, w_ref[:, conv_dim : conv_dim + heads])
    step_ref[u] = raw.astype(BF16).astype(F32).T


def project(got, place, gain, weight, conv_dim, heads):
    users, events, _ = place.shape
    owners, slots, dim = got.shape
    block = lambda width: pl.BlockSpec((1, events, width), lambda u: (u, 0, 0))
    return pl.pallas_call(
        project_kernel,
        out_shape=(
            pltpu.HBM((users, events, dim), BF16),
            pltpu.HBM((users, events, dim), BF16),
            pltpu.VMEM((users, events, conv_dim), BF16),
            pltpu.VMEM((users, heads, events), F32),
            jax.ShapeDtypeStruct((users, 8, conv_dim), BF16),
        ),
        grid=(users,),
        in_specs=[ON_CHIP, block(LANES), full(gain.shape), full(weight.shape)],
        out_specs=(block(dim), block(dim), ON_CHIP, ON_CHIP, full((users, 8, conv_dim))),
        scratch_shapes=[pltpu.VMEM((events, owners * (slots * 2 // 3)), BF16)],
        compiler_params=params(1, 24),
        name="project",
    )(near(got), far(place), gain, far(weight))


def lane_halves(rows_a, rows_b):
    return jnp.where(iota(rows_a.shape, rows_a.ndim - 1) < LANES // 2, rows_a, rows_b)


def running_sums(values):
    lane = iota(values.shape, 1)
    size = values.shape[1]
    ahead, back = values, values
    k = 1
    while k < size:
        ahead = ahead + jnp.where(lane >= k, pltpu.roll(ahead, k, 1), 0.0)
        back = back + jnp.where(lane < size - k, pltpu.roll(back, size - k, 1), 0.0)
        k *= 2
    return ahead, back


def pair_rhs(pair):
    low = iota(pair.shape, 1) < LANES // 2
    zero = jnp.zeros_like(pair)
    return jnp.concatenate([jnp.where(low, pair, zero), jnp.where(low, zero, pair)], axis=0)


def column(row):
    size = row.shape[1]
    return jnp.sum(
        jnp.where(iota((size, size), 0) == iota((size, size), 1), row, 0.0), axis=1, keepdims=True
    )


def states_kernel(
    len_ref,
    conv_ref,
    edge_ref,
    step_ref,
    gap_ref,
    cw_ref,
    cb_ref,
    dt_ref,
    rate_ref,
    xbc_ref,
    cum_ref,
    steps_ref,
    hold_ref,
    decay_ref,
    end_ref,
    prev,
    moves,
    weights,
    totals,
    state,
    pref,
):
    users, events, conv_dim = conv_ref.shape
    heads = step_ref.shape[1]
    chunks = events // CHUNK
    pairs = heads // 2
    inner = pairs * LANES
    n_state = state.shape[1]
    half = LANES // 2

    step_index = pl.program_id(0)

    @pl.when(step_index == 0)
    def _():
        dt = column(dt_ref[...])
        rate = column(rate_ref[...])
        start = first_position(events)
        steps_all, decay_all = [], []
        for u in range(users):
            for k in range(chunks):
                lanes = slice(k * CHUNK, (k + 1) * CHUNK)
                position = start + k * CHUNK + iota((heads, CHUNK), 1)
                alive = jnp.where(position < len_ref[u], 1.0, 0.0)
                raw = step_ref[u, :, lanes] + dt
                steps = alive * (jnp.maximum(raw, 0.0) + jnp.log1p(jnp.exp(-jnp.abs(raw))))
                steps_all.append(steps)
                decay_all.append(-rate * gap_ref[u : u + 1, lanes] * steps)
        steps = jnp.concatenate(steps_all, axis=0)
        ahead, back = running_sums(jnp.concatenate(decay_all, axis=0))
        after = jnp.where(iota(back.shape, 1) < CHUNK - 1, pltpu.roll(back, CHUNK - 1, 1), 0.0)
        cum_ref[...] = ahead
        steps_ref[...] = steps
        weights[...] = jnp.exp(after) * steps
        totals[...] = jnp.broadcast_to(back[:, 0:1], totals.shape)
        state[...] = jnp.zeros_like(state)
        pref[...] = jnp.zeros_like(pref)
        prev[:, 0:8, :] = jnp.zeros((users, 8, conv_dim), BF16)
        prev[:, 8:16, :] = edge_ref[...]
        for k in range(3):
            source = iota((CHUNK, CHUNK + 16), 0) - (3 - k)
            source = jnp.where(source < 0, source + CHUNK + 16, source)
            moves[k * CHUNK : (k + 1) * CHUNK, :] = jnp.where(
                source == iota((CHUNK, CHUNK + 16), 1), 1.0, 0.0
            ).astype(BF16)

    for part, u in [(p, v) for p in range(STATE_CHUNKS) for v in range(users)]:
        c = step_index * STATE_CHUNKS + part
        time = pl.ds(pl.multiple_of(c * CHUNK, CHUNK), CHUNK)
        rows = slice(part * CHUNK, (part + 1) * CHUNK)
        at = 0
        while at < conv_dim:
            width = min(2 * LANES, conv_dim - at)
            cols = slice(at, at + width)
            here = conv_ref[u, time, cols]
            both = jnp.concatenate([here, prev[u, :, cols]], axis=0)
            prev[u, :, cols] = here[CHUNK - 16 :, :]
            total = cb_ref[cols].reshape(1, width) + cw_ref[3:4, cols] * here.astype(F32)
            moved = mm(moves[...], both)
            for k in range(3):
                total = total + cw_ref[k : k + 1, cols] * moved[k * CHUNK : (k + 1) * CHUNK, :]
            xbc_ref[u, rows, cols] = silu(total).astype(BF16)
            at += width
        decay_ref[u, part] = jnp.exp(pref[u])
        hold_ref[u, part] = state[u].astype(BF16)
        coef_t = xbc_ref[u, rows, inner : inner + LANES].astype(F32).T[:n_state, :]
        first = pl.multiple_of((u * chunks + c) * heads, heads)
        weight = weights[pl.ds(first, heads), :]
        total = totals[pl.ds(first, heads), :]
        for j in range(pairs):
            lanes = slice(j * LANES, (j + 1) * LANES)
            a, b = 2 * j, 2 * j + 1
            left = jnp.concatenate(
                [coef_t * weight[a : a + 1, :], coef_t * weight[b : b + 1, :]], axis=0
            ).astype(BF16)
            both = mm(left, xbc_ref[u, rows, lanes])
            add = lane_halves(both[:n_state], both[n_state:])
            tot = lane_halves(total[a : a + 1, :], total[b : b + 1, :])
            state[u, :, lanes] = jnp.exp(tot) * state[u, :, lanes] + add
            pref[u, :, lanes] = pref[u, :, lanes] + tot

    @pl.when(step_index == pl.num_programs(0) - 1)
    def _():
        for h in range(heads):
            lanes = slice((h // 2) * LANES, (h // 2 + 1) * LANES)
            parts = []
            for u in range(users):
                value = state[u, :, lanes]
                low = jnp.broadcast_to(pref[u, :, lanes], (8, LANES))
                if h % 2 != u:
                    value = pltpu.roll(value, half, 1)
                    low = pltpu.roll(low, half, 1)
                high = low.astype(BF16).astype(F32)
                row = iota((8, LANES), 0)
                extra = jnp.where(row == 0, high, jnp.where(row == 1, low - high, 0.0))
                parts.append(jnp.concatenate([value, extra], axis=0))
            end_ref[h] = lane_halves(*parts).astype(BF16)


def chunk_states(lens, conv, edge, step, gap, cw, cb, dt, rate, n_state):
    users, events, conv_dim = conv.shape
    heads = step.shape[1]
    inner = conv_dim - 2 * n_state
    chunks = events // CHUNK
    lines = chunks * users * heads
    return pl.pallas_call(
        states_kernel,
        out_shape=(
            pltpu.HBM((users, events, conv_dim), BF16),
            pltpu.HBM((lines, CHUNK), F32),
            pltpu.HBM((lines, CHUNK), F32),
            pltpu.HBM((users, chunks, n_state, inner), BF16),
            pltpu.HBM((users, chunks, 1, inner), F32),
            pltpu.HBM((heads, n_state + 8, LANES), BF16),
        ),
        grid=(chunks // STATE_CHUNKS,),
        in_specs=[SCALARS, ON_CHIP, full(edge.shape), ON_CHIP]
        + [full(v.shape) for v in (gap, cw, cb, dt, rate)],
        out_specs=(
            pl.BlockSpec((users, STATE_CHUNKS * CHUNK, conv_dim), lambda c: (0, c, 0)),
            full((lines, CHUNK)),
            full((lines, CHUNK)),
            pl.BlockSpec((users, STATE_CHUNKS, n_state, inner), lambda c: (0, c, 0, 0)),
            pl.BlockSpec((users, STATE_CHUNKS, 1, inner), lambda c: (0, c, 0, 0)),
            full((heads, n_state + 8, LANES)),
        ),
        scratch_shapes=[
            pltpu.VMEM((users, 16, conv_dim), BF16),
            pltpu.VMEM((3 * CHUNK, CHUNK + 16), BF16),
            pltpu.VMEM((lines, CHUNK), F32),
            pltpu.VMEM((lines, LANES), F32),
            pltpu.VMEM((users, n_state, inner), F32),
            pltpu.VMEM((users, 1, inner), F32),
        ],
        compiler_params=params(1),
        name="chunk_states",
    )(lens, near(conv), edge, near(step), gap, cw, cb, dt, rate)


def scan_kernel(in_ref, out_ref):
    spans, rows, lanes = in_ref.shape
    n_state = rows - 8
    running = jnp.zeros((n_state, lanes), F32)
    for k in range(spans):
        out_ref[k] = running.astype(BF16)
        block = in_ref[k].astype(F32)
        log_decay = block[n_state : n_state + 1, :] + block[n_state + 1 : n_state + 2, :]
        running = jnp.exp(log_decay) * running + block[:n_state, :]


def scan_spans(ends):
    spans, rows, lanes = ends.shape
    return pl.pallas_call(
        scan_kernel,
        out_shape=jax.ShapeDtypeStruct((spans, rows - 8, lanes), BF16),
        in_specs=[ON_CHIP],
        out_specs=ON_CHIP,
        compiler_params=params(0),
        name="scan_spans",
    )(near(ends))


def local_kernel(normed_ref, w_ref, xbc_ref, cum_ref, steps_ref, *rest):
    y_ref, fade_ref, gates = rest[-3:]
    _, rows, inner = y_ref.shape
    parts = rows // CHUNK
    heads = cum_ref.shape[0] // parts
    pairs = heads // 2
    half = LANES // 2
    gates[...] = silu(mm(normed_ref[0], w_ref[...]).astype(BF16).astype(F32))
    causal = iota((CHUNK, CHUNK), 0) >= iota((CHUNK, CHUNK), 1)
    for part in range(parts):
        here = slice(part * CHUNK, (part + 1) * CHUNK)
        coef = xbc_ref[0, here, inner : inner + LANES]
        scores = jnp.where(causal, nt(coef[:, half:], coef[:, :half]), 0.0)
        cum = cum_ref[part * heads : (part + 1) * heads, :]
        steps = steps_ref[part * heads : (part + 1) * heads, :]
        cum_t = jnp.concatenate([cum, jnp.zeros((LANES - heads, CHUNK), F32)], axis=0).T

        def mixing(h):
            own = jnp.broadcast_to(cum_t[:, h : h + 1], (CHUNK, CHUNK))
            fading = jnp.exp(jnp.minimum(own - cum[h : h + 1, :], 0.0))
            return own, (scores * fading * steps[h : h + 1, :]).astype(BF16)

        for j in range(pairs):
            lanes = slice(j * LANES, (j + 1) * LANES)
            own_a, mix_a = mixing(2 * j)
            own_b, mix_b = mixing(2 * j + 1)
            left = jnp.concatenate([mix_a, mix_b], axis=1)
            gate = gates[here, lanes]
            y_ref[0, here, lanes] = (gate * mm(left, pair_rhs(xbc_ref[0, here, lanes]))).astype(BF16)
            fade_ref[0, here, lanes] = (gate * jnp.exp(lane_halves(own_a, own_b))).astype(BF16)


def local_response(normed, weight, xbc, cum, steps, user, before=()):
    users, events, conv_dim = xbc.shape
    dim, inner = weight.shape
    heads = cum.shape[0] * CHUNK // (users * events)
    rows = LOCAL_CHUNKS * CHUNK
    blocks = events // rows
    block = lambda width: pl.BlockSpec((1, rows, width), lambda i: (user, i, 0))
    lines = pl.BlockSpec((LOCAL_CHUNKS * heads, CHUNK), lambda i: (user * blocks + i, 0))
    result = block(inner)
    return pl.pallas_call(
        local_kernel,
        out_shape=(pltpu.HBM((users, events, inner), BF16),) * 2,
        grid=(blocks,),
        in_specs=[block(dim), ON_CHIP, block(conv_dim), lines, lines] + [ANYWHERE] * len(before),
        out_specs=(result, result),
        scratch_shapes=[pltpu.VMEM((rows, inner), F32)],
        input_output_aliases={5 + k: k for k in range(len(before))},
        compiler_params=params(1),
        name="local_response",
    )(far(normed), near(weight), far(xbc), far(cum), far(steps), *[far(v) for v in before])


def finish_kernel(
    len_ref,
    y_ref,
    fade_ref,
    coef_ref,
    x_ref,
    hold_ref,
    decay_ref,
    hin_ref,
    gain_ref,
    w_ref,
    out_ref,
    incoming,
    same,
    normed,
    *,
    blocks,
):
    u = pl.program_id(0) // blocks
    b = pl.program_id(0) % blocks
    heads = hin_ref.shape[0]
    pairs = heads // 2
    half = LANES // 2
    size = 2 * LANES
    rows = out_ref.shape[1]

    @pl.when(pl.program_id(0) == 0)
    def _():
        same[...] = jnp.where(
            iota((size, size), 0) // half == iota((size, size), 1) // half, 1.0 / half, 0.0
        ).astype(BF16)
        for j in range(pairs):
            a = hin_ref[2 * j].astype(F32)
            b = hin_ref[2 * j + 1].astype(F32)
            lanes = slice(j * LANES, (j + 1) * LANES)
            incoming[0, :, lanes] = lane_halves(a, pltpu.roll(b, half, 1))
            incoming[1, :, lanes] = lane_halves(pltpu.roll(a, half, 1), b)

    for part in range(rows // CHUNK):
        here = slice(part * CHUNK, (part + 1) * CHUNK)
        held = hold_ref[0, part].astype(F32) + decay_ref[0, part] * incoming[u]
        held = held.astype(BF16)
        coef = coef_ref[0, here, half:]
        for j in range(pairs // 2):
            lanes = slice(j * size, (j + 1) * size)
            carried = mm(coef, held[:, lanes])
            gated = y_ref[0, here, lanes].astype(F32) + fade_ref[0, here, lanes].astype(F32) * carried
            mean = mm((gated * gated).astype(BF16), same[...])
            normed[here, lanes] = (
                gated * lax.rsqrt(mean + EPS) * gain_ref[:, lanes]
            ).astype(BF16)
    mixed = mm(normed[...], w_ref[...])
    position = first_position(blocks * rows) + b * rows + iota((rows, 1), 0)
    alive = jnp.where(position < len_ref[u], 1.0, 0.0)
    out_ref[0] = (alive * (x_ref[0].astype(F32) + mixed)).astype(BF16)


def finish(lens, y, fade, xbc, x, hold, decay, hin, gain, weight):
    _, events, inner = y.shape
    n_state = hold.shape[2]
    users, _, dim = x.shape
    size = 2 * LANES
    rows = FINISH_ROWS
    blocks = events // rows
    parts = rows // CHUNK
    wide = pl.BlockSpec((1, rows, inner), lambda i: (i // blocks, i % blocks, 0))
    block = pl.BlockSpec((1, rows, dim), lambda i: (i // blocks, i % blocks, 0))
    per_chunk = lambda *shape: pl.BlockSpec(
        (1, parts) + shape, lambda i: (i // blocks, i % blocks, 0, 0)
    )
    return pl.pallas_call(
        functools.partial(finish_kernel, blocks=blocks),
        out_shape=jax.ShapeDtypeStruct((users, events, dim), BF16),
        grid=(users * blocks,),
        in_specs=[
            SCALARS,
            wide,
            wide,
            pl.BlockSpec((1, rows, LANES), lambda i: (i // blocks, i % blocks, inner // LANES)),
            block,
            per_chunk(n_state, inner),
            per_chunk(1, inner),
            full(hin.shape),
            full(gain.shape),
            full(weight.shape),
        ],
        out_specs=block,
        scratch_shapes=[
            pltpu.VMEM((users, n_state, inner), F32),
            pltpu.VMEM((size, size), BF16),
            pltpu.VMEM((rows, inner), BF16),
        ],
        compiler_params=params(1, 24),
        name="finish",
    )(lens, *[far(v) for v in (y, fade, xbc, x, hold, decay)], hin, gain, weight)


def exchange(values, axes):
    return lax.all_to_all(values, axes, split_axis=0, concat_axis=0, tiled=True)


def per_device(
    item_owner,
    item_row,
    history_len,
    event_gap,
    item_table,
    norm_gain,
    in_weight,
    conv_weight,
    conv_bias,
    dt_bias,
    decay_rate,
    out_gain,
    emitted_projection,
):
    users, events = item_row.shape
    dim = item_table.shape[1]
    heads = dt_bias.shape[0]
    inner = emitted_projection.shape[0]
    conv_dim = conv_weight.shape[1]
    n_state = (conv_dim - inner) // 2
    times = lax.axis_size("tm")
    devices = times * lax.axis_size("table")
    cap = 2 * events // devices
    slots = users * cap
    everyone = ("tm", "table")

    requests, place = route(jnp.swapaxes(item_owner, 1, 2), item_row, devices, cap, 32)
    asked = exchange(requests, everyone)
    rows = fetch(asked, item_table, slots)
    got = exchange(rows.reshape(devices, slots, dim), everyone)
    got, gate_weight, conv_in_weight = lax.optimization_barrier(
        (got, in_weight[:, :inner], in_weight[:, inner:])
    )
    x, normed, conv, step, tail = project(
        got, place, norm_gain[None, :], conv_in_weight, conv_dim, heads
    )
    edge = lax.ppermute(tail, "tm", [(i, i + 1) for i in range(times - 1)])
    xbc, cum, steps, hold, decay, ends = chunk_states(
        history_len,
        conv,
        edge,
        step,
        event_gap,
        conv_weight,
        conv_bias,
        dt_bias[None, :],
        decay_rate[None, :],
        n_state,
    )
    by_head = exchange(ends, "tm")
    y, fade = local_response(normed, gate_weight, xbc, cum, steps, 0)
    by_head, y, fade = lax.optimization_barrier((by_head, y, fade))
    hin = exchange(scan_spans(by_head), "tm")
    y, fade = local_response(normed, gate_weight, xbc, cum, steps, 1, (y, fade))
    return finish(
        history_len,
        y,
        fade,
        xbc,
        x,
        hold,
        decay,
        hin,
        out_gain[None, :],
        emitted_projection,
    )


def solution(mesh):
    in_specs = (
        P("table", "tm", None),
        P("table", "tm"),
        P("table"),
        P("table", "tm"),
        P(("tm", "table"), None),
        P(),
        P(),
        P(),
        P(),
        P(),
        P(),
        P(),
        P(),
    )
    out_specs = P("table", "tm", None)
    return jax.shard_map(
        per_device, mesh=mesh, in_specs=in_specs, out_specs=out_specs, check_vma=False
    )
```
